32 devices in a mesh: dp: 8 (over z, x), tensor: 4 (over y, core).
Axes of the slice: x: 2, y: 2, z: 4, core: 2. Of those that a mesh axis runs over, the one named last changes fastest.
Arguments:
- inputs: bfloat16 [32768, 512], P('dp'), may hold values from -6 to 6
- memory: bfloat16 [32768, 512], P('dp'), may hold values from -6 to 6
- cotangent: bfloat16 [32768, 512], P('dp'), may hold values from -6 to 6
- lengths: int32 [32], P('dp'), may hold values from 128 to 1024, as said below
- key_mask: int32 [32, 1024], P('dp'), may hold values 0 or 1
- owner_list: int32 [8], replicated, may hold values from 0 to 7, each once
- attention_master: float32 [8, 512, 512], P(None, 'dp', 'tensor'), may hold values from -1.06066017 to 1.06066017
- attention_moment: float32 [8, 512, 512], P(None, 'dp', 'tensor'), may hold values from -32 to 32
- attention_second: float32 [8, 512, 512], P(None, 'dp', 'tensor'), may hold values from 108.1344 to 432.5376
- attention_average: float32 [8, 512, 512], P(None, 'dp', 'tensor'), may hold values from -0.25 to 0.25
- attention_basis: float32 [8, 512, 128], P(None, 'tensor'), may hold values from -1 to 1
- feed_master: float32 [2, 512, 2048], P(None, 'dp', 'tensor'), may hold values from -0.26516504 to 0.26516504
- feed_moment: float32 [2, 512, 2048], P(None, 'dp', 'tensor'), may hold values from -32 to 32
- feed_second: float32 [2, 512, 2048], P(None, 'dp', 'tensor'), may hold values from 108.1344 to 432.5376
- feed_average: float32 [2, 512, 2048], P(None, 'dp', 'tensor'), may hold values from -0.25 to 0.25
- feed_basis: float32 [2, 2048, 512], P(None, 'tensor'), may hold values from -1 to 1
- norm_master: float32 [6, 512], P(None, 'dp'), may hold values from -1.5 to 1.5
- norm_moment: float32 [6, 512], P(None, 'dp'), may hold values from -96 to 96
- norm_second: float32 [6, 512], P(None, 'dp'), may hold values from 1114.112 to 4423.68
- norm_average: float32 [6, 512], P(None, 'dp'), may hold values from 0.5 to 1.5
Outputs:
- output: bfloat16 [32768, 512], P(('dp', 'tensor'))
- grad_input: bfloat16 [32768, 512], P(('dp', 'tensor'))
- grad_memory: bfloat16 [32768, 512], P(('dp', 'tensor'))
- attention_moment_new: float32 [8, 512, 512], P(None, 'dp', 'tensor')
- attention_second_new: float32 [8, 512, 512], P(None, 'dp', 'tensor')
- attention_weight_new: float32 [8, 512, 512], P(None, 'dp', 'tensor')
- attention_average_new: float32 [8, 512, 512], P(None, 'dp', 'tensor')
- attention_copy: bfloat16 [8, 512, 512], P(None, 'dp', 'tensor')
- feed_moment_new: float32 [2, 512, 2048], P(None, 'dp', 'tensor')
- feed_second_new: float32 [2, 512, 2048], P(None, 'dp', 'tensor')
- feed_weight_new: float32 [2, 512, 2048], P(None, 'dp', 'tensor')
- feed_average_new: float32 [2, 512, 2048], P(None, 'dp', 'tensor')
- feed_copy: bfloat16 [2, 512, 2048], P(None, 'dp', 'tensor')
- norm_moment_new: float32 [6, 512], P(None, ('dp', 'tensor'))
- norm_second_new: float32 [6, 512], P(None, ('dp', 'tensor'))
- norm_weight_new: float32 [6, 512], P(None, ('dp', 'tensor'))
- norm_average_new: float32 [6, 512], P(None, ('dp', 'tensor'))
- norm_copy: bfloat16 [6, 512], P(None, ('dp', 'tensor'))
The draws below stay inside these ranges and needn't reach their ends.
Inputs may be any that keep to these rules, and one draw needn't show every extreme that they name: `lengths`: at least one sequence has exactly 1024 tokens in use.
All inputs are finite; a program needn't handle non-finite values. No bound on the sum of `key_mask` on one device may be relied on, other than what follows from the above.
Results may differ from the reference program's by a relative error of at most 0.03.
The reference program's roundings to bfloat16 on the way count: a program that leaves them out, or rounds other values in their place, can miss the bound.
Values may be sent and summed in bfloat16 or wider, within the bound.
A program may use at most 256 MiB of HBM per device.

```python
import math
from functools import partial
import jax
import jax.numpy as jnp
from jax import lax

D = 512
HEADS = 8
HDIM = 64
FF = 2048
SEQS = 4
SEQ_LEN = 1024
MEM_LEN = 1024
STEP = 10
TOK_DEV = 4096
MEM_DEV = 4096
SEQS_ALL = 32
TOKENS = 32768
MEMS = 32768
CT = 128
FT = 512
N_DP = 8


def draw_lengths(key, part):
    folded = jax.random.fold_in(key, 3)
    first_key, second_key = jax.random.split(folded)
    values = jax.random.randint(first_key, (SEQS_ALL,), SEQ_LEN // 8, SEQ_LEN + 1)
    chosen = jax.random.randint(second_key, (), 0, SEQS_ALL)
    return jnp.where(jnp.arange(SEQS_ALL) == chosen, SEQ_LEN, values).astype(jnp.int32)


def base_values(key, shape):
    values = jnp.clip(jax.random.normal(key, shape, jnp.float32), -6.0, 6.0)
    return values


def draw_attention_master(key, part):
    factors = jnp.array([1.4, 1.4, 1.0, 4.0, 1.4, 1.4, 1.0, 4.0], jnp.float32)[:, None, None]
    values = base_values(jax.random.fold_in(key, 5), (8, D, D))
    return values * factors * D ** (-0.5)


def draw_feed_master(key, part):
    values = base_values(jax.random.fold_in(key, 7), (2, D, FF))
    factors = jnp.array([D ** (-0.5), 2.0 * FF ** (-0.5)], jnp.float32)[:, None, None]
    return values * factors


def draw_norm_master(key, part):
    gain_key, shift_key = jax.random.split(jax.random.fold_in(key, 9))
    gains = 1.0 + jax.random.uniform(gain_key, (6, D), jnp.float32, -0.3, 0.3)
    shifts = jnp.clip(0.3 * jax.random.normal(shift_key, (6, D), jnp.float32), -1.5, 1.5)
    is_gain = (jnp.arange(6) % 2 == 0)[:, None]
    return jnp.where(is_gain, gains, shifts)


def rotations(key, slots, rows, size):
    levels = size.bit_length() - 1
    angles = jax.random.uniform(key, (slots, rows // size, levels), jnp.float32, -3.14159265, 3.14159265)
    row_index = jnp.arange(rows)
    picked = angles[:, row_index // size, :]
    inside = (row_index % size)[:, None]
    columns = jnp.arange(size)[None, :]
    result = jnp.ones((slots, rows, size), jnp.float32)
    for level in range(levels):
        row_bit = inside // 2 ** level % 2
        column_bit = columns // 2 ** level % 2
        angle = picked[:, :, level][:, :, None]
        cosine = jnp.cos(angle)
        sine = jnp.sin(angle)
        entry = jnp.where(row_bit == column_bit, cosine, jnp.where(row_bit > column_bit, sine, -sine))
        result = result * entry
    return result


def draw_attention_basis(key, part):
    return rotations(jax.random.fold_in(key, 11), 8, D, CT)


def draw_feed_basis(key, part):
    return rotations(jax.random.fold_in(key, 13), 2, FF, FT)


def set_ends(values, rng, smallest, largest):
    longest = values.shape.index(max(values.shape))
    spots = []
    for shift in (0, 1):
        where = [jax.random.randint(jax.random.fold_in(rng, axis), (), 0, length) for axis, length in enumerate(values.shape)]
        where[longest] = (where[longest] + shift) % values.shape[longest]
        spots.append(tuple(where))
    return values.at[spots[0]].set(smallest).at[spots[1]].set(largest)


def shard_levels(key, dims, cuts, low, largest):
    level = 1.0
    for position, blocks in cuts:
        draws = jax.random.uniform(jax.random.fold_in(jax.random.fold_in(key, 6), position), (blocks,), jnp.float32, low / len(cuts), largest / len(cuts))
        level = level * jnp.repeat(jnp.exp(draws), dims[position] // blocks).reshape((-1,) + (1,) * (len(dims) - 1 - position))
    return level


def noise(own_key, dims, deviation, most, pieces=(), kind=jnp.bfloat16):
    loudness = shard_levels(own_key, dims, pieces, -0.22, 0.18) if pieces else 1.0
    values = jax.random.normal(own_key, dims, jnp.float32) * deviation * loudness
    return jnp.minimum(jnp.maximum(values, -most), most).astype(kind)


def setup_inputs(seed: int = 0) -> dict:
    splits = jax.random.split(jax.random.key(seed), 21)
    return {
        "inputs": noise(splits[0], (TOKENS, D), 1.0, 6.0, ((0, 8),)),
        "memory": noise(splits[1], (MEMS, D), 1.0, 6.0, ((0, 8),)),
        "cotangent": noise(splits[2], (TOKENS, D), 1.0, 6.0, ((0, 8),)),
        "lengths": draw_lengths(jax.random.fold_in(splits[20], 71), 0),
        "key_mask": set_ends((jax.random.randint(splits[4], (SEQS_ALL, MEM_LEN), 0, 4) < 3).astype(jnp.int32), jax.random.fold_in(splits[4], 1), 0, 1),
        "owner_list": jax.random.permutation(splits[5], N_DP).astype(jnp.int32),
        "attention_master": draw_attention_master(jax.random.fold_in(splits[20], 71), 0),
        "attention_moment": noise(splits[7], (8, D, D), (0.0278 * TOKENS ** 0.5), 32.0, ((1, 8), (2, 4)), jnp.float32),
        "attention_second": jnp.clip(jnp.exp(math.log(432.5376) - 1.3862944 * jax.random.uniform(splits[8], (8, D, D), jnp.float32) ** shard_levels(splits[8], (8, D, D), ((1, 8), (2, 4)), -0.2, 0.2)), 108.1344, 432.5376),
        "attention_average": noise(splits[9], (8, D, D), D ** -0.5, 0.25, ((1, 8), (2, 4)), jnp.float32),
        "attention_basis": draw_attention_basis(jax.random.fold_in(splits[20], 71), 0),
        "feed_master": draw_feed_master(jax.random.fold_in(splits[20], 71), 0),
        "feed_moment": noise(splits[12], (2, D, FF), (0.0278 * TOKENS ** 0.5), 32.0, ((1, 8), (2, 4)), jnp.float32),
        "feed_second": jnp.clip(jnp.exp(math.log(432.5376) - 1.3862944 * jax.random.uniform(splits[13], (2, D, FF), jnp.float32) ** shard_levels(splits[13], (2, D, FF), ((1, 8), (2, 4)), -0.2, 0.2)), 108.1344, 432.5376),
        "feed_average": noise(splits[14], (2, D, FF), D ** -0.5, 0.25, ((1, 8), (2, 4)), jnp.float32),
        "feed_basis": draw_feed_basis(jax.random.fold_in(splits[20], 71), 0),
        "norm_master": draw_norm_master(jax.random.fold_in(splits[20], 71), 0),
        "norm_moment": noise(splits[17], (6, D), (0.089 * TOKENS ** 0.5), 96.0, ((1, 8),), jnp.float32),
        "norm_second": jnp.clip(jnp.exp(math.log(4423.68) - 1.3789142 * jax.random.uniform(splits[18], (6, D), jnp.float32) ** shard_levels(splits[18], (6, D), ((1, 8),), -0.2, 0.2)), 1114.112, 4423.68),
        "norm_average": jnp.clip(1.0 + 0.1 * jax.random.normal(splits[19], (6, D), jnp.float32), 0.5, 1.5),
    }


@jax.custom_vjp
def low(v):
    return lax.optimization_barrier(v.astype(jnp.bfloat16)).astype(jnp.float32)

@jax.custom_vjp
def low_back(v):
    return v

def low_keep(v):
    return (low(v), None)

def low_pass(kept, grad):
    return (grad,)

def back_keep(v):
    return (v, None)

def back_low(kept, grad):
    return (low(grad),)
low.defvjp(low_keep, low_pass)
low_back.defvjp(back_keep, back_low)
FLOOR_SCORE = -1e+30
NORM_EPSILON = 1e-05
BETA_FIRST = 0.9
BETA_SECOND = 0.95
ADAM_EPSILON = 1e-08
AVERAGE_DECAY = 0.6
RATE_ATTENTION = 0.07
RATE_FEED = 0.03
RATE_NORMS = 0.5
WEIGHT_DECAY = 0.01
HIGHEST = lax.Precision.HIGHEST

def inverse_order(owner_list):
    count = owner_list.shape[0]
    places = jnp.arange(count, dtype=jnp.int32)
    match = owner_list[None, :] == places[:, None]
    return lax.optimization_barrier(jnp.sum(jnp.where(match, places[None, :], 0), axis=1)).astype(jnp.int32)

def reorder(array, axis, index, parts):
    shape = array.shape
    blocks = array.reshape(shape[:axis] + (parts, shape[axis] // parts) + shape[axis + 1:])
    return jnp.take(blocks, index, axis=axis).reshape(shape)

def layer_norm(inputs, gain, shift):
    centred = inputs - lax.optimization_barrier(jnp.mean(inputs, axis=-1, keepdims=True))
    spread = lax.optimization_barrier(jnp.mean(centred * centred, axis=-1, keepdims=True))
    return centred * lax.rsqrt(spread + NORM_EPSILON) * gain + shift

def matmul(left, right):
    return jnp.dot(left, right, precision=HIGHEST)

def attend(parts, causal):
    queries, key_rows, value_rows, key_valid = parts
    rows = queries.shape[0]
    count = key_rows.shape[0]
    query_heads = queries.reshape(rows, HEADS, HDIM)
    key_heads = key_rows.reshape(count, HEADS, HDIM)
    value_heads = value_rows.reshape(count, HEADS, HDIM)
    scores = low_back(jnp.einsum('qhd,khd->hqk', query_heads, key_heads, precision=HIGHEST) * HDIM ** (-0.5))
    allowed = jnp.broadcast_to(key_valid[None, :], (rows, count))
    if causal:
        allowed = allowed & (jnp.arange(count)[None, :] <= jnp.arange(rows)[:, None])
    masked = jnp.where(allowed[None], scores, FLOOR_SCORE)
    highest = lax.optimization_barrier(jnp.max(masked, axis=-1, keepdims=True))
    expd = jnp.exp(masked - highest)
    probs = low(expd / lax.optimization_barrier(jnp.sum(expd, axis=-1, keepdims=True)))
    mixed = jnp.einsum('hqk,khd->qhd', probs, value_heads, precision=HIGHEST)
    return mixed.reshape(rows, HEADS * HDIM)

def layer_forward(rows, memory_rows, attention_param, feed_param, norm_param, lengths, key_mask):
    weights = low(attention_param)
    feeds = low(feed_param)
    norms = low(norm_param)
    seqs = lengths.shape[0]
    tok_rows = rows.shape[0]
    seq_rows = tok_rows // seqs
    mem_rows = memory_rows.shape[0] // seqs

    def project(source, matrix):
        return low(low_back(matmul(source, matrix)))
    self_q = project(rows, weights[0])
    self_k = project(rows, weights[1])
    self_v = project(rows, weights[2])
    every_key = jnp.ones((seqs, seq_rows), dtype=bool)
    self_mix = lax.map(jax.checkpoint(partial(attend, causal=True)), (self_q.reshape(seqs, seq_rows, D), self_k.reshape(seqs, seq_rows, D), self_v.reshape(seqs, seq_rows, D), every_key))
    self_mix = low(low_back(self_mix.reshape(tok_rows, D)))
    first_sum = rows + low_back(matmul(self_mix, weights[3].T))
    first = layer_norm(first_sum, norms[0], norms[1])
    first_low = low(first)
    cross_q = project(first_low, weights[4])
    cross_k = project(memory_rows, weights[5])
    cross_v = project(memory_rows, weights[6])
    key_valid = (key_mask == 1) | (jnp.arange(mem_rows) == 0)[None, :]
    cross_mix = lax.map(jax.checkpoint(partial(attend, causal=False)), (cross_q.reshape(seqs, seq_rows, D), cross_k.reshape(seqs, mem_rows, D), cross_v.reshape(seqs, mem_rows, D), key_valid))
    cross_mix = low(low_back(cross_mix.reshape(tok_rows, D)))
    second_sum = first + low_back(matmul(cross_mix, weights[7].T))
    second = layer_norm(second_sum, norms[2], norms[3])
    second_low = low(second)
    inner = low_back(matmul(second_low, feeds[0]))
    active = low(jax.nn.gelu(inner, approximate=False))
    feed_out = low_back(matmul(active, feeds[1].T))
    third_sum = second + feed_out + rows
    live = (jnp.arange(seq_rows)[None, :] < lengths[:, None]).reshape(tok_rows, 1).astype(jnp.float32)
    return live * layer_norm(third_sum, norms[4], norms[5])

def adam_moments(rotated, moment, second):
    moment_new = BETA_FIRST * moment + (1.0 - BETA_FIRST) * rotated
    second_new = BETA_SECOND * second + (1.0 - BETA_SECOND) * rotated * rotated
    direction = moment_new / (1.0 - BETA_FIRST ** STEP) / (jnp.sqrt(second_new / (1.0 - BETA_SECOND ** STEP)) + ADAM_EPSILON)
    return (moment_new, second_new, direction)

def finish(weight, average, update, rate, decay):
    weight_new = weight - rate * (update + decay * weight)
    average_new = AVERAGE_DECAY * average + (1.0 - AVERAGE_DECAY) * weight_new
    return (weight_new, average_new, weight_new.astype(jnp.bfloat16))

def soap_step(weight, grad, moment, second, average, basis, rate, decay):
    shape = grad.shape
    size = basis.shape[2]
    blocks = shape[2] // size
    bases = basis.reshape(shape[0], blocks, size, size)
    rotated = jnp.einsum('srtc,stce->srte', grad.reshape(shape[0], shape[1], blocks, size), bases, precision=HIGHEST).reshape(shape)
    moment_new, second_new, direction = adam_moments(rotated, moment, second)
    update = jnp.einsum('srte,stce->srtc', direction.reshape(shape[0], shape[1], blocks, size), bases, precision=HIGHEST).reshape(shape)
    return (moment_new, second_new) + finish(weight, average, update, rate, decay)

def reference(inputs, memory, cotangent, lengths, key_mask, owner_list, attention_master, attention_moment, attention_second, attention_average, attention_basis, feed_master, feed_moment, feed_second, feed_average, feed_basis, norm_master, norm_moment, norm_second, norm_average):
    inverse = inverse_order(owner_list)
    attention_param = reorder(attention_master, 1, owner_list, N_DP)
    feed_param = reorder(feed_master, 1, owner_list, N_DP)
    norm_param = reorder(norm_master, 1, owner_list, N_DP)
    items = (inputs.reshape(N_DP, TOK_DEV, D), memory.reshape(N_DP, MEM_DEV, D), cotangent.reshape(N_DP, TOK_DEV, D), lengths.reshape(N_DP, SEQS), key_mask.reshape(N_DP, SEQS, MEM_LEN))

    def group_step(totals, item):
        rows, memory_rows, grad_rows, group_lengths, group_mask = item
        forward = partial(layer_forward, lengths=group_lengths, key_mask=group_mask)
        result, pull = jax.vjp(forward, rows.astype(jnp.float32), memory_rows.astype(jnp.float32), attention_param, feed_param, norm_param)
        grads = pull(grad_rows.astype(jnp.float32))
        totals = (totals[0] + grads[2], totals[1] + grads[3], totals[2] + grads[4])
        return (totals, (result.astype(jnp.bfloat16), grads[0].astype(jnp.bfloat16), grads[1].astype(jnp.bfloat16)))
    zeros = (jnp.zeros(attention_param.shape, jnp.float32), jnp.zeros(feed_param.shape, jnp.float32), jnp.zeros(norm_param.shape, jnp.float32))
    totals, stacked = lax.scan(group_step, zeros, items)
    output = stacked[0].reshape(TOKENS, D)
    grad_input = stacked[1].reshape(TOKENS, D)
    grad_memory = stacked[2].reshape(MEMS, D)
    attention_grad = reorder(totals[0], 1, inverse, N_DP)
    feed_grad = reorder(totals[1], 1, inverse, N_DP)
    norm_grad = reorder(totals[2], 1, inverse, N_DP)
    attention_new = soap_step(attention_master, attention_grad, attention_moment, attention_second, attention_average, attention_basis, RATE_ATTENTION, WEIGHT_DECAY)
    feed_new = soap_step(feed_master, feed_grad, feed_moment, feed_second, feed_average, feed_basis, RATE_FEED, WEIGHT_DECAY)
    moment_new, second_new, direction = adam_moments(norm_grad, norm_moment, norm_second)
    norm_new = (moment_new, second_new) + finish(norm_master, norm_average, direction, RATE_NORMS, 0.0)
    return (output, grad_input, grad_memory, attention_new[0], attention_new[1], attention_new[2], attention_new[3], attention_new[4], feed_new[0], feed_new[1], feed_new[2], feed_new[3], feed_new[4], norm_new[0], norm_new[1], norm_new[2], norm_new[3], norm_new[4])
```

```python
from functools import partial

import jax
import jax.numpy as jnp
from jax import lax
from jax.sharding import PartitionSpec as P

HDIM = 64
STEP = 10


FLOOR_SCORE = -1e30
NORM_EPSILON = 1e-05
BETA_FIRST = 0.9
BETA_SECOND = 0.95
ADAM_EPSILON = 1e-08
AVERAGE_DECAY = 0.6
RATE_ATTENTION = 0.07
RATE_FEED = 0.03
RATE_NORMS = 0.5
WEIGHT_DECAY = 0.01
HIGHEST = lax.Precision.HIGHEST


def place_matrix(owner_list, width):
    blocks = owner_list.shape[0]
    rows = width // blocks
    here = jnp.arange(width, dtype=jnp.int32)
    block = here // rows
    target = jnp.sum(
        jnp.where(block[:, None] == jnp.arange(blocks)[None, :], owner_list[None, :], 0), axis=1
    ) * rows + here % rows
    return (target[:, None] == here[None, :]).astype(jnp.bfloat16)


def layer_norm(inputs, gain, shift):
    centred = inputs - jnp.mean(inputs, axis=-1, keepdims=True)
    spread = jnp.mean(centred * centred, axis=-1, keepdims=True)
    return centred * lax.rsqrt(spread + NORM_EPSILON) * gain + shift


def gelu_exact(values):
    return jax.nn.gelu(values, approximate=False)


def times_rows(left, matrix):
    return jnp.einsum("tc,dc->td", left, matrix, preferred_element_type=jnp.float32)


def times_matrix(left, matrix):
    return jnp.dot(left, matrix, preferred_element_type=jnp.float32)


def outer_rows(left, right):
    return jnp.einsum("td,tc->dc", left, right, preferred_element_type=jnp.float32)


def head_split(rows):
    return rows.reshape(rows.shape[0], rows.shape[1] // HDIM, HDIM)


def block_scores(query_block, key_rows, allowed):
    scores = jnp.einsum(
        "qhd,khd->hqk",
        head_split(query_block),
        head_split(key_rows),
        preferred_element_type=jnp.float32,
    ) * HDIM ** (-0.5)
    return jnp.where(allowed[None], scores, FLOOR_SCORE)


def block_allowed(begin_row, block, key_valid, causal):
    allowed = jnp.broadcast_to(key_valid[None, :], (block, key_valid.shape[0]))
    if causal:
        key_place = jnp.arange(key_valid.shape[0])
        query_place = begin_row + jnp.arange(block)
        allowed = allowed & (key_place[None, :] <= query_place[:, None])
    return allowed


def block_forward(query_block, key_rows, value_rows, allowed):
    masked = block_scores(query_block, key_rows, allowed)
    highest = jnp.max(masked, axis=-1, keepdims=True)
    expd = jnp.exp(masked - highest)
    total = jnp.sum(expd, axis=-1, keepdims=True)
    probs = (expd / total).astype(jnp.bfloat16)
    mixed = jnp.einsum(
        "hqk,khd->qhd", probs, head_split(value_rows), preferred_element_type=jnp.float32
    )
    return (mixed.reshape(query_block.shape), (highest + jnp.log(total))[:, :, 0])


def block_backward(query_block, key_rows, value_rows, allowed, log_total, grad_block):
    masked = block_scores(query_block, key_rows, allowed)
    probs = jnp.exp(masked - log_total[:, :, None])
    grad_heads = head_split(grad_block)
    grad_values = jnp.einsum(
        "hqk,qhd->khd", probs.astype(jnp.bfloat16), grad_heads, preferred_element_type=jnp.float32
    )
    grad_probs = jnp.einsum(
        "qhd,khd->hqk", grad_heads, head_split(value_rows), preferred_element_type=jnp.float32
    )
    centre = jnp.sum(grad_probs * probs, axis=-1, keepdims=True)
    grad_scores = (probs * (grad_probs - centre)).astype(jnp.bfloat16)
    scale = HDIM ** (-0.5)
    grad_queries = (
        jnp.einsum(
            "hqk,khd->qhd", grad_scores, head_split(key_rows), preferred_element_type=jnp.float32
        )
        * scale
    )
    grad_keys = (
        jnp.einsum(
            "hqk,qhd->khd", grad_scores, head_split(query_block), preferred_element_type=jnp.float32
        )
        * scale
    )
    return (
        grad_queries.reshape(query_block.shape),
        grad_keys.reshape(key_rows.shape),
        grad_values.reshape(value_rows.shape),
    )


def sequence_forward(parts, causal):
    query_seq, key_seq, value_seq, key_valid, length = parts
    seq_rows = query_seq.shape[0]
    block = min(512, seq_rows)
    mixes = []
    totals = []
    for begin_row in range(0, seq_rows, block):
        allowed = block_allowed(begin_row, block, key_valid, causal)
        compute = partial(
            block_forward, query_seq[begin_row : begin_row + block], key_seq, value_seq, allowed
        )
        mixed, log_total = compute()
        mixes.append(mixed)
        totals.append(log_total)
    return (jnp.concatenate(mixes, axis=0), jnp.concatenate(totals, axis=1))


def sequence_backward(parts, causal):
    query_seq, key_seq, value_seq, key_valid, length, log_totals, grad_seq = parts
    seq_rows = query_seq.shape[0]
    block = min(512, seq_rows)
    grad_query_list = []
    grad_key_total = jnp.zeros(key_seq.shape, jnp.float32)
    grad_value_total = jnp.zeros(value_seq.shape, jnp.float32)
    for begin_row in range(0, seq_rows, block):
        allowed = block_allowed(begin_row, block, key_valid, causal)
        compute = partial(
            block_backward,
            query_seq[begin_row : begin_row + block],
            key_seq,
            value_seq,
            allowed,
            log_totals[:, begin_row : begin_row + block],
            grad_seq[begin_row : begin_row + block],
        )
        grad_query, grad_key, grad_value = compute()
        grad_query_list.append(grad_query)
        grad_key_total = grad_key_total + grad_key
        grad_value_total = grad_value_total + grad_value
    return (jnp.concatenate(grad_query_list, axis=0), grad_key_total, grad_value_total)


def attention_forward(queries, key_rows, value_rows, key_valid, lengths, causal):
    seqs = lengths.shape[0]
    parts = (
        queries.reshape(seqs, -1, queries.shape[1]),
        key_rows.reshape(seqs, -1, key_rows.shape[1]),
        value_rows.reshape(seqs, -1, value_rows.shape[1]),
        key_valid,
        lengths,
    )
    mixed, totals = lax.map(partial(sequence_forward, causal=causal), parts)
    return (mixed.reshape(queries.shape).astype(jnp.bfloat16), totals)


def attention_backward(queries, key_rows, value_rows, key_valid, lengths, totals, grads, causal):
    seqs = lengths.shape[0]
    parts = (
        queries.reshape(seqs, -1, queries.shape[1]),
        key_rows.reshape(seqs, -1, key_rows.shape[1]),
        value_rows.reshape(seqs, -1, value_rows.shape[1]),
        key_valid,
        lengths,
        totals,
        grads.reshape(seqs, -1, grads.shape[1]),
    )
    grad_query, grad_key, grad_value = lax.map(partial(sequence_backward, causal=causal), parts)
    return (
        grad_query.reshape(queries.shape).astype(jnp.bfloat16),
        grad_key.reshape(key_rows.shape).astype(jnp.bfloat16),
        grad_value.reshape(value_rows.shape).astype(jnp.bfloat16),
    )


def run_layer(inputs, memory, cotangent, lengths, key_mask, weights, feeds, norms):
    tok_rows = inputs.shape[0]
    seqs = lengths.shape[0]
    seq_rows = tok_rows // seqs
    mem_rows = memory.shape[0] // seqs
    live = (
        (jnp.arange(seq_rows)[None, :] < lengths[:, None]).reshape(tok_rows, 1).astype(jnp.float32)
    )
    input_float = inputs.astype(jnp.float32)
    projected = jnp.einsum(
        "td,sdc->stc", inputs, weights[0:3], preferred_element_type=jnp.float32
    ).astype(jnp.bfloat16)
    self_q, self_k, self_v = (projected[0], projected[1], projected[2])
    every_key = jnp.ones((seqs, seq_rows), dtype=bool)
    self_low, self_totals = attention_forward(self_q, self_k, self_v, every_key, lengths, True)
    self_out = times_rows(self_low, weights[3])
    first, first_pull = jax.vjp(layer_norm, input_float + self_out, norms[0], norms[1])
    first_low = first.astype(jnp.bfloat16)
    cross_q = times_matrix(first_low, weights[4]).astype(jnp.bfloat16)
    memory_proj = jnp.einsum(
        "td,sdc->stc", memory, weights[5:7], preferred_element_type=jnp.float32
    ).astype(jnp.bfloat16)
    cross_k, cross_v = (memory_proj[0], memory_proj[1])
    key_valid = (key_mask == 1) | (jnp.arange(mem_rows) == 0)[None, :]
    cross_low, cross_totals = attention_forward(
        cross_q, cross_k, cross_v, key_valid, lengths, False
    )
    cross_out = times_rows(cross_low, weights[7])
    second, second_pull = jax.vjp(layer_norm, first + cross_out, norms[2], norms[3])
    second_low = second.astype(jnp.bfloat16)
    inner = times_matrix(second_low, feeds[0])
    active, gelu_pull = jax.vjp(gelu_exact, inner)
    active_low = active.astype(jnp.bfloat16)
    feed_out = times_rows(active_low, feeds[1])
    third, third_pull = jax.vjp(layer_norm, second + feed_out + input_float, norms[4], norms[5])
    output = (live * third).astype(jnp.bfloat16)
    grad_third, gain_three, shift_three = third_pull(live * cotangent.astype(jnp.float32))
    grad_third_low = grad_third.astype(jnp.bfloat16)
    grad_down = outer_rows(grad_third_low, active_low)
    grad_inner = gelu_pull(times_matrix(grad_third_low, feeds[1]))[0].astype(jnp.bfloat16)
    grad_up = outer_rows(second_low, grad_inner)
    grad_second = times_rows(grad_inner, feeds[0]) + grad_third
    grad_second_sum, gain_two, shift_two = second_pull(grad_second)
    grad_second_low = grad_second_sum.astype(jnp.bfloat16)
    grad_cross_out = outer_rows(grad_second_low, cross_low)
    grad_cross_mix = times_matrix(grad_second_low, weights[7]).astype(jnp.bfloat16)
    grad_cq, grad_ck, grad_cv = attention_backward(
        cross_q, cross_k, cross_v, key_valid, lengths, cross_totals, grad_cross_mix, False
    )
    grad_first = times_rows(grad_cq, weights[4]) + grad_second_sum
    grad_memory = times_rows(grad_ck, weights[5]) + times_rows(grad_cv, weights[6])
    grad_first_sum, gain_one, shift_one = first_pull(grad_first)
    grad_first_low = grad_first_sum.astype(jnp.bfloat16)
    grad_self_out = outer_rows(grad_first_low, self_low)
    grad_self_mix = times_matrix(grad_first_low, weights[3]).astype(jnp.bfloat16)
    grad_sq, grad_sk, grad_sv = attention_backward(
        self_q, self_k, self_v, every_key, lengths, self_totals, grad_self_mix, True
    )
    grad_project = (
        times_rows(grad_sq, weights[0])
        + times_rows(grad_sk, weights[1])
        + times_rows(grad_sv, weights[2])
    )
    attention_grads = jnp.stack(
        [
            outer_rows(inputs, grad_sq),
            outer_rows(inputs, grad_sk),
            outer_rows(inputs, grad_sv),
            grad_self_out,
            outer_rows(first_low, grad_cq),
            outer_rows(memory, grad_ck),
            outer_rows(memory, grad_cv),
            grad_cross_out,
        ]
    )
    feed_grads = jnp.stack([grad_up, grad_down])
    norm_grads = jnp.stack([gain_one, shift_one, gain_two, shift_two, gain_three, shift_three])
    return (
        output,
        grad_project,
        grad_first_sum + grad_third,
        grad_memory,
        attention_grads,
        feed_grads,
        norm_grads,
    )


def adam_moments(rotated, moment, second):
    moment_new = BETA_FIRST * moment + (1.0 - BETA_FIRST) * rotated
    second_new = BETA_SECOND * second + (1.0 - BETA_SECOND) * rotated * rotated
    direction = (
        moment_new
        / (1.0 - BETA_FIRST**STEP)
        / (jnp.sqrt(second_new / (1.0 - BETA_SECOND**STEP)) + ADAM_EPSILON)
    )
    return (moment_new, second_new, direction)


def finish(weight, average, update, rate, decay):
    weight_new = weight - rate * (update + decay * weight)
    average_new = AVERAGE_DECAY * average + (1.0 - AVERAGE_DECAY) * weight_new
    return (weight_new, average_new, weight_new.astype(jnp.bfloat16))


def soap_step(weight, grad, moment, second, average, basis, rate, decay):
    rotated = jnp.einsum("src,sce->sre", grad, basis, precision=HIGHEST)
    moment_new, second_new, direction = adam_moments(rotated, moment, second)
    update = jnp.einsum("sre,sce->src", direction, basis, precision=HIGHEST)
    return (moment_new, second_new) + finish(weight, average, update, rate, decay)


def on_device(
    inputs,
    memory,
    cotangent,
    lengths,
    key_mask,
    owner_list,
    attention_master,
    attention_moment,
    attention_second,
    attention_average,
    attention_basis,
    feed_master,
    feed_moment,
    feed_second,
    feed_average,
    feed_basis,
    norm_master,
    norm_moment,
    norm_second,
    norm_average,
):
    groups = lax.axis_size("dp")
    splits = lax.axis_size("tensor")
    column = lax.axis_index("tensor")
    both = ("dp", "tensor")
    width = inputs.shape[1]
    share = inputs.shape[0] // splits
    seqs = lengths.shape[0] // splits

    def own(array, count):
        return lax.dynamic_slice_in_dim(array, column * count, count, 0)

    place = place_matrix(owner_list, width)

    def permuted(array):
        return jnp.dot(own(array, share), place, preferred_element_type=jnp.float32).astype(
            jnp.bfloat16
        )

    def restored(array):
        return jnp.einsum(
            "td,cd->tc", array.astype(jnp.bfloat16), place, preferred_element_type=jnp.float32
        ).astype(jnp.bfloat16)

    def gathered(master):
        slots, rows, cols = master.shape
        full = lax.all_gather(master.astype(jnp.bfloat16), both, axis=0, tiled=False)
        full = full.reshape(groups, splits, slots, rows, cols)
        return full.transpose(2, 0, 3, 1, 4).reshape(slots, groups * rows, splits * cols)

    weights = gathered(attention_master)
    feeds = gathered(feed_master)
    norms = lax.all_gather(norm_master.astype(jnp.bfloat16), "dp", axis=1, tiled=True).astype(
        jnp.float32
    )
    piece = norms.shape[1] // (groups * splits)

    (
        output,
        grad_project,
        grad_residual,
        grad_memory,
        attention_part,
        feed_part,
        norm_grads,
    ) = run_layer(
        permuted(inputs),
        permuted(memory),
        permuted(cotangent),
        own(lengths, seqs),
        own(key_mask, seqs),
        weights,
        feeds,
        norms,
    )
    output = restored(output)
    grad_input = restored(grad_project + grad_residual)
    grad_memory = restored(grad_memory)

    def scattered(part):
        slots, rows, cols = part.shape
        blocks = part.astype(jnp.bfloat16).reshape(
            slots, groups, rows // groups, splits, cols // splits
        )
        blocks = blocks.transpose(1, 3, 0, 2, 4).reshape(
            groups * splits, slots, rows // groups, cols // splits
        )
        return lax.psum_scatter(blocks, both, scatter_dimension=0, tiled=False).astype(jnp.float32)

    norm_blocks = norm_grads.reshape(6, groups * splits, piece).transpose(1, 0, 2)
    norm_owned = lax.psum_scatter(norm_blocks, both, scatter_dimension=0, tiled=False)
    attention_new = soap_step(
        attention_master,
        scattered(attention_part),
        attention_moment,
        attention_second,
        attention_average,
        attention_basis,
        RATE_ATTENTION,
        WEIGHT_DECAY,
    )
    feed_new = soap_step(
        feed_master,
        scattered(feed_part),
        feed_moment,
        feed_second,
        feed_average,
        feed_basis,
        RATE_FEED,
        WEIGHT_DECAY,
    )
    begin_col = column * piece

    def own_columns(array):
        return lax.dynamic_slice_in_dim(array, begin_col, piece, 1)

    moment_new, second_new, direction = adam_moments(
        norm_owned, own_columns(norm_moment), own_columns(norm_second)
    )
    norm_new = (moment_new, second_new) + finish(
        own_columns(norm_master), own_columns(norm_average), direction, RATE_NORMS, 0.0
    )
    return (output, grad_input, grad_memory) + attention_new + feed_new + norm_new


def solution(mesh):
    in_specs = (
        P("dp", None),
        P("dp", None),
        P("dp", None),
        P("dp"),
        P("dp", None),
        P(),
        P(None, "dp", "tensor"),
        P(None, "dp", "tensor"),
        P(None, "dp", "tensor"),
        P(None, "dp", "tensor"),
        P(None, "tensor", None),
        P(None, "dp", "tensor"),
        P(None, "dp", "tensor"),
        P(None, "dp", "tensor"),
        P(None, "dp", "tensor"),
        P(None, "tensor", None),
        P(None, "dp"),
        P(None, "dp"),
        P(None, "dp"),
        P(None, "dp"),
    )
    out_specs = (
        P(("dp", "tensor"), None),
        P(("dp", "tensor"), None),
        P(("dp", "tensor"), None),
        P(None, "dp", "tensor"),
        P(None, "dp", "tensor"),
        P(None, "dp", "tensor"),
        P(None, "dp", "tensor"),
        P(None, "dp", "tensor"),
        P(None, "dp", "tensor"),
        P(None, "dp", "tensor"),
        P(None, "dp", "tensor"),
        P(None, "dp", "tensor"),
        P(None, "dp", "tensor"),
        P(None, ("dp", "tensor")),
        P(None, ("dp", "tensor")),
        P(None, ("dp", "tensor")),
        P(None, ("dp", "tensor")),
        P(None, ("dp", "tensor")),
    )
    return jax.shard_map(
        on_device, mesh=mesh, in_specs=in_specs, out_specs=out_specs, check_vma=False
    )
```

```python
import math

import jax
import jax.numpy as jnp
from jax import lax
from jax.experimental import pallas as pl
from jax.experimental.pallas import tpu as pltpu
from jax.sharding import PartitionSpec as P

HDIM = 64
STEP = 10


FLOOR_SCORE = -1e30
NORM_EPSILON = 1e-05
BETA_FIRST = 0.9
BETA_SECOND = 0.95
ADAM_EPSILON = 1e-08
AVERAGE_DECAY = 0.6
RATE_ATTENTION = 0.07
RATE_FEED = 0.03
RATE_NORMS = 0.5
WEIGHT_DECAY = 0.01
HIGHEST = lax.Precision.HIGHEST


def place_matrix(owner_list, width):
    blocks = owner_list.shape[0]
    rows = width // blocks
    here = jnp.arange(width, dtype=jnp.int32)
    block = here // rows
    target = jnp.sum(
        jnp.where(block[:, None] == jnp.arange(blocks)[None, :], owner_list[None, :], 0), axis=1
    ) * rows + here % rows
    return (target[:, None] == here[None, :]).astype(jnp.bfloat16)


BF = jnp.bfloat16
F32 = jnp.float32
PAIR = 2 * HDIM
QUERY_BLOCK = 512
ROWS = 64
FEED_ROWS = 256


def nn(left, right):
    return lax.dot_general(left, right, (((1,), (0,)), ((), ())), preferred_element_type=F32)


def nt(left, right):
    return lax.dot_general(left, right, (((1,), (1,)), ((), ())), preferred_element_type=F32)


def tn(left, right):
    return lax.dot_general(left, right, (((0,), (0,)), ((), ())), preferred_element_type=F32)


def lane(shape):
    return lax.broadcasted_iota(jnp.int32, shape, 1)


def causal_floor(scores, key_begin, query_begin):
    key = lax.broadcasted_iota(jnp.int32, scores.shape, 0) + key_begin
    query = lax.broadcasted_iota(jnp.int32, scores.shape, 1) + query_begin
    return jnp.where(key <= query, scores, FLOOR_SCORE)


def head_queries(scaled, half, guarded):
    here = lane(scaled.shape)
    other = jnp.zeros_like(scaled)
    if guarded:
        other = jnp.where(here == (1 - half) * HDIM, jnp.ones_like(scaled), other)
    return jnp.where(here // HDIM == half, scaled, other)


def guarded_keys(keys, guard, half):
    here = lane(keys.shape)
    other = jnp.where(here == (1 - half) * HDIM, guard, jnp.zeros_like(keys))
    return jnp.where(here // HDIM == half, keys, other)


def key_chunks(begin, rows, keys, causal):
    if not causal:
        return [(0, keys, False)]
    chunks = [(0, begin, False)] if begin else []
    return chunks + [(begin, rows, True)]


def pair_forward(q, k, v, guard, mix, logs, pair, keys_ref, values_t, causal):
    rows = q[0].shape[0]
    keys = k[0].shape[0]

    def columns(operand):
        return pl.ds(pl.multiple_of(operand[1] + pair * PAIR, PAIR), PAIR)

    key_all = k[0][:, columns(k)]
    values_t[...] = v[0][:, columns(v)].T
    for half in range(2):
        keys_ref[half] = key_all if guard is None else guarded_keys(key_all, guard[...], half)
    block = min(QUERY_BLOCK if causal else rows, rows)
    for begin in range(0, rows, block):
        scaled = q[0][begin : begin + block, columns(q)] * jnp.asarray(HDIM**-0.5, BF)
        queries = [head_queries(scaled, half, guard is not None) for half in range(2)]
        chunks = key_chunks(begin, block, keys, causal)
        scores = [[], []]
        for first, count, diagonal in chunks:
            for half in range(2):
                score = nt(keys_ref[half, first : first + count, :], queries[half])
                scores[half].append(causal_floor(score, first, begin) if diagonal else score)
        tops = []
        for half in range(2):
            top = jnp.max(scores[half][0], axis=0, keepdims=True)
            for score in scores[half][1:]:
                top = jnp.maximum(top, jnp.max(score, axis=0, keepdims=True))
            tops.append(top)
        mixed = []
        for half in range(2):
            total = None
            out = None
            for (first, count, _), score in zip(chunks, scores[half]):
                expd = jnp.exp(score - tops[half])
                part = jnp.sum(expd, axis=0, keepdims=True)
                value = values_t[half * HDIM : (half + 1) * HDIM, first : first + count]
                term = nn(value, expd.astype(BF))
                total = part if total is None else total + part
                out = term if out is None else out + term
            mixed.append(out * (1.0 / total))
            logs[pair, half : half + 1, begin : begin + block] = tops[half] + jnp.log(total)
        mix[0][begin : begin + block, columns(mix)] = jnp.concatenate(mixed, axis=0).T.astype(BF)


def pair_backward(q, k, v, guard, mix, grad_mix, logs, pair, keys_ref, sums, grads, causal):
    rows = q[0].shape[0]
    keys = k[0].shape[0]
    grad_key, grad_value = sums

    def columns(operand):
        return pl.ds(pl.multiple_of(operand[1] + pair * PAIR, PAIR), PAIR)

    key_all = k[0][:, columns(k)]
    for half in range(2):
        keys_ref[half] = key_all if guard is None else guarded_keys(key_all, guard[...], half)
    keys_t = key_all.T
    block = min(QUERY_BLOCK, rows)
    for begin in range(0, rows, block):
        here = slice(begin, begin + block)
        scaled = q[0][here, columns(q)] * jnp.asarray(HDIM**-0.5, BF)
        grad = grad_mix[0][here, columns(grad_mix)]
        weighed = (grad.astype(F32) * mix[0][here, columns(mix)].astype(F32)).T
        parts = []
        for half in range(2):
            own = lane(scaled.shape) // HDIM == half
            centre = jnp.sum(weighed[half * HDIM : (half + 1) * HDIM, :], axis=0, keepdims=True)
            parts.append(
                (
                    head_queries(scaled, half, guard is not None),
                    jnp.where(own, scaled, jnp.zeros_like(scaled)),
                    jnp.where(own, grad, jnp.zeros_like(grad)),
                    centre,
                    logs[pair, half : half + 1, here],
                )
            )
        grad_query = [None, None]
        for first, count, diagonal in key_chunks(begin, block, keys, causal):
            there = slice(first, first + count)
            value = v[0][there, columns(v)]
            raw = []
            for half in range(2):
                score = nt(keys_ref[half, there, :], parts[half][0])
                if diagonal:
                    score = causal_floor(score, first, begin)
                raw.append((score, nt(value, parts[half][2])))
            low = []
            for half in range(2):
                prob = jnp.exp(raw[half][0] - parts[half][4])
                grad_score = (prob * (raw[half][1] - parts[half][3])).astype(BF)
                low.append((prob.astype(BF), grad_score))
            add_value = nn(low[0][0], parts[0][2]) + nn(low[1][0], parts[1][2])
            add_key = nn(low[0][1], parts[0][1]) + nn(low[1][1], parts[1][1])
            fresh = diagonal if causal else begin == 0
            if fresh:
                grad_value[there, :] = add_value
                grad_key[there, :] = add_key
            else:
                grad_value[there, :] += add_value
                grad_key[there, :] += add_key
            for half in range(2):
                term = nn(keys_t[half * HDIM : (half + 1) * HDIM, there], low[half][1])
                grad_query[half] = term if grad_query[half] is None else grad_query[half] + term
        both = jnp.concatenate(grad_query, axis=0).T * HDIM**-0.5
        grads[0][0][here, columns(grads[0])] = both.astype(BF)
    grads[1][0][:, columns(grads[1])] = grad_key[...].astype(BF)
    grads[2][0][:, columns(grads[2])] = grad_value[...].astype(BF)


def row_loop(rows, body, begin_row=0):
    step = min(ROWS, rows)

    def turn(index, carry):
        body(pl.ds(pl.multiple_of(begin_row + index * step, step), step))
        return carry

    lax.fori_loop(0, rows // step, turn, 0, unroll=2)


def standardised(values):
    centred = values - jnp.mean(values, axis=-1, keepdims=True)
    scale = lax.rsqrt(jnp.mean(centred * centred, axis=-1, keepdims=True) + NORM_EPSILON)
    return centred * scale, scale


def norm_gradient(grad, gain, unit, scale):
    weighted = grad * gain
    return scale * (
        weighted
        - jnp.mean(weighted, axis=-1, keepdims=True)
        - unit * jnp.mean(weighted * unit, axis=-1, keepdims=True)
    )


def fold_rows(values):
    return jnp.sum(values.reshape(values.shape[0] // 8, 8, values.shape[1]), axis=0)


def wide(scale):
    return jnp.broadcast_to(scale, (scale.shape[0], 128))


def store_blocks(blocks, slot, grad, first_split=0):
    groups, _, _, rows, cols = blocks.shape
    low = grad.astype(BF)
    for split in range(low.shape[1] // cols):
        for group in range(groups):
            blocks[group, first_split + split, slot] = low[
                group * rows : (group + 1) * rows, split * cols : (split + 1) * cols
            ]


class Moves:
    def __init__(self, semaphores):
        self.semaphores = semaphores
        self.count = 0
        self.open = []

    def start(self, source, target):
        copy = pltpu.make_async_copy(source, target, self.semaphores.at[self.count])
        self.count += 1
        copy.start()
        return copy

    def send(self, source, target):
        self.open.append(self.start(source, target))

    def finish(self):
        for copy in self.open:
            copy.wait()


def fetch_weights(blocks, weights, semaphore, first, slots):
    groups, splits, _, rows, cols = blocks.shape

    def turn(group, carry):
        for split in range(splits):
            pltpu.make_async_copy(
                blocks.at[group, split, pl.ds(first, slots)],
                weights.at[
                    :, pl.ds(pl.multiple_of(group * rows, rows), rows), pl.ds(split * cols, cols)
                ],
                semaphore,
            ).start()
        return carry

    lax.fori_loop(0, groups, turn, 0)
    return pltpu.make_async_copy(weights, weights, semaphore)


def self_forward(
    x_hbm, place_hbm, blocks_hbm,
    low_hbm, qkv_hbm, mix_hbm, logs_hbm, unit_hbm, scale_hbm,
    x, place, weights, low, qkv, mix, logs, unit, scale, keys_ref, values_t, semaphores, gather_sem,
):
    moves = Moves(semaphores)
    arrivals = [moves.start(x_hbm, x), moves.start(place_hbm, place)]
    gathered = fetch_weights(blocks_hbm, weights, gather_sem, 0, 4)
    for copy in arrivals:
        copy.wait()
    low[...] = nn(x[...], place[...]).astype(BF)
    moves.send(low, low_hbm)
    gathered.wait()
    width = low.shape[1]
    for part in range(3):
        qkv[:, part * width : (part + 1) * width] = nn(low[...], weights[part]).astype(BF)
    moves.send(qkv, qkv_hbm)

    def turn(pair, carry):
        pair_forward(
            (qkv, 0), (qkv, width), (qkv, 2 * width), None, (mix, 0), logs, pair, keys_ref, values_t, True
        )
        return carry

    lax.fori_loop(0, width // PAIR, turn, 0)
    moves.send(mix, mix_hbm)
    moves.send(logs, logs_hbm)
    unit[...] = nt(mix[...], weights[3])

    def normalise(rows):
        unit_rows, scale_rows = standardised(low[rows, :].astype(F32) + unit[rows, :])
        unit[rows, :] = unit_rows
        scale[rows, :] = wide(scale_rows)

    row_loop(low.shape[0], normalise)
    moves.send(unit, unit_hbm)
    moves.send(scale, scale_hbm)
    moves.finish()


def cross_forward(
    memory_hbm, place_hbm, guard_hbm, blocks_hbm, norms, unit_before_hbm,
    low_hbm, query_hbm, key_value_hbm, mix_hbm, logs_hbm, unit_hbm, scale_hbm,
    memory, place, guard, unit_before, weights, low, first_low, query, key_value, mix, logs, unit, scale,
    keys_ref, values_t, semaphores, gather_sem,
):
    moves = Moves(semaphores)
    arrivals = [moves.start(memory_hbm, memory), moves.start(place_hbm, place)]
    gathered = fetch_weights(blocks_hbm, weights, gather_sem, 4, 4)
    before = moves.start(unit_before_hbm, unit_before)
    masked = moves.start(guard_hbm, guard)
    for copy in arrivals:
        copy.wait()
    low[...] = nn(memory[...], place[...]).astype(BF)
    moves.send(low, low_hbm)
    before.wait()
    width = low.shape[1]

    def first_of(rows):
        return unit_before[rows, :] * norms[0:1, :] + norms[1:2, :]

    def lower(rows):
        first_low[rows, :] = first_of(rows).astype(BF)

    row_loop(unit.shape[0], lower)
    gathered.wait()
    query[...] = nn(first_low[...], weights[0]).astype(BF)
    moves.send(query, query_hbm)
    for part in range(2):
        key_value[:, part * width : (part + 1) * width] = nn(low[...], weights[1 + part]).astype(BF)
    moves.send(key_value, key_value_hbm)
    masked.wait()

    def turn(pair, carry):
        pair_forward(
            (query, 0), (key_value, 0), (key_value, width), guard, (mix, 0), logs, pair, keys_ref, values_t, False
        )
        return carry

    lax.fori_loop(0, width // PAIR, turn, 0)
    moves.send(mix, mix_hbm)
    moves.send(logs, logs_hbm)
    unit[...] = nt(mix[...], weights[3])

    def normalise(rows):
        unit_rows, scale_rows = standardised(first_of(rows) + unit[rows, :])
        unit[rows, :] = unit_rows
        scale[rows, :] = wide(scale_rows)

    row_loop(unit.shape[0], normalise)
    moves.send(unit, unit_hbm)
    moves.send(scale, scale_hbm)
    moves.finish()


def gelu_both(values):
    half = 0.5 * (1.0 + lax.erf(values * (0.5**0.5)))
    bell = jnp.exp(-0.5 * values * values) * (0.5 / math.pi) ** 0.5
    return values * half, half + values * bell


def feed_both(
    length_ref, low_hbm, cotangent_hbm, place_hbm, blocks_hbm, norms, unit_hbm, scale_hbm,
    output_hbm, grad_third_hbm, grad_second_hbm, grads_hbm, norm_grads,
    low, cotangent, place, weights, unit, scale, second_low, third_low, active, slope, inner_grad, output,
    grad_third, grad_second, grads, sums, semaphores, gather_sem,
):
    moves = Moves(semaphores)
    first = [moves.start(unit_hbm, unit)]
    gathered = fetch_weights(blocks_hbm, weights, gather_sem, 0, 2)
    others = [
        moves.start(low_hbm, low),
        moves.start(cotangent_hbm, cotangent),
        moves.start(place_hbm, place),
        moves.start(scale_hbm, scale),
    ]
    rows_all, width = low.shape
    hidden = weights.shape[2]
    chunk = min(width, hidden)
    sums[...] = jnp.zeros_like(sums)
    for copy in first:
        copy.wait()

    def second_of(rows):
        return unit[rows, :] * norms[2:3, :] + norms[3:4, :]

    def lower(rows):
        second_low[rows, :] = second_of(rows).astype(BF)

    row_loop(rows_all, lower)
    gathered.wait()
    for copy in others:
        copy.wait()
    length = length_ref[0]
    tile_rows = min(FEED_ROWS, rows_all)

    def tile(index, carry):
        begin = pl.multiple_of(index * tile_rows, tile_rows)
        here = pl.ds(begin, tile_rows)
        cot = nn(cotangent[here, :], place[...])
        for begin_col in range(0, hidden, chunk):
            cols = slice(begin_col, begin_col + chunk)
            value, slope_part = gelu_both(nn(second_low[here, :], weights[0, :, cols]))
            active[here, cols] = value.astype(BF)
            slope[:, cols] = slope_part
        fed = nt(active[here, :], weights[1])
        for part in range(0, tile_rows, ROWS):
            rows = pl.ds(pl.multiple_of(begin + part, ROWS), ROWS)
            place_rows = lax.broadcasted_iota(jnp.int32, (ROWS, 1), 0) + (begin + part)
            live = jnp.where(place_rows < length, 1.0, 0.0)
            third_sum = second_of(rows) + fed[part : part + ROWS, :] + low[rows, :].astype(F32)
            unit_rows, scale_rows = standardised(third_sum)
            third = live * (unit_rows * norms[4:5, :] + norms[5:6, :])
            output[rows, :] = third.astype(BF)
            grad = live * cot[part : part + ROWS, :]
            grad_rows = norm_gradient(grad, norms[4:5, :], unit_rows, scale_rows)
            grad_third[rows, :] = grad_rows
            third_low[rows, :] = grad_rows.astype(BF)
            sums[2] += fold_rows(grad * unit_rows)
            sums[3] += fold_rows(grad)
        output[here, :] = nt(output[here, :], place[...]).astype(BF)
        for begin_col in range(0, hidden, chunk):
            cols = slice(begin_col, begin_col + chunk)
            back = nn(third_low[here, :], weights[1, :, cols]) * slope[:, cols]
            inner_grad[here, cols] = back.astype(BF)
        fed_back = nt(inner_grad[here, :], weights[0])
        for part in range(0, tile_rows, ROWS):
            rows = pl.ds(pl.multiple_of(begin + part, ROWS), ROWS)
            unit_rows = unit[rows, :]
            grad = fed_back[part : part + ROWS, :] + grad_third[rows, :]
            grad_second[rows, :] = norm_gradient(
                grad, norms[2:3, :], unit_rows, scale[rows, 0:1]
            )
            sums[0] += fold_rows(grad * unit_rows)
            sums[1] += fold_rows(grad)
        return carry

    lax.fori_loop(0, rows_all // tile_rows, tile, 0)
    moves.send(output, output_hbm)
    moves.send(grad_third, grad_third_hbm)
    moves.send(grad_second, grad_second_hbm)
    norm_grads[...] = jnp.sum(sums[...], axis=1)
    cols_one = grads.shape[4]
    for split in range(hidden // cols_one):
        cols = slice(split * cols_one, (split + 1) * cols_one)
        store_blocks(grads, 0, tn(second_low[...], inner_grad[:, cols]), split)
        store_blocks(grads, 1, tn(third_low[...], active[:, cols]), split)
    moves.send(grads, grads_hbm)
    moves.finish()


def cross_backward(
    grad_second_hbm, mix_hbm, blocks_hbm, query_hbm, key_value_hbm, logs_hbm, guard_hbm, memory_low_hbm,
    unit_hbm, scale_hbm, place_hbm, norms,
    grad_memory_hbm, grad_first_hbm, grads_hbm, norm_grads,
    grad_second, mix, weights, query, key_value, logs, guard, memory_low, unit, scale, place,
    second_low, grad_mix, query_grad, key_value_grad, first_low, grad_memory, grad_first, grads, sums,
    keys_ref, key_sum, value_sum, semaphores, gather_sem,
):
    moves = Moves(semaphores)
    start = moves.start(grad_second_hbm, grad_second)
    gathered = fetch_weights(blocks_hbm, weights, gather_sem, 4, 4)
    stage = [
        moves.start(mix_hbm, mix),
        moves.start(query_hbm, query),
        moves.start(key_value_hbm, key_value),
        moves.start(logs_hbm, logs),
        moves.start(guard_hbm, guard),
    ]
    late = [
        moves.start(memory_low_hbm, memory_low),
        moves.start(unit_hbm, unit),
        moves.start(scale_hbm, scale),
        moves.start(place_hbm, place),
    ]
    rows_all, width = mix.shape
    start.wait()

    def lower(rows):
        second_low[rows, :] = grad_second[rows, :].astype(BF)

    row_loop(rows_all, lower)
    gathered.wait()
    for copy in stage:
        copy.wait()
    grad_mix[...] = nn(second_low[...], weights[3]).astype(BF)

    def turn(pair, carry):
        pair_backward(
            (query, 0), (key_value, 0), (key_value, width), guard, (mix, 0), (grad_mix, 0), logs, pair,
            keys_ref, (key_sum, value_sum), ((query_grad, 0), (key_value_grad, 0), (key_value_grad, width)), False,
        )
        return carry

    lax.fori_loop(0, width // PAIR, turn, 0)
    for copy in late:
        copy.wait()
    unit_low = nt(key_value_grad[:, :width], weights[1]) + nt(key_value_grad[:, width:], weights[2])
    grad_memory[...] = unit_low.astype(BF)
    grad_memory[...] = nt(grad_memory[...], place[...]).astype(BF)
    moves.send(grad_memory, grad_memory_hbm)
    grad_first[...] = nt(query_grad[...], weights[0])
    sums[...] = jnp.zeros_like(sums)

    def back(rows):
        unit_rows = unit[rows, :]
        grad = grad_first[rows, :] + grad_second[rows, :]
        first_low[rows, :] = (unit_rows * norms[0:1, :] + norms[1:2, :]).astype(BF)
        grad_first[rows, :] = norm_gradient(grad, norms[0:1, :], unit_rows, scale[rows, 0:1])
        sums[0] += fold_rows(grad * unit_rows)
        sums[1] += fold_rows(grad)

    row_loop(rows_all, back)
    moves.send(grad_first, grad_first_hbm)
    norm_grads[...] = jnp.sum(sums[...], axis=1)
    store_blocks(grads, 0, tn(first_low[...], query_grad[...]))
    store_blocks(grads, 1, tn(memory_low[...], key_value_grad[:, :width]))
    store_blocks(grads, 2, tn(memory_low[...], key_value_grad[:, width:]))
    store_blocks(grads, 3, tn(second_low[...], mix[...]))
    moves.send(grads, grads_hbm)
    moves.finish()


def self_backward(
    grad_first_hbm, mix_hbm, blocks_hbm, qkv_hbm, logs_hbm, low_hbm, grad_third_hbm, place_hbm,
    grad_input_hbm, grads_hbm,
    grad_first, mix, weights, qkv, logs, low, grad_third, place,
    first_low, grad_mix, qkv_grad, grad_input, grads, keys_ref, key_sum, value_sum, semaphores, gather_sem,
):
    moves = Moves(semaphores)
    start = moves.start(grad_first_hbm, grad_first)
    gathered = fetch_weights(blocks_hbm, weights, gather_sem, 0, 4)
    stage = [moves.start(mix_hbm, mix), moves.start(qkv_hbm, qkv), moves.start(logs_hbm, logs)]
    late = [
        moves.start(low_hbm, low),
        moves.start(grad_third_hbm, grad_third),
        moves.start(place_hbm, place),
    ]
    rows_all, width = mix.shape
    start.wait()

    def lower(rows):
        first_low[rows, :] = grad_first[rows, :].astype(BF)

    row_loop(rows_all, lower)
    gathered.wait()
    for copy in stage:
        copy.wait()
    grad_mix[...] = nn(first_low[...], weights[3]).astype(BF)

    def turn(pair, carry):
        pair_backward(
            (qkv, 0), (qkv, width), (qkv, 2 * width), None, (mix, 0), (grad_mix, 0), logs, pair,
            keys_ref, (key_sum, value_sum), ((qkv_grad, 0), (qkv_grad, width), (qkv_grad, 2 * width)), True,
        )
        return carry

    lax.fori_loop(0, width // PAIR, turn, 0)
    for copy in late:
        copy.wait()
    store_blocks(grads, 3, tn(first_low[...], mix[...]))
    for part in range(3):
        store_blocks(grads, part, tn(low[...], qkv_grad[:, part * width : (part + 1) * width]))
    moves.send(grads, grads_hbm)
    total = grad_first[...] + grad_third[...]
    for part in range(3):
        total = total + nt(qkv_grad[:, part * width : (part + 1) * width], weights[part])
    grad_input[...] = total.astype(BF)
    grad_input[...] = nt(grad_input[...], place[...]).astype(BF)
    moves.send(grad_input, grad_input_hbm)
    moves.finish()


ANY = pl.BlockSpec(memory_space=pl.ANY)
WHOLE = pl.BlockSpec(memory_space=pltpu.VMEM)
SCALAR = pl.BlockSpec(memory_space=pltpu.SMEM)


def shape_of(array):
    return jax.ShapeDtypeStruct(array[0], array[1])


def run_kernel(body, name, operands, specs, outs, out_specs, scratch, copies, limit, flops):
    moved = sum(math.prod(s) * jnp.dtype(d).itemsize for s, d in outs)
    moved += sum(math.prod(o.shape) * o.dtype.itemsize for o in operands)
    return pl.pallas_call(
        body,
        name=name,
        in_specs=specs,
        out_specs=out_specs,
        out_shape=[shape_of(o) for o in outs],
        scratch_shapes=[pltpu.VMEM(s, d) for s, d in scratch]
        + [pltpu.SemaphoreType.DMA((copies,)), pltpu.SemaphoreType.DMA],
        compiler_params=pltpu.CompilerParams(vmem_limit_bytes=limit),
        cost_estimate=pl.CostEstimate(flops=flops, bytes_accessed=moved, transcendentals=0),
    )(*operands)


def run_layer(x, memory, cotangent, length, guard, place, attention, feed, norms):
    rows, width = x.shape
    keys = memory.shape[0]
    groups, splits, _, own_rows, own_cols = attention.shape
    hidden = splits * feed.shape[4]
    pairs = width // PAIR
    wide_low, wide_full = ((rows, width), BF), ((rows, width), F32)
    memory_low_t = ((keys, width), BF)
    scale_t = ((rows, 128), F32)
    logs_t = ((pairs, 2, rows), F32)
    place_t = ((width, width), BF)
    four = ((4, width, width), BF)
    qkv_t = ((rows, 3 * width), BF)
    key_value_t = ((keys, 2 * width), BF)
    guard_t = ((keys, PAIR), BF)
    keys_t = ((2, keys, PAIR), BF)
    values_t = ((PAIR, keys), BF)
    key_sum_t = ((keys, PAIR), F32)
    blocks_t = ((groups, splits, 4, own_rows, own_cols), BF)
    feed_blocks_t = ((groups, splits, 2, own_rows, feed.shape[4]), BF)
    pair_flops = 2 * rows * keys * width
    dense = 2 * rows * width * width

    low, qkv, self_mix, self_logs, unit_one, scale_one = run_kernel(
        self_forward, "self_forward",
        (x, place, attention), [ANY] * 3,
        [wide_low, qkv_t, wide_low, logs_t, wide_full, scale_t], [ANY] * 6,
        [wide_low, place_t, four, wide_low, qkv_t, wide_low, logs_t, wide_full, scale_t, keys_t, values_t],
        16, 48 << 20, 5 * dense + 6 * pair_flops,
    )
    memory_low, query, key_value, cross_mix, cross_logs, unit_two, scale_two = run_kernel(
        cross_forward, "cross_forward",
        (memory, place, guard, attention, norms, unit_one), [ANY] * 4 + [WHOLE, ANY],
        [memory_low_t, wide_low, key_value_t, wide_low, logs_t, wide_full, scale_t], [ANY] * 7,
        [memory_low_t, place_t, guard_t, wide_full, four, memory_low_t, wide_low, wide_low, key_value_t,
         wide_low, logs_t, wide_full, scale_t, keys_t, values_t],
        16, 56 << 20, 5 * dense + 8 * pair_flops,
    )
    output, grad_third, grad_second, feed_grads, feed_norms = run_kernel(
        feed_both, "feed_both",
        (length, low, cotangent, place, feed, norms, unit_two, scale_two),
        [SCALAR] + [ANY] * 4 + [WHOLE] + [ANY] * 2,
        [wide_low, wide_full, wide_full, feed_blocks_t, ((4, width), F32)], [ANY] * 4 + [WHOLE],
        [wide_low, wide_low, place_t, ((2, width, hidden), BF), wide_full, scale_t, wide_low, wide_low,
         ((rows, hidden), BF), ((min(FEED_ROWS, rows), hidden), F32), ((rows, hidden), BF), wide_low,
         wide_full, wide_full, feed_blocks_t, ((4, 8, width), F32)],
        16, 56 << 20, 2 * dense + 12 * rows * width * hidden,
    )
    grad_memory, grad_first, cross_grads, cross_norms = run_kernel(
        cross_backward, "cross_backward",
        (grad_second, cross_mix, attention, query, key_value, cross_logs, guard, memory_low, unit_one,
         scale_one, place, norms),
        [ANY] * 11 + [WHOLE],
        [memory_low_t, wide_full, blocks_t, ((2, width), F32)], [ANY] * 3 + [WHOLE],
        [wide_full, wide_low, four, wide_low, key_value_t, logs_t, guard_t, memory_low_t, wide_full, scale_t,
         place_t, wide_low, wide_low, wide_low, key_value_t, wide_low, memory_low_t, wide_full, blocks_t,
         ((2, 8, width), F32), keys_t, key_sum_t, key_sum_t],
        24, 58 << 20, 9 * dense + 20 * pair_flops,
    )
    grad_input, self_grads = run_kernel(
        self_backward, "self_backward",
        (grad_first, self_mix, attention, qkv, self_logs, low, grad_third, place), [ANY] * 8,
        [wide_low, blocks_t], [ANY] * 2,
        [wide_full, wide_low, four, qkv_t, logs_t, wide_low, wide_full, place_t, wide_low, wide_low, qkv_t,
         wide_low, blocks_t, keys_t, key_sum_t, key_sum_t],
        16, 56 << 20, 9 * dense + 15 * pair_flops,
    )
    norm_grads = jnp.concatenate([cross_norms, feed_norms], axis=0)
    return output, grad_input, grad_memory, self_grads, cross_grads, feed_grads, norm_grads


def adam_moments(rotated, moment, second):
    moment_new = BETA_FIRST * moment + (1.0 - BETA_FIRST) * rotated
    second_new = BETA_SECOND * second + (1.0 - BETA_SECOND) * rotated * rotated
    direction = (
        moment_new
        / (1.0 - BETA_FIRST**STEP)
        / (jnp.sqrt(second_new / (1.0 - BETA_SECOND**STEP)) + ADAM_EPSILON)
    )
    return (moment_new, second_new, direction)


def finish(weight, average, update, rate, decay):
    weight_new = weight - rate * (update + decay * weight)
    average_new = AVERAGE_DECAY * average + (1.0 - AVERAGE_DECAY) * weight_new
    return (weight_new, average_new, weight_new.astype(jnp.bfloat16))


def soap_step(weight, grad, moment, second, average, basis, rate, decay):
    rotated = jnp.einsum("src,sce->sre", grad, basis, precision=HIGHEST)
    moment_new, second_new, direction = adam_moments(rotated, moment, second)
    update = jnp.einsum("sre,sce->src", direction, basis, precision=HIGHEST)
    return (moment_new, second_new) + finish(weight, average, update, rate, decay)


def on_device(
    inputs,
    memory,
    cotangent,
    lengths,
    key_mask,
    owner_list,
    attention_master,
    attention_moment,
    attention_second,
    attention_average,
    attention_basis,
    feed_master,
    feed_moment,
    feed_second,
    feed_average,
    feed_basis,
    norm_master,
    norm_moment,
    norm_second,
    norm_average,
):
    groups = lax.axis_size("dp")
    splits = lax.axis_size("tensor")
    column = lax.axis_index("tensor")
    both = ("dp", "tensor")
    width = inputs.shape[1]
    share = inputs.shape[0] // splits
    seqs = lengths.shape[0] // splits

    def own(array, count):
        return lax.dynamic_slice_in_dim(array, column * count, count, 0)

    place = place_matrix(owner_list, width)

    def gathered(master):
        blocks = lax.all_gather(master.astype(BF), both, axis=0, tiled=False)
        return blocks.reshape(groups, splits, *master.shape)

    norms = lax.all_gather(norm_master.astype(BF), "dp", axis=1, tiled=True).astype(F32)
    piece = norms.shape[1] // (groups * splits)
    key_rows = memory.shape[0] // splits
    valid = (own(key_mask, seqs) == 1) | (jnp.arange(key_rows) == 0)[None, :]
    guard = jnp.where(valid, 0.0, FLOOR_SCORE).astype(BF)
    guard = jnp.broadcast_to(guard.reshape(key_rows, 1), (key_rows, PAIR))

    output, grad_input, grad_memory, self_grads, cross_grads, feed_grads, norm_grads = run_layer(
        own(inputs, share),
        own(memory, key_rows),
        own(cotangent, share),
        own(lengths, seqs),
        guard,
        place,
        gathered(attention_master),
        gathered(feed_master),
        jnp.concatenate([norms, jnp.zeros((2, width), F32)], axis=0),
    )

    def scattered(blocks):
        blocks = blocks.reshape(groups * splits, *blocks.shape[2:])
        return lax.psum_scatter(blocks, both, scatter_dimension=0, tiled=False).astype(F32)

    feed_owned = scattered(feed_grads)
    cross_owned = scattered(cross_grads)
    attention_owned = jnp.concatenate([scattered(self_grads), cross_owned], axis=0)
    norm_blocks = norm_grads.reshape(6, groups * splits, piece).transpose(1, 0, 2)
    norm_owned = lax.psum_scatter(norm_blocks, both, scatter_dimension=0, tiled=False)
    attention_new = soap_step(
        attention_master,
        attention_owned,
        attention_moment,
        attention_second,
        attention_average,
        attention_basis,
        RATE_ATTENTION,
        WEIGHT_DECAY,
    )
    feed_new = soap_step(
        feed_master,
        feed_owned,
        feed_moment,
        feed_second,
        feed_average,
        feed_basis,
        RATE_FEED,
        WEIGHT_DECAY,
    )
    begin_col = column * piece

    def own_columns(array):
        return lax.dynamic_slice_in_dim(array, begin_col, piece, 1)

    moment_new, second_new, direction = adam_moments(
        norm_owned, own_columns(norm_moment), own_columns(norm_second)
    )
    norm_new = (moment_new, second_new) + finish(
        own_columns(norm_master), own_columns(norm_average), direction, RATE_NORMS, 0.0
    )
    return (output, grad_input, grad_memory) + attention_new + feed_new + norm_new


def solution(mesh):
    in_specs = (
        P("dp", None),
        P("dp", None),
        P("dp", None),
        P("dp"),
        P("dp", None),
        P(),
        P(None, "dp", "tensor"),
        P(None, "dp", "tensor"),
        P(None, "dp", "tensor"),
        P(None, "dp", "tensor"),
        P(None, "tensor", None),
        P(None, "dp", "tensor"),
        P(None, "dp", "tensor"),
        P(None, "dp", "tensor"),
        P(None, "dp", "tensor"),
        P(None, "tensor", None),
        P(None, "dp"),
        P(None, "dp"),
        P(None, "dp"),
        P(None, "dp"),
    )
    out_specs = (
        P(("dp", "tensor"), None),
        P(("dp", "tensor"), None),
        P(("dp", "tensor"), None),
        P(None, "dp", "tensor"),
        P(None, "dp", "tensor"),
        P(None, "dp", "tensor"),
        P(None, "dp", "tensor"),
        P(None, "dp", "tensor"),
        P(None, "dp", "tensor"),
        P(None, "dp", "tensor"),
        P(None, "dp", "tensor"),
        P(None, "dp", "tensor"),
        P(None, "dp", "tensor"),
        P(None, ("dp", "tensor")),
        P(None, ("dp", "tensor")),
        P(None, ("dp", "tensor")),
        P(None, ("dp", "tensor")),
        P(None, ("dp", "tensor")),
    )
    return jax.shard_map(
        on_device, mesh=mesh, in_specs=in_specs, out_specs=out_specs, check_vma=False
    )
```

```python
import functools
import math

import jax
import jax.numpy as jnp
from jax import lax
from jax.experimental import pallas as pl
from jax.experimental.pallas import tpu as pltpu
from jax.sharding import PartitionSpec as P

HDIM = 64
STEP = 10


FLOOR_SCORE = -1e30
NORM_EPSILON = 1e-05
BETA_FIRST = 0.9
BETA_SECOND = 0.95
ADAM_EPSILON = 1e-08
AVERAGE_DECAY = 0.6
RATE_ATTENTION = 0.07
RATE_FEED = 0.03
RATE_NORMS = 0.5
WEIGHT_DECAY = 0.01
HIGHEST = lax.Precision.HIGHEST


def place_matrix(owner_list, width):
    blocks = owner_list.shape[0]
    rows = width // blocks
    here = jnp.arange(width, dtype=jnp.int32)
    block = here // rows
    target = jnp.sum(
        jnp.where(block[:, None] == jnp.arange(blocks)[None, :], owner_list[None, :], 0), axis=1
    ) * rows + here % rows
    return (target[:, None] == here[None, :]).astype(jnp.bfloat16)


BF = jnp.bfloat16
F32 = jnp.float32
PAIR = 2 * HDIM
QUERY_BLOCK = 512
ROWS = 64
FEED_ROWS = 256


def nn(left, right):
    return lax.dot_general(left, right, (((1,), (0,)), ((), ())), preferred_element_type=F32)


def nt(left, right):
    return lax.dot_general(left, right, (((1,), (1,)), ((), ())), preferred_element_type=F32)


def tn(left, right):
    return lax.dot_general(left, right, (((0,), (0,)), ((), ())), preferred_element_type=F32)


def lane(shape):
    return lax.broadcasted_iota(jnp.int32, shape, 1)


def causal_floor(scores, key_begin, query_begin):
    key = lax.broadcasted_iota(jnp.int32, scores.shape, 0) + key_begin
    query = lax.broadcasted_iota(jnp.int32, scores.shape, 1) + query_begin
    return jnp.where(key <= query, scores, FLOOR_SCORE)


def head_queries(scaled, half, guarded):
    here = lane(scaled.shape)
    other = jnp.zeros_like(scaled)
    if guarded:
        other = jnp.where(here == (1 - half) * HDIM, jnp.ones_like(scaled), other)
    return jnp.where(here // HDIM == half, scaled, other)


def guarded_keys(keys, guard, half):
    here = lane(keys.shape)
    other = jnp.where(here == (1 - half) * HDIM, guard, jnp.zeros_like(keys))
    return jnp.where(here // HDIM == half, keys, other)


def key_chunks(begin, rows, keys, causal):
    if not causal:
        return [(0, keys, False)]
    chunks = [(0, begin, False)] if begin else []
    return chunks + [(begin, rows, True)]


def pair_forward(q, k, v, guard, mix, logs, pair, keys_ref, values_t, causal):
    rows = q[0].shape[0]
    keys = k[0].shape[0]

    def columns(operand):
        return pl.ds(pl.multiple_of(operand[1] + pair * PAIR, PAIR), PAIR)

    key_all = k[0][:, columns(k)]
    values_t[...] = v[0][:, columns(v)].T
    for half in range(2):
        keys_ref[half] = key_all if guard is None else guarded_keys(key_all, guard[...], half)
    block = min(QUERY_BLOCK if causal else rows, rows)
    for begin in range(0, rows, block):
        scaled = q[0][begin : begin + block, columns(q)] * jnp.asarray(HDIM**-0.5, BF)
        queries = [head_queries(scaled, half, guard is not None) for half in range(2)]
        chunks = key_chunks(begin, block, keys, causal)
        scores = [[], []]
        for first, count, diagonal in chunks:
            for half in range(2):
                score = nt(keys_ref[half, first : first + count, :], queries[half])
                scores[half].append(causal_floor(score, first, begin) if diagonal else score)
        tops = []
        for half in range(2):
            top = jnp.max(scores[half][0], axis=0, keepdims=True)
            for score in scores[half][1:]:
                top = jnp.maximum(top, jnp.max(score, axis=0, keepdims=True))
            tops.append(top)
        mixed = []
        for half in range(2):
            total = None
            out = None
            for (first, count, _), score in zip(chunks, scores[half]):
                expd = jnp.exp(score - tops[half])
                part = jnp.sum(expd, axis=0, keepdims=True)
                value = values_t[half * HDIM : (half + 1) * HDIM, first : first + count]
                term = nn(value, expd.astype(BF))
                total = part if total is None else total + part
                out = term if out is None else out + term
            mixed.append(out * (1.0 / total))
            logs[pair, half : half + 1, begin : begin + block] = tops[half] + jnp.log(total)
        mix[0][begin : begin + block, columns(mix)] = jnp.concatenate(mixed, axis=0).T.astype(BF)


def pair_backward(q, k, v, guard, mix, grad_mix, logs, pair, keys_ref, sums, grads, causal):
    rows = q[0].shape[0]
    keys = k[0].shape[0]
    grad_key, grad_value = sums

    def columns(operand):
        return pl.ds(pl.multiple_of(operand[1] + pair * PAIR, PAIR), PAIR)

    key_all = k[0][:, columns(k)]
    for half in range(2):
        keys_ref[half] = key_all if guard is None else guarded_keys(key_all, guard[...], half)
    keys_t = key_all.T
    block = min(QUERY_BLOCK, rows)
    for begin in range(0, rows, block):
        here = slice(begin, begin + block)
        scaled = q[0][here, columns(q)] * jnp.asarray(HDIM**-0.5, BF)
        grad = grad_mix[0][here, columns(grad_mix)]
        weighed = (grad.astype(F32) * mix[0][here, columns(mix)].astype(F32)).T
        parts = []
        for half in range(2):
            own = lane(scaled.shape) // HDIM == half
            centre = jnp.sum(weighed[half * HDIM : (half + 1) * HDIM, :], axis=0, keepdims=True)
            parts.append(
                (
                    head_queries(scaled, half, guard is not None),
                    jnp.where(own, scaled, jnp.zeros_like(scaled)),
                    jnp.where(own, grad, jnp.zeros_like(grad)),
                    centre,
                    logs[pair, half : half + 1, here],
                )
            )
        grad_query = [None, None]
        for first, count, diagonal in key_chunks(begin, block, keys, causal):
            there = slice(first, first + count)
            value = v[0][there, columns(v)]
            raw = []
            for half in range(2):
                score = nt(keys_ref[half, there, :], parts[half][0])
                if diagonal:
                    score = causal_floor(score, first, begin)
                raw.append((score, nt(value, parts[half][2])))
            low = []
            for half in range(2):
                prob = jnp.exp(raw[half][0] - parts[half][4])
                grad_score = (prob * (raw[half][1] - parts[half][3])).astype(BF)
                low.append((prob.astype(BF), grad_score))
            add_value = nn(low[0][0], parts[0][2]) + nn(low[1][0], parts[1][2])
            add_key = nn(low[0][1], parts[0][1]) + nn(low[1][1], parts[1][1])
            fresh = diagonal if causal else begin == 0
            if fresh:
                grad_value[there, :] = add_value
                grad_key[there, :] = add_key
            else:
                grad_value[there, :] += add_value
                grad_key[there, :] += add_key
            for half in range(2):
                term = nn(keys_t[half * HDIM : (half + 1) * HDIM, there], low[half][1])
                grad_query[half] = term if grad_query[half] is None else grad_query[half] + term
        both = jnp.concatenate(grad_query, axis=0).T * HDIM**-0.5
        grads[0][0][here, columns(grads[0])] = both.astype(BF)
    grads[1][0][:, columns(grads[1])] = grad_key[...].astype(BF)
    grads[2][0][:, columns(grads[2])] = grad_value[...].astype(BF)


def row_loop(rows, body, begin_row=0):
    step = min(ROWS, rows)

    def turn(index, carry):
        body(pl.ds(pl.multiple_of(begin_row + index * step, step), step))
        return carry

    lax.fori_loop(0, rows // step, turn, 0, unroll=2)


def standardised(values):
    centred = values - jnp.mean(values, axis=-1, keepdims=True)
    scale = lax.rsqrt(jnp.mean(centred * centred, axis=-1, keepdims=True) + NORM_EPSILON)
    return centred * scale, scale


def norm_gradient(grad, gain, unit, scale):
    weighted = grad * gain
    return scale * (
        weighted
        - jnp.mean(weighted, axis=-1, keepdims=True)
        - unit * jnp.mean(weighted * unit, axis=-1, keepdims=True)
    )


def fold_rows(values):
    return jnp.sum(values.reshape(values.shape[0] // 8, 8, values.shape[1]), axis=0)


def wide(scale):
    return jnp.broadcast_to(scale, (scale.shape[0], 128))


def store_blocks(blocks, slot, grad, first_split=0):
    groups, _, _, rows, cols = blocks.shape
    low = grad.astype(BF)
    for split in range(low.shape[1] // cols):
        for group in range(groups):
            blocks[group, first_split + split, slot] = low[
                group * rows : (group + 1) * rows, split * cols : (split + 1) * cols
            ]


class Moves:
    def __init__(self, semaphores):
        self.semaphores = semaphores
        self.count = 0
        self.open = []

    def start(self, source, target):
        copy = pltpu.make_async_copy(source, target, self.semaphores.at[self.count])
        self.count += 1
        copy.start()
        return copy

    def send(self, source, target):
        self.open.append(self.start(source, target))

    def finish(self):
        for copy in self.open:
            copy.wait()


def fetch_weights(blocks, weights, semaphore, first, slots):
    groups, splits, _, rows, cols = blocks.shape

    def turn(group, carry):
        for split in range(splits):
            pltpu.make_async_copy(
                blocks.at[group, split, pl.ds(first, slots)],
                weights.at[
                    :, pl.ds(pl.multiple_of(group * rows, rows), rows), pl.ds(split * cols, cols)
                ],
                semaphore,
            ).start()
        return carry

    lax.fori_loop(0, groups, turn, 0)
    return pltpu.make_async_copy(weights, weights, semaphore)


def self_forward(
    x_hbm, place_hbm, blocks_hbm,
    low_hbm, qkv_hbm, mix_hbm, logs_hbm, unit_hbm, scale_hbm,
    x, place, weights, low, qkv, mix, logs, unit, scale, keys_ref, values_t, semaphores, gather_sem,
):
    moves = Moves(semaphores)
    arrivals = [moves.start(x_hbm, x), moves.start(place_hbm, place)]
    gathered = fetch_weights(blocks_hbm, weights, gather_sem, 0, 4)
    for copy in arrivals:
        copy.wait()
    low[...] = nn(x[...], place[...]).astype(BF)
    moves.send(low, low_hbm)
    gathered.wait()
    width = low.shape[1]
    for part in range(3):
        qkv[:, part * width : (part + 1) * width] = nn(low[...], weights[part]).astype(BF)
    moves.send(qkv, qkv_hbm)

    def turn(pair, carry):
        pair_forward(
            (qkv, 0), (qkv, width), (qkv, 2 * width), None, (mix, 0), logs, pair, keys_ref, values_t, True
        )
        return carry

    lax.fori_loop(0, width // PAIR, turn, 0)
    moves.send(mix, mix_hbm)
    moves.send(logs, logs_hbm)
    unit[...] = nt(mix[...], weights[3])

    def normalise(rows):
        unit_rows, scale_rows = standardised(low[rows, :].astype(F32) + unit[rows, :])
        unit[rows, :] = unit_rows
        scale[rows, :] = wide(scale_rows)

    row_loop(low.shape[0], normalise)
    moves.send(unit, unit_hbm)
    moves.send(scale, scale_hbm)
    moves.finish()


def cross_forward(
    memory_hbm, place_hbm, guard_hbm, blocks_hbm, norms, unit_before_hbm,
    low_hbm, query_hbm, key_value_hbm, mix_hbm, logs_hbm, unit_hbm, scale_hbm,
    memory, place, guard, unit_before, weights, low, first_low, query, key_value, mix, logs, unit, scale,
    keys_ref, values_t, semaphores, gather_sem,
):
    moves = Moves(semaphores)
    arrivals = [moves.start(memory_hbm, memory), moves.start(place_hbm, place)]
    gathered = fetch_weights(blocks_hbm, weights, gather_sem, 4, 4)
    before = moves.start(unit_before_hbm, unit_before)
    masked = moves.start(guard_hbm, guard)
    for copy in arrivals:
        copy.wait()
    low[...] = nn(memory[...], place[...]).astype(BF)
    moves.send(low, low_hbm)
    before.wait()
    width = low.shape[1]

    def first_of(rows):
        return unit_before[rows, :] * norms[0:1, :] + norms[1:2, :]

    def lower(rows):
        first_low[rows, :] = first_of(rows).astype(BF)

    row_loop(unit.shape[0], lower)
    gathered.wait()
    query[...] = nn(first_low[...], weights[0]).astype(BF)
    moves.send(query, query_hbm)
    for part in range(2):
        key_value[:, part * width : (part + 1) * width] = nn(low[...], weights[1 + part]).astype(BF)
    moves.send(key_value, key_value_hbm)
    masked.wait()

    def turn(pair, carry):
        pair_forward(
            (query, 0), (key_value, 0), (key_value, width), guard, (mix, 0), logs, pair, keys_ref, values_t, False
        )
        return carry

    lax.fori_loop(0, width // PAIR, turn, 0)
    moves.send(mix, mix_hbm)
    moves.send(logs, logs_hbm)
    unit[...] = nt(mix[...], weights[3])

    def normalise(rows):
        unit_rows, scale_rows = standardised(first_of(rows) + unit[rows, :])
        unit[rows, :] = unit_rows
        scale[rows, :] = wide(scale_rows)

    row_loop(unit.shape[0], normalise)
    moves.send(unit, unit_hbm)
    moves.send(scale, scale_hbm)
    moves.finish()


def gelu_both(values):
    half = 0.5 * (1.0 + lax.erf(values * (0.5**0.5)))
    bell = jnp.exp(-0.5 * values * values) * (0.5 / math.pi) ** 0.5
    return values * half, half + values * bell


def feed_both(
    length_ref, low_hbm, cotangent_hbm, place_hbm, blocks_hbm, norms, unit_hbm, scale_hbm,
    output_hbm, grad_third_hbm, grad_second_hbm, grads_hbm, norm_grads,
    low, cotangent, place, weights, unit, scale, second_low, third_low, active, slope, inner_grad, output,
    grad_third, grad_second, grads, sums, semaphores, gather_sem,
):
    moves = Moves(semaphores)
    first = [moves.start(unit_hbm, unit)]
    gathered = fetch_weights(blocks_hbm, weights, gather_sem, 0, 2)
    others = [
        moves.start(low_hbm, low),
        moves.start(cotangent_hbm, cotangent),
        moves.start(place_hbm, place),
        moves.start(scale_hbm, scale),
    ]
    rows_all, width = low.shape
    hidden = weights.shape[2]
    chunk = min(width, hidden)
    sums[...] = jnp.zeros_like(sums)
    for copy in first:
        copy.wait()

    def second_of(rows):
        return unit[rows, :] * norms[2:3, :] + norms[3:4, :]

    def lower(rows):
        second_low[rows, :] = second_of(rows).astype(BF)

    row_loop(rows_all, lower)
    gathered.wait()
    for copy in others:
        copy.wait()
    length = length_ref[0]
    tile_rows = min(FEED_ROWS, rows_all)

    def tile(index, carry):
        begin = pl.multiple_of(index * tile_rows, tile_rows)
        here = pl.ds(begin, tile_rows)
        cot = nn(cotangent[here, :], place[...])
        for begin_col in range(0, hidden, chunk):
            cols = slice(begin_col, begin_col + chunk)
            value, slope_part = gelu_both(nn(second_low[here, :], weights[0, :, cols]))
            active[here, cols] = value.astype(BF)
            slope[:, cols] = slope_part
        fed = nt(active[here, :], weights[1])
        for part in range(0, tile_rows, ROWS):
            rows = pl.ds(pl.multiple_of(begin + part, ROWS), ROWS)
            place_rows = lax.broadcasted_iota(jnp.int32, (ROWS, 1), 0) + (begin + part)
            live = jnp.where(place_rows < length, 1.0, 0.0)
            third_sum = second_of(rows) + fed[part : part + ROWS, :] + low[rows, :].astype(F32)
            unit_rows, scale_rows = standardised(third_sum)
            third = live * (unit_rows * norms[4:5, :] + norms[5:6, :])
            output[rows, :] = third.astype(BF)
            grad = live * cot[part : part + ROWS, :]
            grad_rows = norm_gradient(grad, norms[4:5, :], unit_rows, scale_rows)
            grad_third[rows, :] = grad_rows
            third_low[rows, :] = grad_rows.astype(BF)
            sums[2] += fold_rows(grad * unit_rows)
            sums[3] += fold_rows(grad)
        output[here, :] = nt(output[here, :], place[...]).astype(BF)
        for begin_col in range(0, hidden, chunk):
            cols = slice(begin_col, begin_col + chunk)
            back = nn(third_low[here, :], weights[1, :, cols]) * slope[:, cols]
            inner_grad[here, cols] = back.astype(BF)
        fed_back = nt(inner_grad[here, :], weights[0])
        for part in range(0, tile_rows, ROWS):
            rows = pl.ds(pl.multiple_of(begin + part, ROWS), ROWS)
            unit_rows = unit[rows, :]
            grad = fed_back[part : part + ROWS, :] + grad_third[rows, :]
            grad_second[rows, :] = norm_gradient(
                grad, norms[2:3, :], unit_rows, scale[rows, 0:1]
            )
            sums[0] += fold_rows(grad * unit_rows)
            sums[1] += fold_rows(grad)
        return carry

    lax.fori_loop(0, rows_all // tile_rows, tile, 0)
    moves.send(output, output_hbm)
    moves.send(grad_third, grad_third_hbm)
    moves.send(grad_second, grad_second_hbm)
    norm_grads[...] = jnp.sum(sums[...], axis=1)
    cols_one = grads.shape[4]
    for split in range(hidden // cols_one):
        cols = slice(split * cols_one, (split + 1) * cols_one)
        store_blocks(grads, 0, tn(second_low[...], inner_grad[:, cols]), split)
        store_blocks(grads, 1, tn(third_low[...], active[:, cols]), split)
    moves.send(grads, grads_hbm)
    moves.finish()


def cross_backward(
    grad_second_hbm, mix_hbm, blocks_hbm, query_hbm, key_value_hbm, logs_hbm, guard_hbm, memory_low_hbm,
    unit_hbm, scale_hbm, place_hbm, norms,
    grad_memory_hbm, grad_first_hbm, grads_hbm, norm_grads,
    grad_second, mix, weights, query, key_value, logs, guard, memory_low, unit, scale, place,
    second_low, grad_mix, query_grad, key_value_grad, first_low, grad_memory, grad_first, grads, sums,
    keys_ref, key_sum, value_sum, semaphores, gather_sem,
):
    moves = Moves(semaphores)
    start = moves.start(grad_second_hbm, grad_second)
    gathered = fetch_weights(blocks_hbm, weights, gather_sem, 4, 4)
    stage = [
        moves.start(mix_hbm, mix),
        moves.start(query_hbm, query),
        moves.start(key_value_hbm, key_value),
        moves.start(logs_hbm, logs),
        moves.start(guard_hbm, guard),
    ]
    late = [
        moves.start(memory_low_hbm, memory_low),
        moves.start(unit_hbm, unit),
        moves.start(scale_hbm, scale),
        moves.start(place_hbm, place),
    ]
    rows_all, width = mix.shape
    start.wait()

    def lower(rows):
        second_low[rows, :] = grad_second[rows, :].astype(BF)

    row_loop(rows_all, lower)
    gathered.wait()
    for copy in stage:
        copy.wait()
    grad_mix[...] = nn(second_low[...], weights[3]).astype(BF)

    def turn(pair, carry):
        pair_backward(
            (query, 0), (key_value, 0), (key_value, width), guard, (mix, 0), (grad_mix, 0), logs, pair,
            keys_ref, (key_sum, value_sum), ((query_grad, 0), (key_value_grad, 0), (key_value_grad, width)), False,
        )
        return carry

    lax.fori_loop(0, width // PAIR, turn, 0)
    for copy in late:
        copy.wait()
    unit_low = nt(key_value_grad[:, :width], weights[1]) + nt(key_value_grad[:, width:], weights[2])
    grad_memory[...] = unit_low.astype(BF)
    grad_memory[...] = nt(grad_memory[...], place[...]).astype(BF)
    moves.send(grad_memory, grad_memory_hbm)
    grad_first[...] = nt(query_grad[...], weights[0])
    sums[...] = jnp.zeros_like(sums)

    def back(rows):
        unit_rows = unit[rows, :]
        grad = grad_first[rows, :] + grad_second[rows, :]
        first_low[rows, :] = (unit_rows * norms[0:1, :] + norms[1:2, :]).astype(BF)
        grad_first[rows, :] = norm_gradient(grad, norms[0:1, :], unit_rows, scale[rows, 0:1])
        sums[0] += fold_rows(grad * unit_rows)
        sums[1] += fold_rows(grad)

    row_loop(rows_all, back)
    moves.send(grad_first, grad_first_hbm)
    norm_grads[...] = jnp.sum(sums[...], axis=1)
    store_blocks(grads, 0, tn(first_low[...], query_grad[...]))
    store_blocks(grads, 1, tn(memory_low[...], key_value_grad[:, :width]))
    store_blocks(grads, 2, tn(memory_low[...], key_value_grad[:, width:]))
    store_blocks(grads, 3, tn(second_low[...], mix[...]))
    moves.send(grads, grads_hbm)
    moves.finish()


def self_backward(
    grad_first_hbm, mix_hbm, blocks_hbm, qkv_hbm, logs_hbm, low_hbm, grad_third_hbm, place_hbm,
    grad_input_hbm, grads_hbm,
    grad_first, mix, weights, qkv, logs, low, grad_third, place,
    first_low, grad_mix, qkv_grad, grad_input, grads, keys_ref, key_sum, value_sum, semaphores, gather_sem,
):
    moves = Moves(semaphores)
    start = moves.start(grad_first_hbm, grad_first)
    gathered = fetch_weights(blocks_hbm, weights, gather_sem, 0, 4)
    stage = [moves.start(mix_hbm, mix), moves.start(qkv_hbm, qkv), moves.start(logs_hbm, logs)]
    late = [
        moves.start(low_hbm, low),
        moves.start(grad_third_hbm, grad_third),
        moves.start(place_hbm, place),
    ]
    rows_all, width = mix.shape
    start.wait()

    def lower(rows):
        first_low[rows, :] = grad_first[rows, :].astype(BF)

    row_loop(rows_all, lower)
    gathered.wait()
    for copy in stage:
        copy.wait()
    grad_mix[...] = nn(first_low[...], weights[3]).astype(BF)

    def turn(pair, carry):
        pair_backward(
            (qkv, 0), (qkv, width), (qkv, 2 * width), None, (mix, 0), (grad_mix, 0), logs, pair,
            keys_ref, (key_sum, value_sum), ((qkv_grad, 0), (qkv_grad, width), (qkv_grad, 2 * width)), True,
        )
        return carry

    lax.fori_loop(0, width // PAIR, turn, 0)
    for copy in late:
        copy.wait()
    store_blocks(grads, 3, tn(first_low[...], mix[...]))
    for part in range(3):
        store_blocks(grads, part, tn(low[...], qkv_grad[:, part * width : (part + 1) * width]))
    moves.send(grads, grads_hbm)
    total = grad_first[...] + grad_third[...]
    for part in range(3):
        total = total + nt(qkv_grad[:, part * width : (part + 1) * width], weights[part])
    grad_input[...] = total.astype(BF)
    grad_input[...] = nt(grad_input[...], place[...]).astype(BF)
    moves.send(grad_input, grad_input_hbm)
    moves.finish()


ANY = pl.BlockSpec(memory_space=pl.ANY)
WHOLE = pl.BlockSpec(memory_space=pltpu.VMEM)
SCALAR = pl.BlockSpec(memory_space=pltpu.SMEM)


def shape_of(array):
    return jax.ShapeDtypeStruct(array[0], array[1])


def run_kernel(body, name, operands, specs, outs, out_specs, scratch, copies, limit, flops):
    moved = sum(math.prod(s) * jnp.dtype(d).itemsize for s, d in outs)
    moved += sum(math.prod(o.shape) * o.dtype.itemsize for o in operands)
    return pl.pallas_call(
        body,
        name=name,
        in_specs=specs,
        out_specs=out_specs,
        out_shape=[shape_of(o) for o in outs],
        scratch_shapes=[pltpu.VMEM(s, d) for s, d in scratch]
        + [pltpu.SemaphoreType.DMA((copies,)), pltpu.SemaphoreType.DMA],
        compiler_params=pltpu.CompilerParams(vmem_limit_bytes=limit),
        cost_estimate=pl.CostEstimate(flops=flops, bytes_accessed=moved, transcendentals=0),
    )(*operands)


MESH_ID = pl.DeviceIdType.MESH


class Axis:
    def __init__(self, mesh_axis, stride, size):
        self.mesh_axis, self.stride, self.size = mesh_axis, stride, size

    def own(self):
        return lax.rem(lax.axis_index(self.mesh_axis) // self.stride, self.size)

    def peer(self, offset):
        own = self.own()
        there = lax.rem(own + offset, self.size)
        return there, {
            self.mesh_axis: lax.axis_index(self.mesh_axis) + (there - own) * self.stride
        }


def physical_axes(groups, splits):
    if (groups, splits) == (8, 4):
        axes = {
            "z": Axis("dp", 2, 4),
            "x": Axis("dp", 1, 2),
            "y": Axis("tensor", 2, 2),
            "core": Axis("tensor", 1, 2),
        }
    elif (groups, splits) == (32, 4):
        axes = {
            "z": Axis("dp", 8, 4),
            "x": Axis("dp", 2, 4),
            "core": Axis("dp", 1, 2),
            "y": Axis("tensor", 1, 4),
        }
    else:
        raise ValueError("unknown mesh")
    return axes, (("z", "x", "y", "core"), ("z", "y", "x", "core"))


def greet(axes):
    barrier = pltpu.get_barrier_semaphore()
    count = 0
    for axis in axes.values():
        for offset in range(1, axis.size):
            pl.semaphore_signal(barrier, inc=1, device_id=axis.peer(offset)[1], device_id_type=MESH_ID)
            count += 1
    pl.semaphore_wait(barrier, count)


class Links:
    def __init__(self, send_sems, recv_sems):
        self.send_sems, self.recv_sems = send_sems, recv_sems
        self.count = 0

    def start(self, source, target, device):
        copy = pltpu.make_async_remote_copy(
            src_ref=source,
            dst_ref=target,
            send_sem=self.send_sems.at[self.count],
            recv_sem=self.recv_sems.at[self.count],
            device_id=device,
            device_id_type=MESH_ID,
        )
        self.count += 1
        copy.start()
        return copy


def gather_steps(axes, orders, shards, outs, chunks, links, moves):
    names = list(axes)

    def region(order, done, chunk):
        index = [
            slice(None) if name in order[:done] else axes[name].own() for name in names
        ]
        return outs[chunk[0]].at[(*index, *chunk[1])]

    sent = [[[] for _ in range(4)] for _ in chunks]
    placed = [moves.start(shard, outs[i].at[tuple(axes[n].own() for n in names)]) for i, shard in enumerate(shards)]

    def send(number, phase):
        order = orders[number % 2]
        axis = axes[order[phase]]
        part = region(order, phase, chunks[number])
        source = shards[chunks[number][0]].at[chunks[number][1]] if phase == 0 else part
        for offset in range(1, axis.size):
            sent[number][phase].append(links.start(source, part, axis.peer(offset)[1]))

    def step(turn):
        if turn == 0:
            for number in range(len(chunks)):
                send(number, 0)
            for copy in placed:
                copy.wait()
        for phase in (1, 2, 3, 4):
            number = turn - (phase - 1)
            if 0 <= number < len(chunks):
                for copy in sent[number][phase - 1]:
                    copy.wait_recv()
                if phase < 4:
                    send(number, phase)
        if turn == len(chunks) + 2:
            for of_chunk in sent:
                for of_phase in of_chunk:
                    for copy in of_phase:
                        copy.wait_send()

    return [functools.partial(step, turn) for turn in range(len(chunks) + 3)]


def gather_count(axes, chunks):
    return chunks * sum(axis.size - 1 for axis in axes.values())


def reduce_steps(axes, orders, sources, sums, arrivals, outs, chunks, links, moves):
    names = list(axes)
    sent = [[[] for _ in range(4)] for _ in chunks]
    loads = {}

    def order_of(number):
        return orders[number % 2][::-1]

    def part(ref, order, phase, coordinate, chunk, without=()):
        index = []
        for name in names:
            if name in without or name in order[:0]:
                continue
            if name == order[phase]:
                index.append(coordinate)
            elif name in order[:phase]:
                index.append(axes[name].own())
            else:
                index.append(slice(None))
        return ref.at[(*index, *chunk[1])]

    def send(number, phase):
        order = order_of(number)
        axis = axes[order[phase]]
        which = chunks[number][0]
        for offset in range(1, axis.size):
            there, device = axis.peer(offset)
            if phase == 0:
                source = part(sources[which], order, 0, there, chunks[number])
            else:
                source = part(sums[which], order, phase, there, chunks[number], order[:1])
            target = arrivals[phase][number].at[offset - 1]
            sent[number][phase].append(links.start(source, target, device))

    def load(number):
        order = order_of(number)
        which = chunks[number][0]
        source = part(sources[which], order, 0, axes[order[0]].own(), chunks[number])
        loads[number] = moves.start(source, sums[which].at[(*[slice(None)] * (len(names) - 1), *chunks[number][1])])

    def add(number, phase):
        order = order_of(number)
        which = chunks[number][0]
        own = axes[order[phase]].own()
        if phase == 0:
            target = sums[which].at[(*[slice(None)] * (len(names) - 1), *chunks[number][1])]
        else:
            target = part(sums[which], order, phase, own, chunks[number], order[:1])
        came = arrivals[phase][number]
        lead = len(target.shape) - len(chunk_shape(sources[which], len(names), chunks[number]))
        count = math.prod(target.shape[:lead])

        def one(position, carry):
            index = []
            rest = position
            for size in reversed(target.shape[:lead]):
                index.append(lax.rem(rest, size))
                rest = rest // size
            index = tuple(reversed(index))
            total = target[index].astype(F32)
            for peer in range(came.shape[0]):
                total = total + came[(peer, *index)].astype(F32)
            if phase == 3:
                outs[which][chunks[number][1]] = total
            else:
                target[index] = total.astype(target.dtype)
            return carry

        if count == 1:
            one(0, 0)
        else:
            lax.fori_loop(0, count, one, 0)

    def step(turn):
        if turn == 0:
            for number in range(len(chunks)):
                send(number, 0)
            for number in range(len(chunks)):
                load(number)
        for phase in (0, 1, 2, 3):
            number = turn - phase
            if 0 <= number < len(chunks):
                for copy in sent[number][phase]:
                    copy.wait_recv()
                if phase == 0:
                    loads[number].wait()
                add(number, phase)
                if phase < 3:
                    send(number, phase + 1)
        if turn == len(chunks) + 2:
            for of_chunk in sent:
                for of_phase in of_chunk:
                    for copy in of_phase:
                        copy.wait_send()

    return [functools.partial(step, turn) for turn in range(len(chunks) + 3)]


def chunk_shape(source, lead, chunk):
    shape = []
    for position, size in enumerate(source.shape[lead:]):
        if position < len(chunk[1]):
            item = chunk[1][position]
            if isinstance(item, slice):
                first, last, _ = item.indices(size)
                shape.append(last - first)
        else:
            shape.append(size)
    return tuple(shape)


def arrival_shapes(axes, orders, blocks, chunks):
    shapes = []
    for phase in range(4):
        of_phase = []
        for number, chunk in enumerate(chunks):
            order = orders[number % 2][::-1]
            region = [
                axis.size for name, axis in axes.items() if name not in order[: phase + 1]
            ]
            block = blocks[chunk[0]]
            of_phase.append(
                (
                    (axes[order[phase]].size - 1, *region, *chunk_shape(block, len(axes), chunk)),
                    block.dtype,
                )
            )
        shapes.append(of_phase)
    return shapes


def pieces(blocks, array, slots):
    if slots == 2:
        cols = blocks[-1] // 2
        return [
            (array, (slot, slice(None), slice(part * cols, (part + 1) * cols)))
            for slot in range(2)
            for part in range(2)
        ]
    return [(array, (slice(first, first + 2),)) for first in range(0, slots, 2)]


def gather_parameters(shards, groups, splits):
    axes, orders = physical_axes(groups, splits)
    dims = tuple(axis.size for axis in axes.values())
    attention = pieces(shards[0].shape, 0, shards[0].shape[0])
    chunks = attention[:2] + [(2, ())] + attention[2:] + pieces(shards[1].shape, 1, 2)
    count = gather_count(axes, len(chunks))

    def body(*refs):
        ins, outs, (local, send, recv) = refs[:3], refs[3:6], refs[6:]
        greet(axes)
        for step in gather_steps(axes, orders, ins, outs, chunks, Links(send, recv), Moves(local)):
            step()

    blocks = pl.pallas_call(
        body,
        name="gather_parameters",
        in_specs=[ANY] * 3,
        out_specs=[ANY] * 3,
        out_shape=[jax.ShapeDtypeStruct((*dims, *s.shape), s.dtype) for s in shards],
        scratch_shapes=[
            pltpu.SemaphoreType.DMA((3,)),
            pltpu.SemaphoreType.DMA((count,)),
            pltpu.SemaphoreType.DMA((count,)),
        ],
        compiler_params=pltpu.CompilerParams(collective_id=0, has_side_effects=True),
    )(*shards)
    return [b.reshape(groups, splits, *s.shape) for b, s in zip(blocks, shards)]


def reduce_gradients(blocks):
    groups, splits = blocks[0].shape[:2]
    axes, orders = physical_axes(groups, splits)
    dims = tuple(axis.size for axis in axes.values())
    shards = [b.shape[2:] for b in blocks]
    blocks = [b.reshape(*dims, *s) for b, s in zip(blocks, shards)]
    chunks = [(3, ())] + pieces(shards[2], 2, 2) + pieces(shards[1], 1, 4) + pieces(shards[0], 0, 4)
    shapes = arrival_shapes(axes, orders, blocks, chunks)
    flat = [shape for of_phase in shapes for shape in of_phase]
    first = orders[0][-1]
    kept = tuple(axis.size for name, axis in axes.items() if name != first)
    count = gather_count(axes, len(chunks))
    number = len(chunks)

    def body(*refs):
        ins, outs, sums, rest = refs[:4], refs[4:8], refs[8:12], refs[12:]
        arrived, (local, send, recv) = rest[: len(flat)], rest[len(flat) :]
        arrivals = [arrived[phase * number : (phase + 1) * number] for phase in range(4)]
        greet(axes)
        links = Links(send, recv)
        for step in reduce_steps(
            axes, orders, ins, sums, arrivals, outs, chunks, links, Moves(local)
        ):
            step()

    return pl.pallas_call(
        body,
        name="reduce_gradients",
        in_specs=[ANY] * 4,
        out_specs=[WHOLE] * 4,
        out_shape=[jax.ShapeDtypeStruct(s, F32) for s in shards],
        scratch_shapes=[pltpu.VMEM((*kept, *s), b.dtype) for b, s in zip(blocks, shards)]
        + [pltpu.VMEM(*shape) for shape in flat]
        + [
            pltpu.SemaphoreType.DMA((number,)),
            pltpu.SemaphoreType.DMA((count,)),
            pltpu.SemaphoreType.DMA((count,)),
        ],
        compiler_params=pltpu.CompilerParams(
            collective_id=1, has_side_effects=True, vmem_limit_bytes=40 << 20
        ),
    )(*blocks)


def run_layer(x, memory, cotangent, length, guard, place, attention, feed, norms):
    rows, width = x.shape
    keys = memory.shape[0]
    groups, splits, _, own_rows, own_cols = attention.shape
    hidden = splits * feed.shape[4]
    pairs = width // PAIR
    wide_low, wide_full = ((rows, width), BF), ((rows, width), F32)
    memory_low_t = ((keys, width), BF)
    scale_t = ((rows, 128), F32)
    logs_t = ((pairs, 2, rows), F32)
    place_t = ((width, width), BF)
    four = ((4, width, width), BF)
    qkv_t = ((rows, 3 * width), BF)
    key_value_t = ((keys, 2 * width), BF)
    guard_t = ((keys, PAIR), BF)
    keys_t = ((2, keys, PAIR), BF)
    values_t = ((PAIR, keys), BF)
    key_sum_t = ((keys, PAIR), F32)
    blocks_t = ((groups, splits, 4, own_rows, own_cols), BF)
    feed_blocks_t = ((groups, splits, 2, own_rows, feed.shape[4]), BF)
    pair_flops = 2 * rows * keys * width
    dense = 2 * rows * width * width

    low, qkv, self_mix, self_logs, unit_one, scale_one = run_kernel(
        self_forward, "self_forward",
        (x, place, attention), [ANY] * 3,
        [wide_low, qkv_t, wide_low, logs_t, wide_full, scale_t], [ANY] * 6,
        [wide_low, place_t, four, wide_low, qkv_t, wide_low, logs_t, wide_full, scale_t, keys_t, values_t],
        16, 48 << 20, 5 * dense + 6 * pair_flops,
    )
    memory_low, query, key_value, cross_mix, cross_logs, unit_two, scale_two = run_kernel(
        cross_forward, "cross_forward",
        (memory, place, guard, attention, norms, unit_one), [ANY] * 4 + [WHOLE, ANY],
        [memory_low_t, wide_low, key_value_t, wide_low, logs_t, wide_full, scale_t], [ANY] * 7,
        [memory_low_t, place_t, guard_t, wide_full, four, memory_low_t, wide_low, wide_low, key_value_t,
         wide_low, logs_t, wide_full, scale_t, keys_t, values_t],
        16, 56 << 20, 5 * dense + 8 * pair_flops,
    )
    output, grad_third, grad_second, feed_grads, feed_norms = run_kernel(
        feed_both, "feed_both",
        (length, low, cotangent, place, feed, norms, unit_two, scale_two),
        [SCALAR] + [ANY] * 4 + [WHOLE] + [ANY] * 2,
        [wide_low, wide_full, wide_full, feed_blocks_t, ((4, width), F32)], [ANY] * 4 + [WHOLE],
        [wide_low, wide_low, place_t, ((2, width, hidden), BF), wide_full, scale_t, wide_low, wide_low,
         ((rows, hidden), BF), ((min(FEED_ROWS, rows), hidden), F32), ((rows, hidden), BF), wide_low,
         wide_full, wide_full, feed_blocks_t, ((4, 8, width), F32)],
        16, 56 << 20, 2 * dense + 12 * rows * width * hidden,
    )
    grad_memory, grad_first, cross_grads, cross_norms = run_kernel(
        cross_backward, "cross_backward",
        (grad_second, cross_mix, attention, query, key_value, cross_logs, guard, memory_low, unit_one,
         scale_one, place, norms),
        [ANY] * 11 + [WHOLE],
        [memory_low_t, wide_full, blocks_t, ((2, width), F32)], [ANY] * 3 + [WHOLE],
        [wide_full, wide_low, four, wide_low, key_value_t, logs_t, guard_t, memory_low_t, wide_full, scale_t,
         place_t, wide_low, wide_low, wide_low, key_value_t, wide_low, memory_low_t, wide_full, blocks_t,
         ((2, 8, width), F32), keys_t, key_sum_t, key_sum_t],
        24, 58 << 20, 9 * dense + 20 * pair_flops,
    )
    grad_input, self_grads = run_kernel(
        self_backward, "self_backward",
        (grad_first, self_mix, attention, qkv, self_logs, low, grad_third, place), [ANY] * 8,
        [wide_low, blocks_t], [ANY] * 2,
        [wide_full, wide_low, four, qkv_t, logs_t, wide_low, wide_full, place_t, wide_low, wide_low, qkv_t,
         wide_low, blocks_t, keys_t, key_sum_t, key_sum_t],
        16, 56 << 20, 9 * dense + 15 * pair_flops,
    )
    norm_grads = jnp.concatenate([cross_norms, feed_norms], axis=0)
    return output, grad_input, grad_memory, self_grads, cross_grads, feed_grads, norm_grads


def adam_moments(rotated, moment, second):
    moment_new = BETA_FIRST * moment + (1.0 - BETA_FIRST) * rotated
    second_new = BETA_SECOND * second + (1.0 - BETA_SECOND) * rotated * rotated
    direction = (
        moment_new
        / (1.0 - BETA_FIRST**STEP)
        / (jnp.sqrt(second_new / (1.0 - BETA_SECOND**STEP)) + ADAM_EPSILON)
    )
    return (moment_new, second_new, direction)


def finish(weight, average, update, rate, decay):
    weight_new = weight - rate * (update + decay * weight)
    average_new = AVERAGE_DECAY * average + (1.0 - AVERAGE_DECAY) * weight_new
    return (weight_new, average_new, weight_new.astype(jnp.bfloat16))


def soap_step(weight, grad, moment, second, average, basis, rate, decay):
    rotated = jnp.einsum("src,sce->sre", grad, basis, precision=HIGHEST)
    moment_new, second_new, direction = adam_moments(rotated, moment, second)
    update = jnp.einsum("sre,sce->src", direction, basis, precision=HIGHEST)
    return (moment_new, second_new) + finish(weight, average, update, rate, decay)


def on_device(
    inputs,
    memory,
    cotangent,
    lengths,
    key_mask,
    owner_list,
    attention_master,
    attention_moment,
    attention_second,
    attention_average,
    attention_basis,
    feed_master,
    feed_moment,
    feed_second,
    feed_average,
    feed_basis,
    norm_master,
    norm_moment,
    norm_second,
    norm_average,
):
    groups = lax.axis_size("dp")
    splits = lax.axis_size("tensor")
    column = lax.axis_index("tensor")
    width = inputs.shape[1]
    share = inputs.shape[0] // splits
    seqs = lengths.shape[0] // splits

    def own(array, count):
        return lax.dynamic_slice_in_dim(array, column * count, count, 0)

    place = place_matrix(owner_list, width)

    slots, own_rows = norm_master.shape
    norm_low = jnp.pad(norm_master.astype(BF), ((0, 16 - slots), (0, 128 - own_rows)))
    attention, feed, norm_blocks = gather_parameters(
        (attention_master.astype(BF), feed_master.astype(BF), norm_low), groups, splits
    )
    norms = norm_blocks[:, 0, :8, :own_rows].transpose(1, 0, 2).reshape(8, width).astype(F32)
    piece = own_rows // splits
    key_rows = memory.shape[0] // splits
    valid = (own(key_mask, seqs) == 1) | (jnp.arange(key_rows) == 0)[None, :]
    guard = jnp.where(valid, 0.0, FLOOR_SCORE).astype(BF)
    guard = jnp.broadcast_to(guard.reshape(key_rows, 1), (key_rows, PAIR))

    output, grad_input, grad_memory, self_grads, cross_grads, feed_grads, norm_grads = run_layer(
        own(inputs, share),
        own(memory, key_rows),
        own(cotangent, share),
        own(lengths, seqs),
        guard,
        place,
        attention,
        feed,
        norms,
    )

    norm_parts = norm_grads.reshape(slots, groups, splits, piece).transpose(1, 2, 0, 3)
    norm_parts = jnp.pad(norm_parts, ((0, 0), (0, 0), (0, 8 - slots), (0, 128 - piece)))
    self_owned, cross_owned, feed_owned, norm_owned = reduce_gradients(
        (self_grads, cross_grads, feed_grads, norm_parts)
    )
    attention_owned = jnp.concatenate([self_owned, cross_owned], axis=0)
    norm_owned = norm_owned[:slots, :piece]
    attention_new = soap_step(
        attention_master,
        attention_owned,
        attention_moment,
        attention_second,
        attention_average,
        attention_basis,
        RATE_ATTENTION,
        WEIGHT_DECAY,
    )
    feed_new = soap_step(
        feed_master,
        feed_owned,
        feed_moment,
        feed_second,
        feed_average,
        feed_basis,
        RATE_FEED,
        WEIGHT_DECAY,
    )
    begin_col = column * piece

    def own_columns(array):
        return lax.dynamic_slice_in_dim(array, begin_col, piece, 1)

    moment_new, second_new, direction = adam_moments(
        norm_owned, own_columns(norm_moment), own_columns(norm_second)
    )
    norm_new = (moment_new, second_new) + finish(
        own_columns(norm_master), own_columns(norm_average), direction, RATE_NORMS, 0.0
    )
    return (output, grad_input, grad_memory) + attention_new + feed_new + norm_new


def solution(mesh):
    in_specs = (
        P("dp", None),
        P("dp", None),
        P("dp", None),
        P("dp"),
        P("dp", None),
        P(),
        P(None, "dp", "tensor"),
        P(None, "dp", "tensor"),
        P(None, "dp", "tensor"),
        P(None, "dp", "tensor"),
        P(None, "tensor", None),
        P(None, "dp", "tensor"),
        P(None, "dp", "tensor"),
        P(None, "dp", "tensor"),
        P(None, "dp", "tensor"),
        P(None, "tensor", None),
        P(None, "dp"),
        P(None, "dp"),
        P(None, "dp"),
        P(None, "dp"),
    )
    out_specs = (
        P(("dp", "tensor"), None),
        P(("dp", "tensor"), None),
        P(("dp", "tensor"), None),
        P(None, "dp", "tensor"),
        P(None, "dp", "tensor"),
        P(None, "dp", "tensor"),
        P(None, "dp", "tensor"),
        P(None, "dp", "tensor"),
        P(None, "dp", "tensor"),
        P(None, "dp", "tensor"),
        P(None, "dp", "tensor"),
        P(None, "dp", "tensor"),
        P(None, "dp", "tensor"),
        P(None, ("dp", "tensor")),
        P(None, ("dp", "tensor")),
        P(None, ("dp", "tensor")),
        P(None, ("dp", "tensor")),
        P(None, ("dp", "tensor")),
    )
    return jax.shard_map(
        on_device, mesh=mesh, in_specs=in_specs, out_specs=out_specs, check_vma=False
    )
```

```python
import functools
import math

import jax
import jax.numpy as jnp
from jax import lax
from jax.experimental import pallas as pl
from jax.experimental.pallas import tpu as pltpu
from jax.sharding import PartitionSpec as P

HDIM = 64
STEP = 10


FLOOR_SCORE = -1e30
NORM_EPSILON = 1e-05
BETA_FIRST = 0.9
BETA_SECOND = 0.95
ADAM_EPSILON = 1e-08
AVERAGE_DECAY = 0.6
RATE_ATTENTION = 0.07
RATE_FEED = 0.03
RATE_NORMS = 0.5
WEIGHT_DECAY = 0.01
HIGHEST = lax.Precision.HIGHEST


BF = jnp.bfloat16
F32 = jnp.float32
PAIR = 2 * HDIM
QUERY_BLOCK = 512
ROWS = 64
FEED_ROWS = 256


def nn(left, right):
    return lax.dot_general(left, right, (((1,), (0,)), ((), ())), preferred_element_type=F32)


def nt(left, right):
    return lax.dot_general(left, right, (((1,), (1,)), ((), ())), preferred_element_type=F32)


def tn(left, right):
    return lax.dot_general(left, right, (((0,), (0,)), ((), ())), preferred_element_type=F32)


def lane(shape):
    return lax.broadcasted_iota(jnp.int32, shape, 1)


def causal_floor(scores, key_begin, query_begin):
    key = lax.broadcasted_iota(jnp.int32, scores.shape, 0) + key_begin
    query = lax.broadcasted_iota(jnp.int32, scores.shape, 1) + query_begin
    return jnp.where(key <= query, scores, FLOOR_SCORE)


def head_queries(scaled, half, guarded):
    here = lane(scaled.shape)
    other = jnp.zeros_like(scaled)
    if guarded:
        other = jnp.where(here == (1 - half) * HDIM, jnp.ones_like(scaled), other)
    return jnp.where(here // HDIM == half, scaled, other)


def guarded_keys(keys, guard, half):
    here = lane(keys.shape)
    other = jnp.where(here == (1 - half) * HDIM, guard, jnp.zeros_like(keys))
    return jnp.where(here // HDIM == half, keys, other)


def key_chunks(begin, rows, keys, causal):
    if not causal:
        return [(0, keys, False)]
    chunks = [(0, begin, False)] if begin else []
    return chunks + [(begin, rows, True)]


def pair_forward(q, k, v, guard, mix, logs, pair, keys_ref, values_t, causal):
    rows = q[0].shape[0]
    keys = k[0].shape[0]

    def columns(operand):
        return pl.ds(pl.multiple_of(operand[1] + pair * PAIR, PAIR), PAIR)

    key_all = k[0][:, columns(k)]
    values_t[...] = v[0][:, columns(v)].T
    for half in range(2):
        keys_ref[half] = key_all if guard is None else guarded_keys(key_all, guard[...], half)
    block = min(QUERY_BLOCK if causal else rows, rows)
    for begin in range(0, rows, block):
        scaled = q[0][begin : begin + block, columns(q)] * jnp.asarray(HDIM**-0.5, BF)
        queries = [head_queries(scaled, half, guard is not None) for half in range(2)]
        chunks = key_chunks(begin, block, keys, causal)
        scores = [[], []]
        for first, count, diagonal in chunks:
            for half in range(2):
                score = nt(keys_ref[half, first : first + count, :], queries[half])
                scores[half].append(causal_floor(score, first, begin) if diagonal else score)
        tops = []
        for half in range(2):
            top = jnp.max(scores[half][0], axis=0, keepdims=True)
            for score in scores[half][1:]:
                top = jnp.maximum(top, jnp.max(score, axis=0, keepdims=True))
            tops.append(top)
        mixed = []
        for half in range(2):
            total = None
            out = None
            for (first, count, _), score in zip(chunks, scores[half]):
                expd = jnp.exp(score - tops[half])
                part = jnp.sum(expd, axis=0, keepdims=True)
                value = values_t[half * HDIM : (half + 1) * HDIM, first : first + count]
                term = nn(value, expd.astype(BF))
                total = part if total is None else total + part
                out = term if out is None else out + term
            mixed.append(out * (1.0 / total))
            logs[pair, half : half + 1, begin : begin + block] = tops[half] + jnp.log(total)
        mix[0][begin : begin + block, columns(mix)] = jnp.concatenate(mixed, axis=0).T.astype(BF)


def pair_backward(q, k, v, guard, mix, grad_mix, logs, pair, keys_ref, sums, grads, causal):
    rows = q[0].shape[0]
    keys = k[0].shape[0]
    grad_key, grad_value = sums

    def columns(operand):
        return pl.ds(pl.multiple_of(operand[1] + pair * PAIR, PAIR), PAIR)

    key_all = k[0][:, columns(k)]
    for half in range(2):
        keys_ref[half] = key_all if guard is None else guarded_keys(key_all, guard[...], half)
    keys_t = key_all.T
    block = min(QUERY_BLOCK, rows)
    for begin in range(0, rows, block):
        here = slice(begin, begin + block)
        scaled = q[0][here, columns(q)] * jnp.asarray(HDIM**-0.5, BF)
        grad = grad_mix[0][here, columns(grad_mix)]
        weighed = (grad.astype(F32) * mix[0][here, columns(mix)].astype(F32)).T
        parts = []
        for half in range(2):
            own = lane(scaled.shape) // HDIM == half
            centre = jnp.sum(weighed[half * HDIM : (half + 1) * HDIM, :], axis=0, keepdims=True)
            parts.append(
                (
                    head_queries(scaled, half, guard is not None),
                    jnp.where(own, scaled, jnp.zeros_like(scaled)),
                    jnp.where(own, grad, jnp.zeros_like(grad)),
                    centre,
                    logs[pair, half : half + 1, here],
                )
            )
        grad_query = [None, None]
        for first, count, diagonal in key_chunks(begin, block, keys, causal):
            there = slice(first, first + count)
            value = v[0][there, columns(v)]
            raw = []
            for half in range(2):
                score = nt(keys_ref[half, there, :], parts[half][0])
                if diagonal:
                    score = causal_floor(score, first, begin)
                raw.append((score, nt(value, parts[half][2])))
            low = []
            for half in range(2):
                prob = jnp.exp(raw[half][0] - parts[half][4])
                grad_score = (prob * (raw[half][1] - parts[half][3])).astype(BF)
                low.append((prob.astype(BF), grad_score))
            add_value = nn(low[0][0], parts[0][2]) + nn(low[1][0], parts[1][2])
            add_key = nn(low[0][1], parts[0][1]) + nn(low[1][1], parts[1][1])
            fresh = diagonal if causal else begin == 0
            if fresh:
                grad_value[there, :] = add_value
                grad_key[there, :] = add_key
            else:
                grad_value[there, :] += add_value
                grad_key[there, :] += add_key
            for half in range(2):
                term = nn(keys_t[half * HDIM : (half + 1) * HDIM, there], low[half][1])
                grad_query[half] = term if grad_query[half] is None else grad_query[half] + term
        both = jnp.concatenate(grad_query, axis=0).T * HDIM**-0.5
        grads[0][0][here, columns(grads[0])] = both.astype(BF)
    grads[1][0][:, columns(grads[1])] = grad_key[...].astype(BF)
    grads[2][0][:, columns(grads[2])] = grad_value[...].astype(BF)


def row_loop(rows, body, begin_row=0):
    step = min(ROWS, rows)

    def turn(index, carry):
        body(pl.ds(pl.multiple_of(begin_row + index * step, step), step))
        return carry

    lax.fori_loop(0, rows // step, turn, 0, unroll=2)


def standardised(values):
    centred = values - jnp.mean(values, axis=-1, keepdims=True)
    scale = lax.rsqrt(jnp.mean(centred * centred, axis=-1, keepdims=True) + NORM_EPSILON)
    return centred * scale, scale


def norm_gradient(grad, gain, unit, scale):
    weighted = grad * gain
    return scale * (
        weighted
        - jnp.mean(weighted, axis=-1, keepdims=True)
        - unit * jnp.mean(weighted * unit, axis=-1, keepdims=True)
    )


def fold_rows(values):
    return jnp.sum(values.reshape(values.shape[0] // 8, 8, values.shape[1]), axis=0)


def wide(scale):
    return jnp.broadcast_to(scale, (scale.shape[0], 128))


class Moves:
    def __init__(self, semaphores):
        self.semaphores = semaphores
        self.count = 0
        self.open = []

    def start(self, source, target):
        copy = pltpu.make_async_copy(source, target, self.semaphores.at[self.count])
        self.count += 1
        copy.start()
        return copy

    def send(self, source, target):
        self.open.append(self.start(source, target))

    def finish(self):
        for copy in self.open:
            copy.wait()


MESH_ID = pl.DeviceIdType.MESH


class Axis:
    def __init__(self, mesh_axis, stride, size):
        self.mesh_axis, self.stride, self.size = mesh_axis, stride, size

    def own(self):
        return lax.rem(lax.axis_index(self.mesh_axis) // self.stride, self.size)

    def peer(self, offset):
        own = self.own()
        there = lax.rem(own + offset, self.size)
        return there, {
            self.mesh_axis: lax.axis_index(self.mesh_axis) + (there - own) * self.stride
        }


class Grid:
    def __init__(self, groups, splits):
        if (groups, splits) == (8, 4):
            self.axes = {
                "z": Axis("dp", 2, 4),
                "x": Axis("dp", 1, 2),
                "y": Axis("tensor", 2, 2),
                "core": Axis("tensor", 1, 2),
            }
        elif (groups, splits) == (32, 4):
            self.axes = {
                "z": Axis("dp", 8, 4),
                "x": Axis("dp", 2, 4),
                "core": Axis("dp", 1, 2),
                "y": Axis("tensor", 1, 4),
            }
        else:
            raise ValueError("unknown mesh")
        self.orders = (("z", "x", "y", "core"), ("z", "y", "x", "core"))
        self.names = tuple(self.axes)
        self.dims = tuple(axis.size for axis in self.axes.values())
        self.copies = sum(axis.size - 1 for axis in self.axes.values())

    def greet(self):
        barrier = pltpu.get_barrier_semaphore()
        for axis in self.axes.values():
            for offset in range(1, axis.size):
                device = axis.peer(offset)[1]
                pl.semaphore_signal(barrier, inc=1, device_id=device, device_id_type=MESH_ID)
        pl.semaphore_wait(barrier, self.copies)

    def places(self):
        for flat in range(math.prod(self.dims)):
            index = []
            rest = flat
            for size in reversed(self.dims):
                index.append(rest % size)
                rest //= size
            splits = math.prod(a.size for a in self.axes.values() if a.mesh_axis == "tensor")
            yield flat // splits, flat % splits, tuple(reversed(index))


class Links:
    def __init__(self, send_sems, recv_sems):
        self.send_sems, self.recv_sems = send_sems, recv_sems
        self.count = 0
        self.open = []

    def start(self, source, target, device):
        copy = pltpu.make_async_remote_copy(
            src_ref=source,
            dst_ref=target,
            send_sem=self.send_sems.at[self.count],
            recv_sem=self.recv_sems.at[self.count],
            device_id=device,
            device_id_type=MESH_ID,
        )
        self.count += 1
        copy.start()
        self.open.append(copy)
        return copy

    def finish(self):
        for copy in self.open:
            copy.wait_send()


class Gather:
    def __init__(self, grid, shards, outs, pairs, links, moves):
        self.grid, self.shards, self.outs, self.pairs = grid, shards, outs, pairs
        self.links, self.moves = links, moves
        self.sent = {}

    def region(self, order, phase, chunk):
        index = [
            slice(None) if name in order[:phase] else self.grid.axes[name].own()
            for name in self.grid.names
        ]
        return self.outs[chunk[0]].at[(*index, *chunk[1])]

    def send(self, pair, member, phase):
        chunk = self.pairs[pair][member]
        order = self.grid.orders[member % 2]
        axis = self.grid.axes[order[phase]]
        target = self.region(order, phase, chunk)
        source = self.shards[chunk[0]].at[chunk[1]] if phase == 0 else target
        self.sent[pair, member, phase] = [
            self.links.start(source, target, axis.peer(offset)[1]) for offset in range(1, axis.size)
        ]

    def begin(self):
        for pair, chunks in enumerate(self.pairs):
            for member in range(len(chunks)):
                self.send(pair, member, 0)
        own = tuple(axis.own() for axis in self.grid.axes.values())
        self.placed = [
            self.moves.start(shard, out.at[own]) for shard, out in zip(self.shards, self.outs)
        ]

    def turns(self):
        return len(self.pairs) + 3

    def turn(self, number):
        if number == 0:
            for copy in self.placed:
                copy.wait()
        for phase in (1, 2, 3, 4):
            pair = number - (phase - 1)
            if not 0 <= pair < len(self.pairs):
                continue
            for member in range(len(self.pairs[pair])):
                for copy in self.sent[pair, member, phase - 1]:
                    copy.wait_recv()
                if phase < 4:
                    self.send(pair, member, phase)


class Part:
    def __init__(self, blocks, index, arrivals, out, half=None):
        self.blocks, self.index, self.arrivals, self.out, self.half = blocks, index, arrivals, out, half


class Reduce:
    def __init__(self, grid, links, moves):
        self.grid, self.links, self.moves = grid, links, moves
        self.sent = {}
        self.loads = {}

    def order(self, member):
        return self.grid.orders[member % 2][::-1]

    def view(self, part, member, phase, coordinate):
        order = self.order(member)
        held = part.half is not None and phase >= 0
        index = []
        for name in self.grid.names:
            if held and name == order[0]:
                continue
            if phase >= 0 and name == order[phase]:
                index.append(coordinate)
            elif name in order[: max(phase, 0)]:
                index.append(self.grid.axes[name].own())
            else:
                index.append(slice(None))
        return (part.half if held else part.blocks).at[(*index, *part.index)]

    def outgoing(self, part, member, phase, coordinate):
        if phase == 0 and part.half is not None:
            order = self.order(member)
            index = [coordinate if n == order[0] else slice(None) for n in self.grid.names]
            return part.blocks.at[(*index, *part.index)]
        return self.view(part, member, phase, coordinate)

    def send(self, key, part, member, phase):
        axis = self.grid.axes[self.order(member)[phase]]
        copies = []
        for offset in range(1, axis.size):
            there, device = axis.peer(offset)
            source = self.outgoing(part, member, phase, there)
            copies.append(self.links.start(source, part.arrivals[phase].at[offset - 1], device))
        self.sent[key, phase] = copies

    def begin(self, pairs):
        for pair in pairs:
            for member, part in enumerate(pair):
                self.send(part, part, member, 0)
        for pair in pairs:
            for member, part in enumerate(pair):
                if part.half is not None:
                    own = self.grid.axes[self.order(member)[0]].own()
                    target = part.half.at[
                        (*[slice(None)] * (len(self.grid.names) - 1), *part.index)
                    ]
                    self.loads[part] = self.moves.start(
                        self.outgoing(part, member, 0, own), target
                    )

    def advance(self, pair, phase):
        for member, part in enumerate(pair):
            for copy in self.sent[part, phase]:
                copy.wait_recv()
            if phase == 0 and part.half is not None:
                self.loads[part].wait()
            self.add(part, member, phase)
            if phase < 3:
                self.send(part, part, member, phase + 1)

    def add(self, part, member, phase):
        own = self.grid.axes[self.order(member)[phase]].own()
        target = self.view(part, member, phase, own)
        came = part.arrivals[phase]
        lead = 3 - phase

        def one(position, carry):
            index = []
            rest = position
            for size in reversed(came.shape[1 : 1 + lead]):
                index.append(lax.rem(rest, size))
                rest = rest // size
            index = tuple(reversed(index))
            total = target[index].astype(F32)
            for peer in range(came.shape[0]):
                total = total + came[(peer, *index)].astype(F32)
            if phase == 3:
                part.out[...] = total
            else:
                target[index] = total.astype(target.dtype)
            return carry

        if lead == 0:
            one(0, 0)
        else:
            lax.fori_loop(0, math.prod(came.shape[1 : 1 + lead]), one, 0)

    def turns(self, pairs):
        return len(pairs) + 3

    def turn(self, pairs, number):
        for phase in (0, 1, 2, 3):
            if 0 <= number - phase < len(pairs):
                self.advance(pairs[number - phase], phase)


class Total:
    def __init__(self, grid, value, arrivals, links):
        self.grid, self.value, self.arrivals, self.links = grid, value, arrivals, links
        self.order = grid.orders[0][::-1]

    def send(self, phase):
        axis = self.grid.axes[self.order[phase]]
        self.sent = [
            self.links.start(self.value.at[phase], self.arrivals[phase].at[offset - 1], axis.peer(offset)[1])
            for offset in range(1, axis.size)
        ]

    def advance(self, phase):
        for copy in self.sent:
            copy.wait_recv()
        total = self.value[phase]
        for peer in range(self.arrivals[phase].shape[0]):
            total = total + self.arrivals[phase][peer]
        self.value[phase + 1] = total
        if phase < 3:
            self.send(phase + 1)


def arrival_shapes(grid, member, shard, dtype):
    order = grid.orders[member % 2][::-1]
    return [
        (
            (
                grid.axes[order[phase]].size - 1,
                *[a.size for n, a in grid.axes.items() if n not in order[: phase + 1]],
                *shard,
            ),
            dtype,
        )
        for phase in range(4)
    ]


ANY = pl.BlockSpec(memory_space=pl.ANY)
WHOLE = pl.BlockSpec(memory_space=pltpu.VMEM)
SCALAR = pl.BlockSpec(memory_space=pltpu.SMEM)


class Refs:
    def __init__(self, names, refs):
        for name, ref in zip(names, refs):
            setattr(self, name, ref)


def run_kernel(body, name, ins, outs, scratch, limit, flops, copies, remote=None, collective_id=None):
    names = [*ins, *outs, *scratch]
    semaphores = [pltpu.SemaphoreType.DMA((copies,)), pltpu.SemaphoreType.DMA((2,))]
    if remote is not None:
        semaphores += [pltpu.SemaphoreType.DMA((remote,))] * 2
    moved = sum(math.prod(s) * jnp.dtype(d).itemsize for s, d, _ in outs.values())
    moved += sum(a.size * a.dtype.itemsize for a, _ in ins.values())

    def kernel(*refs):
        body(Refs([*names, "sems"], [*refs[: len(names)], refs[len(names) :]]))

    results = pl.pallas_call(
        kernel,
        name=name,
        in_specs=[spec for _, spec in ins.values()],
        out_specs=[spec for _, _, spec in outs.values()],
        out_shape=[jax.ShapeDtypeStruct(s, d) for s, d, _ in outs.values()],
        scratch_shapes=[pltpu.VMEM(s, d) for s, d in scratch.values()] + semaphores,
        compiler_params=pltpu.CompilerParams(
            vmem_limit_bytes=limit,
            collective_id=collective_id,
            has_side_effects=remote is not None,
        ),
        cost_estimate=pl.CostEstimate(flops=flops, bytes_accessed=moved, transcendentals=0),
    )(*[array for array, _ in ins.values()])
    return Refs(list(outs), results)


def fetch_weights(grid, blocks, weights, semaphore, first, slots, to=0):
    rows, cols = blocks.shape[-2:]
    target = weights.at[pl.ds(to, slots)]
    for group, split, index in grid.places():
        pltpu.make_async_copy(
            blocks.at[(*index, pl.ds(first, slots))],
            target.at[:, pl.ds(group * rows, rows), pl.ds(split * cols, cols)],
            semaphore,
        ).start()
    return pltpu.make_async_copy(target, target, semaphore)


def store_blocks(grid, blocks, slot, grad, first_split=0):
    rows, cols = blocks.shape[-2:]
    low = grad.astype(BF)
    for group, split, index in grid.places():
        begin = (split - first_split) * cols
        if 0 <= begin < low.shape[1]:
            blocks[(*index, slot)] = low[group * rows : (group + 1) * rows, begin : begin + cols]


def forward(grid, lead_turns, r):
    moves = Moves(r.sems[0])
    column = lax.axis_index("tensor")
    rows_all, width = r.low.shape
    keys = r.memory_low.shape[0]
    masters = [
        moves.start(r.attention_master, r.attention_float),
        moves.start(r.feed_master, r.feed_float),
    ]
    x_here = moves.start(r.inputs.at[pl.ds(pl.multiple_of(column * rows_all, rows_all), rows_all)], r.mix_one)
    memory_here = moves.start(r.memory.at[pl.ds(pl.multiple_of(column * keys, keys), keys)], r.mix_two)
    own_rows = r.norm_master.shape[1]
    slots = r.norm_master.shape[0]
    spot = lax.broadcasted_iota(jnp.int32, (own_rows, width), 1)
    spot_row = lax.broadcasted_iota(jnp.int32, (own_rows, width), 0) + lax.axis_index("dp") * own_rows
    spread = jnp.where(spot == spot_row, 1.0, 0.0).astype(BF)
    r.norm_shard[...] = jnp.zeros_like(r.norm_shard)
    r.norm_shard[0:slots, :] = nn(r.norm_master[...].astype(BF), spread).astype(BF)
    for copy in masters:
        copy.wait()
    r.attention_shard[...] = r.attention_float[...].astype(BF)
    r.feed_shard[...] = r.feed_float[...].astype(BF)
    grid.greet()
    attention_pairs = [[(0, (2 * p,)), (0, (2 * p + 1,))] for p in range(4)]
    attention_pairs[1].append((2, ()))
    quarter = r.feed_shard.shape[2] // 4
    feed_chunks = [
        (1, (slot, slice(None), slice(q * quarter, (q + 1) * quarter))) for slot in range(2) for q in range(4)
    ]
    feed_pairs = [feed_chunks[2 * p : 2 * p + 2] for p in range(4)]
    links = Links(r.sems[2], r.sems[3])
    gather = Gather(
        grid,
        (r.attention_shard, r.feed_shard, r.norm_shard),
        (r.attention, r.feed, r.norm_blocks),
        attention_pairs + feed_pairs,
        links,
        moves,
    )
    gather.begin()
    turns = iter(range(gather.turns()))

    def more(count):
        for _ in range(count):
            number = next(turns, None)
            if number is not None:
                gather.turn(number)

    blocks = r.owner_list.shape[0]
    block_rows = width // blocks
    for block in range(blocks):
        here = lax.broadcasted_iota(jnp.int32, (block_rows, width), 1)
        there = lax.broadcasted_iota(jnp.int32, (block_rows, width), 0) + r.owner_list[block] * block_rows
        r.place[block * block_rows : (block + 1) * block_rows, :] = jnp.where(here == there, 1.0, 0.0).astype(BF)
    moves.send(r.place, r.place_out)
    x_here.wait()
    more(1)
    r.low[...] = nn(r.mix_one[...], r.place[...]).astype(BF)
    moves.send(r.low, r.low_out)
    more(1)
    memory_here.wait()
    r.memory_low[...] = nn(r.mix_two[...], r.place[...]).astype(BF)
    moves.send(r.memory_low, r.memory_low_out)
    more(1)
    mask = r.key_mask[pl.ds(column, 1), :]
    first = lax.broadcasted_iota(jnp.int32, (1, keys), 1) == 0
    bias = jnp.where((mask == 1) | first, 0.0, FLOOR_SCORE)
    r.guard[...] = jnp.broadcast_to(bias, (PAIR, keys)).T.astype(BF)
    moves.send(r.guard, r.guard_out)
    more(lead_turns - 3)
    self_weights = fetch_weights(grid, r.attention, r.weights, r.sems[1].at[0], 0, 4)
    norm_here = moves.start(r.norm_blocks, r.norm_all)
    self_weights.wait()
    for part in range(3):
        r.qkv[:, part * width : (part + 1) * width] = nn(r.low[...], r.weights[part]).astype(BF)
    moves.send(r.qkv, r.qkv_out)
    more(1)
    for pair in range(width // PAIR):
        pair_forward(
            (r.qkv, 0), (r.qkv, width), (r.qkv, 2 * width), None, (r.mix_one, 0), r.logs_one, pair,
            r.keys_ref, r.values_t, True,
        )
        if pair % 2 == 1:
            more(1)
    moves.send(r.mix_one, r.mix_one_out)
    moves.send(r.logs_one, r.logs_one_out)
    r.unit_one[...] = nt(r.mix_one[...], r.weights[3])
    norm_here.wait()
    total = jnp.zeros((8, width), F32)
    for group, split, index in grid.places():
        if split == 0:
            total = total + r.norm_all[index][0:8, :].astype(F32)
    r.norms[...] = total

    def first_rows(rows):
        unit_rows, scale_rows = standardised(r.low[rows, :].astype(F32) + r.unit_one[rows, :])
        r.unit_one[rows, :] = unit_rows
        r.scale_one[rows, :] = wide(scale_rows)
        r.first_low[rows, :] = (unit_rows * r.norms[0:1, :] + r.norms[1:2, :]).astype(BF)

    row_loop(rows_all, first_rows)
    moves.send(r.unit_one, r.unit_one_out)
    moves.send(r.scale_one, r.scale_one_out)
    more(1)
    cross_weights = fetch_weights(grid, r.attention, r.weights, r.sems[1].at[1], 4, 4, 4)
    cross_weights.wait()
    r.query[...] = nn(r.first_low[...], r.weights[4]).astype(BF)
    moves.send(r.query, r.query_out)
    for part in range(2):
        r.key_value[:, part * width : (part + 1) * width] = nn(r.memory_low[...], r.weights[5 + part]).astype(BF)
    moves.send(r.key_value, r.key_value_out)
    for pair in range(width // PAIR):
        more(1)
        pair_forward(
            (r.query, 0), (r.key_value, 0), (r.key_value, width), r.guard, (r.mix_two, 0), r.logs_two, pair,
            r.keys_ref, r.values_t, False,
        )
    more(gather.turns())
    moves.send(r.mix_two, r.mix_two_out)
    moves.send(r.logs_two, r.logs_two_out)
    r.unit_two[...] = nt(r.mix_two[...], r.weights[7])

    def second_rows(rows):
        second_sum = r.unit_one[rows, :] * r.norms[0:1, :] + r.norms[1:2, :] + r.unit_two[rows, :]
        unit_rows, scale_rows = standardised(second_sum)
        r.unit_two[rows, :] = unit_rows
        r.scale_two[rows, :] = wide(scale_rows)

    row_loop(rows_all, second_rows)
    moves.send(r.unit_two, r.unit_two_out)
    moves.send(r.scale_two, r.scale_two_out)
    links.finish()
    moves.finish()


def gelu_both(values):
    half = 0.5 * (1.0 + lax.erf(values * (0.5**0.5)))
    bell = jnp.exp(-0.5 * values * values) * (0.5 / math.pi) ** 0.5
    return values * half, half + values * bell


def feed_both(grid, r):
    moves = Moves(r.sems[0])
    column = lax.axis_index("tensor")
    rows_all, width = r.low.shape
    first = moves.start(r.unit_in, r.unit)
    gathered = fetch_weights(grid, r.feed, r.weights, r.sems[1].at[0], 0, 2)
    begin_row = pl.multiple_of(column * rows_all, rows_all)
    others = [
        moves.start(r.low_in, r.low),
        moves.start(r.cotangent_in.at[pl.ds(begin_row, rows_all)], r.cotangent),
        moves.start(r.place_in, r.place),
        moves.start(r.scale_in, r.scale),
    ]
    hidden = r.weights.shape[2]
    chunk = min(width, hidden)
    r.sums[...] = jnp.zeros_like(r.sums)
    first.wait()
    norms = r.norms

    def second_of(rows):
        return r.unit[rows, :] * norms[2:3, :] + norms[3:4, :]

    def lower(rows):
        r.second_low[rows, :] = second_of(rows).astype(BF)

    row_loop(rows_all, lower)
    gathered.wait()
    for copy in others:
        copy.wait()
    length = r.lengths[column]
    tile_rows = min(FEED_ROWS, rows_all)

    def tile(index, carry):
        begin = pl.multiple_of(index * tile_rows, tile_rows)
        here = pl.ds(begin, tile_rows)
        cot = nn(r.cotangent[here, :], r.place[...])
        for begin_col in range(0, hidden, chunk):
            cols = slice(begin_col, begin_col + chunk)
            value, slope_part = gelu_both(nn(r.second_low[here, :], r.weights[0, :, cols]))
            r.active[here, cols] = value.astype(BF)
            r.slope[:, cols] = slope_part
        fed = nt(r.active[here, :], r.weights[1])
        for part in range(0, tile_rows, ROWS):
            rows = pl.ds(pl.multiple_of(begin + part, ROWS), ROWS)
            place_rows = lax.broadcasted_iota(jnp.int32, (ROWS, 1), 0) + (begin + part)
            live = jnp.where(place_rows < length, 1.0, 0.0)
            third_sum = second_of(rows) + fed[part : part + ROWS, :] + r.low[rows, :].astype(F32)
            unit_rows, scale_rows = standardised(third_sum)
            third = live * (unit_rows * norms[4:5, :] + norms[5:6, :])
            r.output[rows, :] = third.astype(BF)
            grad = live * cot[part : part + ROWS, :]
            grad_rows = norm_gradient(grad, norms[4:5, :], unit_rows, scale_rows)
            r.grad_third[rows, :] = grad_rows
            r.third_low[rows, :] = grad_rows.astype(BF)
            r.sums[2] += fold_rows(grad * unit_rows)
            r.sums[3] += fold_rows(grad)
        r.output[here, :] = nt(r.output[here, :], r.place[...]).astype(BF)
        for begin_col in range(0, hidden, chunk):
            cols = slice(begin_col, begin_col + chunk)
            back = nn(r.third_low[here, :], r.weights[1, :, cols]) * r.slope[:, cols]
            r.inner_grad[here, cols] = back.astype(BF)
        fed_back = nt(r.inner_grad[here, :], r.weights[0])
        for part in range(0, tile_rows, ROWS):
            rows = pl.ds(pl.multiple_of(begin + part, ROWS), ROWS)
            unit_rows = r.unit[rows, :]
            grad = fed_back[part : part + ROWS, :] + r.grad_third[rows, :]
            r.grad_second[rows, :] = norm_gradient(grad, norms[2:3, :], unit_rows, r.scale[rows, 0:1])
            r.sums[0] += fold_rows(grad * unit_rows)
            r.sums[1] += fold_rows(grad)
        return carry

    lax.fori_loop(0, rows_all // tile_rows, tile, 0)
    moves.send(r.output, r.output_out)
    moves.send(r.grad_third, r.grad_third_out)
    moves.send(r.grad_second, r.grad_second_out)
    r.norm_grads[...] = jnp.sum(r.sums[...], axis=1)
    cols_one = r.grads.shape[-1]
    for split in range(hidden // cols_one):
        cols = slice(split * cols_one, (split + 1) * cols_one)
        store_blocks(grid, r.grads, 0, tn(r.second_low[...], r.inner_grad[:, cols]), split)
        store_blocks(grid, r.grads, 1, tn(r.third_low[...], r.active[:, cols]), split)
    moves.send(r.grads, r.grads_out)
    moves.finish()


def backward(grid, names, r):
    moves = Moves(r.sems[0])
    links = Links(r.sems[2], r.sems[3])
    rows_all, width = r.mix.shape
    grid.greet()
    quarter = r.feed_grads.shape[-1] // 4

    def arrived(member, phases):
        return [getattr(r, name) for name in phases]

    feed_pairs = []
    for p in range(4):
        pair = []
        for member in range(2):
            slot, q = divmod(2 * p + member, 4)
            cols = slice(q * quarter, (q + 1) * quarter)
            pair.append(
                Part(
                    r.feed_grads, (slot, slice(None), cols), arrived(member, names["feed", p, member]),
                    r.feed_sum.at[slot, :, cols], r.feed_half,
                )
            )
        feed_pairs.append(pair)

    def attention_pairs(kind, blocks, first):
        return [
            [
                Part(
                    blocks, (2 * p + member,), arrived(member, names[kind, p, member]),
                    r.attention_sum.at[first + 2 * p + member],
                )
                for member in range(2)
            ]
            for p in range(2)
        ]

    cross_pairs = attention_pairs("cross", r.cross_grads, 4)
    self_pairs = attention_pairs("self", r.self_grads, 0)
    reduce = Reduce(grid, links, moves)
    reduce.begin(feed_pairs)

    start = moves.start(r.grad_second_in, r.grad_second)
    gathered = fetch_weights(grid, r.attention, r.weights, r.sems[1].at[0], 4, 4, 4)
    stage = [
        moves.start(r.mix_two_in, r.mix),
        moves.start(r.query_in, r.qkv.at[:, pl.ds(0, width)]),
        moves.start(r.key_value_in, r.qkv.at[:, pl.ds(width, 2 * width)]),
        moves.start(r.logs_two_in, r.logs),
        moves.start(r.guard_in, r.guard),
    ]
    late = [
        moves.start(r.memory_low_in, r.memory_low),
        moves.start(r.unit_in, r.unit),
        moves.start(r.scale_in, r.scale),
        moves.start(r.place_in, r.place),
    ]
    self_weights = fetch_weights(grid, r.attention, r.weights, r.sems[1].at[1], 0, 4, 0)
    start.wait()

    def lower(rows):
        r.grad_low[rows, :] = r.grad_second[rows, :].astype(BF)

    row_loop(rows_all, lower)
    gathered.wait()
    for copy in stage:
        copy.wait()
    r.grad_mix[...] = nn(r.grad_low[...], r.weights[7]).astype(BF)
    store_blocks(grid, r.cross_grads, 3, tn(r.grad_low[...], r.mix[...]))
    for pair in range(width // PAIR):
        reduce.turn(feed_pairs, pair)
        pair_backward(
            (r.qkv, 0), (r.qkv, width), (r.qkv, 2 * width), r.guard, (r.mix, 0), (r.grad_mix, 0), r.logs, pair,
            r.keys_ref, (r.key_sum, r.value_sum), ((r.qkv_grad, 0), (r.qkv_grad, width), (r.qkv_grad, 2 * width)),
            False,
        )
    reduce.turn(feed_pairs, 4)
    stage = [
        moves.start(r.mix_one_in, r.mix),
        moves.start(r.qkv_in, r.qkv),
        moves.start(r.logs_one_in, r.logs),
        moves.start(r.low_in, r.low),
    ]
    for copy in late:
        copy.wait()
    back_memory = nt(r.qkv_grad[:, width : 2 * width], r.weights[5]) + nt(r.qkv_grad[:, 2 * width :], r.weights[6])
    r.outgoing[...] = back_memory.astype(BF)
    r.outgoing[...] = nt(r.outgoing[...], r.place[...]).astype(BF)
    moves.send(r.outgoing, r.grad_memory_out)
    reduce.turn(feed_pairs, 5)
    r.grad_first[...] = nt(r.qkv_grad[:, :width], r.weights[4])
    r.sums[...] = jnp.zeros_like(r.sums)
    norms = r.norms

    def back(rows):
        unit_rows = r.unit[rows, :]
        grad = r.grad_first[rows, :] + r.grad_second[rows, :]
        r.first_low[rows, :] = (unit_rows * norms[0:1, :] + norms[1:2, :]).astype(BF)
        grad_rows = norm_gradient(grad, norms[0:1, :], unit_rows, r.scale[rows, 0:1])
        r.grad_first[rows, :] = grad_rows
        r.grad_low[rows, :] = grad_rows.astype(BF)
        r.sums[0] += fold_rows(grad * unit_rows)
        r.sums[1] += fold_rows(grad)

    row_loop(rows_all, back)
    third = moves.start(r.grad_third_in, r.unit)
    r.norm_value[0] = jnp.concatenate(
        [jnp.sum(r.sums[...], axis=1), r.feed_norms[...], jnp.zeros((2, width), F32)], axis=0
    )
    total = Total(grid, r.norm_value, [getattr(r, name) for name in names["norm"]], links)
    total.send(0)
    reduce.turn(feed_pairs, 6)
    store_blocks(grid, r.cross_grads, 0, tn(r.first_low[...], r.qkv_grad[:, :width]))
    store_blocks(grid, r.cross_grads, 1, tn(r.memory_low[...], r.qkv_grad[:, width : 2 * width]))
    store_blocks(grid, r.cross_grads, 2, tn(r.memory_low[...], r.qkv_grad[:, 2 * width :]))
    reduce.begin(cross_pairs)

    self_weights.wait()
    for copy in stage:
        copy.wait()
    r.grad_mix[...] = nn(r.grad_low[...], r.weights[3]).astype(BF)
    store_blocks(grid, r.self_grads, 3, tn(r.grad_low[...], r.mix[...]))
    for pair in range(width // PAIR):
        reduce.turn(cross_pairs, pair)
        total.advance(pair)
        pair_backward(
            (r.qkv, 0), (r.qkv, width), (r.qkv, 2 * width), None, (r.mix, 0), (r.grad_mix, 0), r.logs, pair,
            r.keys_ref, (r.key_sum, r.value_sum), ((r.qkv_grad, 0), (r.qkv_grad, width), (r.qkv_grad, 2 * width)),
            True,
        )
    for part in range(3):
        grad = tn(r.low[...], r.qkv_grad[:, part * width : (part + 1) * width])
        store_blocks(grid, r.self_grads, part, grad)
    reduce.begin(self_pairs)
    reduce.turn(cross_pairs, 4)
    third.wait()
    back_input = r.grad_first[...] + r.unit[...]
    for part in range(3):
        back_input = back_input + nt(r.qkv_grad[:, part * width : (part + 1) * width], r.weights[part])
    r.input_low[...] = back_input.astype(BF)
    reduce.turn(self_pairs, 0)
    r.input_low[...] = nt(r.input_low[...], r.place[...]).astype(BF)
    moves.send(r.input_low, r.grad_input_out)
    for number in range(1, reduce.turns(self_pairs)):
        reduce.turn(self_pairs, number)
    r.norm_sum[...] = r.norm_value[4]
    links.finish()
    moves.finish()


def run_layer(
    inputs, memory, cotangent, lengths, key_mask, owner_list, attention_master, feed_master, norm_master, groups, splits
):
    grid = Grid(groups, splits)
    width = inputs.shape[1]
    rows = inputs.shape[0] // splits
    keys = memory.shape[0] // splits
    own_rows = attention_master.shape[1]
    attention_t, feed_t = attention_master.shape, feed_master.shape
    hidden = splits * feed_t[2]
    pairs = width // PAIR
    low_t, full_t, keys_low_t = ((rows, width), BF), ((rows, width), F32), ((keys, width), BF)
    scale_t, logs_t, place_t = ((rows, 128), F32), ((pairs, 2, rows), F32), ((width, width), BF)
    qkv_t, key_value_t = ((rows, 3 * width), BF), ((keys, 2 * width), BF)
    guard_t, halves_t, norm_t = ((keys, PAIR), BF), ((2, keys, PAIR), BF), ((8, width), F32)
    eight_t = ((8, width, width), BF)
    attention_blocks, feed_blocks = (*grid.dims, *attention_t), (*grid.dims, *feed_t)
    norm_shard_t = ((16, width), BF)
    pair_flops = 2 * rows * keys * width
    dense = 2 * rows * width * width

    def hbm(item):
        return (*item, ANY)

    f = run_kernel(
        functools.partial(forward, grid, 5),
        "forward",
        {
            "inputs": (inputs, ANY),
            "memory": (memory, ANY),
            "key_mask": (key_mask, WHOLE),
            "owner_list": (owner_list, SCALAR),
            "attention_master": (attention_master, ANY),
            "feed_master": (feed_master, ANY),
            "norm_master": (norm_master, WHOLE),
        },
        {
            "attention": (attention_blocks, BF, ANY),
            "feed": (feed_blocks, BF, ANY),
            "norm_blocks": ((*grid.dims, *norm_shard_t[0]), BF, ANY),
            "place_out": hbm(place_t),
            "guard_out": hbm(guard_t),
            "low_out": hbm(low_t),
            "memory_low_out": hbm(keys_low_t),
            "qkv_out": hbm(qkv_t),
            "mix_one_out": hbm(low_t),
            "logs_one_out": hbm(logs_t),
            "unit_one_out": hbm(full_t),
            "scale_one_out": hbm(scale_t),
            "query_out": hbm(low_t),
            "key_value_out": hbm(key_value_t),
            "mix_two_out": hbm(low_t),
            "logs_two_out": hbm(logs_t),
            "unit_two_out": hbm(full_t),
            "scale_two_out": hbm(scale_t),
            "norms": (*norm_t, WHOLE),
        },
        {
            "attention_float": (attention_t, F32),
            "feed_float": (feed_t, F32),
            "attention_shard": (attention_t, BF),
            "feed_shard": (feed_t, BF),
            "norm_shard": norm_shard_t,
            "norm_all": ((*grid.dims, *norm_shard_t[0]), BF),
            "place": place_t,
            "guard": guard_t,
            "low": low_t,
            "memory_low": keys_low_t,
            "weights": eight_t,
            "qkv": qkv_t,
            "mix_one": low_t,
            "logs_one": logs_t,
            "unit_one": full_t,
            "scale_one": scale_t,
            "first_low": low_t,
            "query": low_t,
            "key_value": key_value_t,
            "mix_two": low_t,
            "logs_two": logs_t,
            "unit_two": full_t,
            "scale_two": scale_t,
            "keys_ref": halves_t,
            "values_t": ((PAIR, keys), BF),
        },
        58 << 20,
        10 * dense + 14 * pair_flops,
        32,
        17 * grid.copies,
        0,
    )
    d = run_kernel(
        functools.partial(feed_both, grid),
        "feed_both",
        {
            "lengths": (lengths, SCALAR),
            "low_in": (f.low_out, ANY),
            "cotangent_in": (cotangent, ANY),
            "place_in": (f.place_out, ANY),
            "feed": (f.feed, ANY),
            "norms": (f.norms, WHOLE),
            "unit_in": (f.unit_two_out, ANY),
            "scale_in": (f.scale_two_out, ANY),
        },
        {
            "output_out": hbm(low_t),
            "grad_third_out": hbm(full_t),
            "grad_second_out": hbm(full_t),
            "grads_out": (feed_blocks, BF, ANY),
            "norm_grads": ((4, width), F32, WHOLE),
        },
        {
            "low": low_t,
            "cotangent": low_t,
            "place": place_t,
            "weights": ((2, width, hidden), BF),
            "unit": full_t,
            "scale": scale_t,
            "second_low": low_t,
            "third_low": low_t,
            "active": ((rows, hidden), BF),
            "slope": ((min(FEED_ROWS, rows), hidden), F32),
            "inner_grad": ((rows, hidden), BF),
            "output": low_t,
            "grad_third": full_t,
            "grad_second": full_t,
            "grads": (feed_blocks, BF),
            "sums": ((4, 8, width), F32),
        },
        56 << 20,
        2 * dense + 12 * rows * width * hidden,
        16,
    )

    scratch = {
        "grad_second": full_t,
        "mix": low_t,
        "weights": eight_t,
        "qkv": qkv_t,
        "logs": logs_t,
        "guard": guard_t,
        "memory_low": keys_low_t,
        "low": low_t,
        "unit": full_t,
        "scale": scale_t,
        "place": place_t,
        "grad_low": low_t,
        "grad_mix": low_t,
        "qkv_grad": qkv_t,
        "first_low": low_t,
        "outgoing": keys_low_t,
        "input_low": low_t,
        "grad_first": full_t,
        "cross_grads": ((*grid.dims, 4, *attention_t[1:]), BF),
        "self_grads": ((*grid.dims, 4, *attention_t[1:]), BF),
        "feed_half": ((*[a.size for n, a in grid.axes.items() if n != "core"], *feed_t), BF),
        "sums": ((2, 8, width), F32),
        "norm_value": ((5, 8, width), F32),
        "keys_ref": halves_t,
        "key_sum": ((keys, PAIR), F32),
        "value_sum": ((keys, PAIR), F32),
    }
    names = {}
    kinds = [("feed", p, m, (feed_t[1], feed_t[2] // 4)) for p in range(4) for m in range(2)]
    kinds += [
        (kind, p, m, attention_t[1:]) for kind in ("cross", "self") for p in range(2) for m in range(2)
    ]
    for kind, p, m, shard in kinds:
        names[kind, p, m] = []
        for phase, shape in enumerate(arrival_shapes(grid, m, shard, BF)):
            name = f"{kind}{p}{m}{phase}"
            scratch[name] = shape
            names[kind, p, m].append(name)
    names["norm"] = []
    for phase, axis in enumerate(grid.orders[0][::-1]):
        scratch[f"norm{phase}"] = ((grid.axes[axis].size - 1, 8, width), F32)
        names["norm"].append(f"norm{phase}")
    b = run_kernel(
        functools.partial(backward, grid, names),
        "backward",
        {
            "grad_second_in": (d.grad_second_out, ANY),
            "mix_two_in": (f.mix_two_out, ANY),
            "attention": (f.attention, ANY),
            "query_in": (f.query_out, ANY),
            "key_value_in": (f.key_value_out, ANY),
            "logs_two_in": (f.logs_two_out, ANY),
            "guard_in": (f.guard_out, ANY),
            "memory_low_in": (f.memory_low_out, ANY),
            "unit_in": (f.unit_one_out, ANY),
            "scale_in": (f.scale_one_out, ANY),
            "place_in": (f.place_out, ANY),
            "mix_one_in": (f.mix_one_out, ANY),
            "qkv_in": (f.qkv_out, ANY),
            "logs_one_in": (f.logs_one_out, ANY),
            "low_in": (f.low_out, ANY),
            "grad_third_in": (d.grad_third_out, ANY),
            "feed_grads": (d.grads_out, ANY),
            "norms": (f.norms, WHOLE),
            "feed_norms": (d.norm_grads, WHOLE),
        },
        {
            "grad_memory_out": hbm(keys_low_t),
            "grad_input_out": hbm(low_t),
            "attention_sum": (attention_t, F32, WHOLE),
            "feed_sum": (feed_t, F32, WHOLE),
            "norm_sum": (*norm_t, WHOLE),
        },
        scratch,
        61 << 20,
        18 * dense + 35 * pair_flops,
        40,
        17 * grid.copies,
        1,
    )
    return d.output_out, b.grad_input_out, b.grad_memory_out, b.attention_sum, b.feed_sum, b.norm_sum


def adam_moments(rotated, moment, second):
    moment_new = BETA_FIRST * moment + (1.0 - BETA_FIRST) * rotated
    second_new = BETA_SECOND * second + (1.0 - BETA_SECOND) * rotated * rotated
    direction = (
        moment_new
        / (1.0 - BETA_FIRST**STEP)
        / (jnp.sqrt(second_new / (1.0 - BETA_SECOND**STEP)) + ADAM_EPSILON)
    )
    return (moment_new, second_new, direction)


def finish(weight, average, update, rate, decay):
    weight_new = weight - rate * (update + decay * weight)
    average_new = AVERAGE_DECAY * average + (1.0 - AVERAGE_DECAY) * weight_new
    return (weight_new, average_new, weight_new.astype(jnp.bfloat16))


def soap_step(weight, grad, moment, second, average, basis, rate, decay):
    rotated = jnp.einsum("src,sce->sre", grad, basis, precision=HIGHEST)
    moment_new, second_new, direction = adam_moments(rotated, moment, second)
    update = jnp.einsum("sre,sce->src", direction, basis, precision=HIGHEST)
    return (moment_new, second_new) + finish(weight, average, update, rate, decay)


def on_device(
    inputs,
    memory,
    cotangent,
    lengths,
    key_mask,
    owner_list,
    attention_master,
    attention_moment,
    attention_second,
    attention_average,
    attention_basis,
    feed_master,
    feed_moment,
    feed_second,
    feed_average,
    feed_basis,
    norm_master,
    norm_moment,
    norm_second,
    norm_average,
):
    groups = lax.axis_size("dp")
    splits = lax.axis_size("tensor")
    column = lax.axis_index("tensor")
    output, grad_input, grad_memory, attention_owned, feed_owned, norm_sum = run_layer(
        inputs,
        memory,
        cotangent,
        lengths,
        key_mask,
        owner_list,
        attention_master,
        feed_master,
        norm_master,
        groups,
        splits,
    )
    slots, own_rows = norm_master.shape
    piece = own_rows // splits
    norm_first = lax.axis_index("dp") * own_rows + column * piece
    norm_owned = lax.dynamic_slice_in_dim(norm_sum, norm_first, piece, 1)[:slots]
    attention_new = soap_step(
        attention_master,
        attention_owned,
        attention_moment,
        attention_second,
        attention_average,
        attention_basis,
        RATE_ATTENTION,
        WEIGHT_DECAY,
    )
    feed_new = soap_step(
        feed_master,
        feed_owned,
        feed_moment,
        feed_second,
        feed_average,
        feed_basis,
        RATE_FEED,
        WEIGHT_DECAY,
    )
    begin_col = column * piece

    def own_columns(array):
        return lax.dynamic_slice_in_dim(array, begin_col, piece, 1)

    moment_new, second_new, direction = adam_moments(
        norm_owned, own_columns(norm_moment), own_columns(norm_second)
    )
    norm_new = (moment_new, second_new) + finish(
        own_columns(norm_master), own_columns(norm_average), direction, RATE_NORMS, 0.0
    )
    return (output, grad_input, grad_memory) + attention_new + feed_new + norm_new


def solution(mesh):
    in_specs = (
        P("dp", None),
        P("dp", None),
        P("dp", None),
        P("dp"),
        P("dp", None),
        P(),
        P(None, "dp", "tensor"),
        P(None, "dp", "tensor"),
        P(None, "dp", "tensor"),
        P(None, "dp", "tensor"),
        P(None, "tensor", None),
        P(None, "dp", "tensor"),
        P(None, "dp", "tensor"),
        P(None, "dp", "tensor"),
        P(None, "dp", "tensor"),
        P(None, "tensor", None),
        P(None, "dp"),
        P(None, "dp"),
        P(None, "dp"),
        P(None, "dp"),
    )
    out_specs = (
        P(("dp", "tensor"), None),
        P(("dp", "tensor"), None),
        P(("dp", "tensor"), None),
        P(None, "dp", "tensor"),
        P(None, "dp", "tensor"),
        P(None, "dp", "tensor"),
        P(None, "dp", "tensor"),
        P(None, "dp", "tensor"),
        P(None, "dp", "tensor"),
        P(None, "dp", "tensor"),
        P(None, "dp", "tensor"),
        P(None, "dp", "tensor"),
        P(None, "dp", "tensor"),
        P(None, ("dp", "tensor")),
        P(None, ("dp", "tensor")),
        P(None, ("dp", "tensor")),
        P(None, ("dp", "tensor")),
        P(None, ("dp", "tensor")),
    )
    return jax.shard_map(
        on_device, mesh=mesh, in_specs=in_specs, out_specs=out_specs, check_vma=False
    )
```

```python
import functools
import math

import jax
import jax.numpy as jnp
from jax import lax
from jax.experimental import pallas as pl
from jax.experimental.pallas import tpu as pltpu
from jax.sharding import PartitionSpec as P

HDIM = 64
STEP = 10


FLOOR_SCORE = -1e30
NORM_EPSILON = 1e-05
BETA_FIRST = 0.9
BETA_SECOND = 0.95
ADAM_EPSILON = 1e-08
AVERAGE_DECAY = 0.6
RATE_ATTENTION = 0.07
RATE_FEED = 0.03
RATE_NORMS = 0.5
WEIGHT_DECAY = 0.01
HIGHEST = lax.Precision.HIGHEST


BF = jnp.bfloat16
F32 = jnp.float32
PAIR = 2 * HDIM
QUERY_BLOCK = 512
ROWS = 64
FEED_ROWS = 256


def nn(left, right):
    return lax.dot_general(left, right, (((1,), (0,)), ((), ())), preferred_element_type=F32)


def nt(left, right):
    return lax.dot_general(left, right, (((1,), (1,)), ((), ())), preferred_element_type=F32)


def tn(left, right):
    return lax.dot_general(left, right, (((0,), (0,)), ((), ())), preferred_element_type=F32)


def lane(shape):
    return lax.broadcasted_iota(jnp.int32, shape, 1)


def causal_floor(scores, key_begin, query_begin):
    key = lax.broadcasted_iota(jnp.int32, scores.shape, 0) + key_begin
    query = lax.broadcasted_iota(jnp.int32, scores.shape, 1) + query_begin
    return jnp.where(key <= query, scores, FLOOR_SCORE)


def head_queries(scaled, half, guarded):
    here = lane(scaled.shape)
    other = jnp.zeros_like(scaled)
    if guarded:
        other = jnp.where(here == (1 - half) * HDIM, jnp.ones_like(scaled), other)
    return jnp.where(here // HDIM == half, scaled, other)


def guarded_keys(keys, guard, half):
    here = lane(keys.shape)
    other = jnp.where(here == (1 - half) * HDIM, guard, jnp.zeros_like(keys))
    return jnp.where(here // HDIM == half, keys, other)


def key_chunks(begin, rows, keys, causal):
    if not causal:
        return [(0, keys, False)]
    chunks = [(0, begin, False)] if begin else []
    return chunks + [(begin, rows, True)]


def pair_forward(q, k, v, guard, mix, logs, pair, keys_ref, values_t, causal):
    rows = q[0].shape[0]
    keys = k[0].shape[0]

    def columns(operand):
        return pl.ds(pl.multiple_of(operand[1] + pair * PAIR, PAIR), PAIR)

    key_all = k[0][:, columns(k)]
    values_t[...] = v[0][:, columns(v)].T
    for half in range(2):
        keys_ref[half] = key_all if guard is None else guarded_keys(key_all, guard[...], half)
    block = min(QUERY_BLOCK if causal else rows, rows)
    for begin in range(0, rows, block):
        scaled = q[0][begin : begin + block, columns(q)] * jnp.asarray(HDIM**-0.5, BF)
        queries = [head_queries(scaled, half, guard is not None) for half in range(2)]
        chunks = key_chunks(begin, block, keys, causal)
        scores = [[], []]
        for first, count, diagonal in chunks:
            for half in range(2):
                score = nt(keys_ref[half, first : first + count, :], queries[half])
                scores[half].append(causal_floor(score, first, begin) if diagonal else score)
        tops = []
        for half in range(2):
            top = jnp.max(scores[half][0], axis=0, keepdims=True)
            for score in scores[half][1:]:
                top = jnp.maximum(top, jnp.max(score, axis=0, keepdims=True))
            tops.append(top)
        mixed = []
        for half in range(2):
            total = None
            out = None
            for (first, count, _), score in zip(chunks, scores[half]):
                expd = jnp.exp(score - tops[half])
                part = jnp.sum(expd, axis=0, keepdims=True)
                value = values_t[half * HDIM : (half + 1) * HDIM, first : first + count]
                term = nn(value, expd.astype(BF))
                total = part if total is None else total + part
                out = term if out is None else out + term
            mixed.append(out * (1.0 / total))
            logs[pair, half : half + 1, begin : begin + block] = tops[half] + jnp.log(total)
        mix[0][begin : begin + block, columns(mix)] = jnp.concatenate(mixed, axis=0).T.astype(BF)


def pair_backward(q, k, v, guard, mix, grad_mix, logs, pair, keys_ref, sums, grads, causal):
    rows = q[0].shape[0]
    keys = k[0].shape[0]
    grad_key, grad_value = sums

    def columns(operand):
        return pl.ds(pl.multiple_of(operand[1] + pair * PAIR, PAIR), PAIR)

    key_all = k[0][:, columns(k)]
    for half in range(2):
        keys_ref[half] = key_all if guard is None else guarded_keys(key_all, guard[...], half)
    keys_t = key_all.T
    block = min(QUERY_BLOCK, rows)
    for begin in range(0, rows, block):
        here = slice(begin, begin + block)
        scaled = q[0][here, columns(q)] * jnp.asarray(HDIM**-0.5, BF)
        grad = grad_mix[0][here, columns(grad_mix)]
        weighed = (grad.astype(F32) * mix[0][here, columns(mix)].astype(F32)).T
        parts = []
        for half in range(2):
            own = lane(scaled.shape) // HDIM == half
            centre = jnp.sum(weighed[half * HDIM : (half + 1) * HDIM, :], axis=0, keepdims=True)
            parts.append(
                (
                    head_queries(scaled, half, guard is not None),
                    jnp.where(own, scaled, jnp.zeros_like(scaled)),
                    jnp.where(own, grad, jnp.zeros_like(grad)),
                    centre,
                    logs[pair, half : half + 1, here],
                )
            )
        grad_query = [None, None]
        for first, count, diagonal in key_chunks(begin, block, keys, causal):
            there = slice(first, first + count)
            value = v[0][there, columns(v)]
            raw = []
            for half in range(2):
                score = nt(keys_ref[half, there, :], parts[half][0])
                if diagonal:
                    score = causal_floor(score, first, begin)
                raw.append((score, nt(value, parts[half][2])))
            low = []
            for half in range(2):
                prob = jnp.exp(raw[half][0] - parts[half][4])
                grad_score = (prob * (raw[half][1] - parts[half][3])).astype(BF)
                low.append((prob.astype(BF), grad_score))
            add_value = nn(low[0][0], parts[0][2]) + nn(low[1][0], parts[1][2])
            add_key = nn(low[0][1], parts[0][1]) + nn(low[1][1], parts[1][1])
            fresh = diagonal if causal else begin == 0
            if fresh:
                grad_value[there, :] = add_value
                grad_key[there, :] = add_key
            else:
                grad_value[there, :] += add_value
                grad_key[there, :] += add_key
            for half in range(2):
                term = nn(keys_t[half * HDIM : (half + 1) * HDIM, there], low[half][1])
                grad_query[half] = term if grad_query[half] is None else grad_query[half] + term
        both = jnp.concatenate(grad_query, axis=0).T * HDIM**-0.5
        grads[0][0][here, columns(grads[0])] = both.astype(BF)
    grads[1][0][:, columns(grads[1])] = grad_key[...].astype(BF)
    grads[2][0][:, columns(grads[2])] = grad_value[...].astype(BF)


def row_loop(rows, body, begin_row=0):
    step = min(ROWS, rows)

    def turn(index, carry):
        body(pl.ds(pl.multiple_of(begin_row + index * step, step), step))
        return carry

    lax.fori_loop(0, rows // step, turn, 0, unroll=2)


def standardised(values):
    centred = values - jnp.mean(values, axis=-1, keepdims=True)
    scale = lax.rsqrt(jnp.mean(centred * centred, axis=-1, keepdims=True) + NORM_EPSILON)
    return centred * scale, scale


def norm_gradient(grad, gain, unit, scale):
    weighted = grad * gain
    return scale * (
        weighted
        - jnp.mean(weighted, axis=-1, keepdims=True)
        - unit * jnp.mean(weighted * unit, axis=-1, keepdims=True)
    )


def fold_rows(values):
    return jnp.sum(values.reshape(values.shape[0] // 8, 8, values.shape[1]), axis=0)


def wide(scale):
    return jnp.broadcast_to(scale, (scale.shape[0], 128))


class Moves:
    def __init__(self, semaphores):
        self.semaphores = semaphores
        self.count = 0
        self.open = []

    def start(self, source, target):
        copy = pltpu.make_async_copy(source, target, self.semaphores.at[self.count])
        self.count += 1
        copy.start()
        return copy

    def send(self, source, target):
        self.open.append(self.start(source, target))

    def finish(self):
        for copy in self.open:
            copy.wait()


MESH_ID = pl.DeviceIdType.MESH


class Axis:
    def __init__(self, mesh_axis, stride, size):
        self.mesh_axis, self.stride, self.size = mesh_axis, stride, size

    def own(self):
        return lax.rem(lax.axis_index(self.mesh_axis) // self.stride, self.size)

    def peer(self, offset):
        own = self.own()
        there = lax.rem(own + offset, self.size)
        return there, {
            self.mesh_axis: lax.axis_index(self.mesh_axis) + (there - own) * self.stride
        }


class Grid:
    def __init__(self, groups, splits):
        if (groups, splits) == (8, 4):
            self.axes = {
                "z": Axis("dp", 2, 4),
                "x": Axis("dp", 1, 2),
                "y": Axis("tensor", 2, 2),
                "core": Axis("tensor", 1, 2),
            }
        elif (groups, splits) == (32, 4):
            self.axes = {
                "z": Axis("dp", 8, 4),
                "x": Axis("dp", 2, 4),
                "core": Axis("dp", 1, 2),
                "y": Axis("tensor", 1, 4),
            }
        else:
            raise ValueError("unknown mesh")
        self.orders = (("z", "x", "y", "core"), ("z", "y", "x", "core"))
        self.names = tuple(self.axes)
        self.dims = tuple(axis.size for axis in self.axes.values())
        self.copies = sum(axis.size - 1 for axis in self.axes.values())

    def greet(self):
        barrier = pltpu.get_barrier_semaphore()
        for axis in self.axes.values():
            for offset in range(1, axis.size):
                device = axis.peer(offset)[1]
                pl.semaphore_signal(barrier, inc=1, device_id=device, device_id_type=MESH_ID)

    def meet(self):
        pl.semaphore_wait(pltpu.get_barrier_semaphore(), self.copies)

    def places(self):
        for flat in range(math.prod(self.dims)):
            index = []
            rest = flat
            for size in reversed(self.dims):
                index.append(rest % size)
                rest //= size
            splits = math.prod(a.size for a in self.axes.values() if a.mesh_axis == "tensor")
            yield flat // splits, flat % splits, tuple(reversed(index))


class Links:
    def __init__(self, send_sems, recv_sems):
        self.send_sems, self.recv_sems = send_sems, recv_sems
        self.count = 0
        self.open = []

    def start(self, source, target, device):
        copy = pltpu.make_async_remote_copy(
            src_ref=source,
            dst_ref=target,
            send_sem=self.send_sems.at[self.count],
            recv_sem=self.recv_sems.at[self.count],
            device_id=device,
            device_id_type=MESH_ID,
        )
        self.count += 1
        copy.start()
        self.open.append(copy)
        return copy

    def finish(self):
        for copy in self.open:
            copy.wait_send()


class Gather:
    def __init__(self, grid, shards, outs, pairs, links, moves):
        self.grid, self.shards, self.outs, self.pairs = grid, shards, outs, pairs
        self.links, self.moves = links, moves
        self.sent = {}

    def region(self, order, phase, chunk):
        index = [
            slice(None) if name in order[:phase] else self.grid.axes[name].own()
            for name in self.grid.names
        ]
        return self.outs[chunk[0]].at[(*index, *chunk[1])]

    def send(self, pair, member, phase):
        chunk = self.pairs[pair][member]
        order = self.grid.orders[member % 2]
        axis = self.grid.axes[order[phase]]
        target = self.region(order, phase, chunk)
        source = self.shards[chunk[0]].at[chunk[1]] if phase == 0 else target
        self.sent[pair, member, phase] = [
            self.links.start(source, target, axis.peer(offset)[1]) for offset in range(1, axis.size)
        ]

    def begin(self):
        for pair, chunks in enumerate(self.pairs):
            for member in range(len(chunks)):
                self.send(pair, member, 0)
        own = tuple(axis.own() for axis in self.grid.axes.values())
        self.placed = [
            self.moves.start(shard, out.at[own]) for shard, out in zip(self.shards, self.outs)
        ]

    def place_own(self):
        for copy in self.placed:
            copy.wait()

    def advance(self, pair, phase):
        for member in range(len(self.pairs[pair])):
            for copy in self.sent[pair, member, phase - 1]:
                copy.wait_recv()
            if phase < 4:
                self.send(pair, member, phase)

    def run(self, steps):
        for pair, phase in steps:
            self.advance(pair, phase)


class Part:
    def __init__(self, blocks, index, arrivals, out, half=None):
        self.blocks, self.index, self.arrivals, self.out, self.half = blocks, index, arrivals, out, half


class Reduce:
    def __init__(self, grid, links, moves):
        self.grid, self.links, self.moves = grid, links, moves
        self.sent = {}
        self.loads = {}

    def order(self, member):
        return self.grid.orders[member % 2][::-1]

    def view(self, part, member, phase, coordinate):
        order = self.order(member)
        held = part.half is not None and phase >= 0
        index = []
        for name in self.grid.names:
            if held and name == order[0]:
                continue
            if phase >= 0 and name == order[phase]:
                index.append(coordinate)
            elif name in order[: max(phase, 0)]:
                index.append(self.grid.axes[name].own())
            else:
                index.append(slice(None))
        return (part.half if held else part.blocks).at[(*index, *part.index)]

    def outgoing(self, part, member, phase, coordinate):
        if phase == 0 and part.half is not None:
            order = self.order(member)
            index = [coordinate if n == order[0] else slice(None) for n in self.grid.names]
            return part.blocks.at[(*index, *part.index)]
        return self.view(part, member, phase, coordinate)

    def send(self, key, part, member, phase):
        axis = self.grid.axes[self.order(member)[phase]]
        copies = []
        for offset in range(1, axis.size):
            there, device = axis.peer(offset)
            source = self.outgoing(part, member, phase, there)
            copies.append(self.links.start(source, part.arrivals[phase].at[offset - 1], device))
        self.sent[key, phase] = copies

    def begin(self, pairs):
        for pair in pairs:
            for member, part in enumerate(pair):
                self.send(part, part, member, 0)
        for pair in pairs:
            for member, part in enumerate(pair):
                if part.half is not None:
                    own = self.grid.axes[self.order(member)[0]].own()
                    target = part.half.at[
                        (*[slice(None)] * (len(self.grid.names) - 1), *part.index)
                    ]
                    self.loads[part] = self.moves.start(
                        self.outgoing(part, member, 0, own), target
                    )

    def advance(self, pair, phase):
        for member, part in enumerate(pair):
            for copy in self.sent[part, phase]:
                copy.wait_recv()
            if phase == 0 and part.half is not None:
                self.loads[part].wait()
            self.add(part, member, phase)
            if phase < 3:
                self.send(part, part, member, phase + 1)

    def add(self, part, member, phase):
        own = self.grid.axes[self.order(member)[phase]].own()
        target = self.view(part, member, phase, own)
        came = part.arrivals[phase]
        if phase < 3 and came.shape[0] == 1:
            target[...] = target[...] + came[0]
            return
        total = target[...].astype(F32)
        for peer in range(came.shape[0]):
            total = total + came[peer].astype(F32)
        if phase == 3:
            part.out[...] = total
        else:
            target[...] = total.astype(target.dtype)

    def run(self, *steps):
        for pair, phase in steps:
            self.advance(pair, phase)


class Total:
    def __init__(self, grid, value, arrivals, links):
        self.grid, self.value, self.arrivals, self.links = grid, value, arrivals, links
        self.order = grid.orders[0][::-1]

    def send(self, phase):
        axis = self.grid.axes[self.order[phase]]
        self.sent = [
            self.links.start(self.value.at[phase], self.arrivals[phase].at[offset - 1], axis.peer(offset)[1])
            for offset in range(1, axis.size)
        ]

    def advance(self, phase):
        for copy in self.sent:
            copy.wait_recv()
        total = self.value[phase]
        for peer in range(self.arrivals[phase].shape[0]):
            total = total + self.arrivals[phase][peer]
        self.value[phase + 1] = total
        if phase < 3:
            self.send(phase + 1)


def arrival_shapes(grid, member, shard, dtype):
    order = grid.orders[member % 2][::-1]
    return [
        (
            (
                grid.axes[order[phase]].size - 1,
                *[a.size for n, a in grid.axes.items() if n not in order[: phase + 1]],
                *shard,
            ),
            dtype,
        )
        for phase in range(4)
    ]


ANY = pl.BlockSpec(memory_space=pl.ANY)
WHOLE = pl.BlockSpec(memory_space=pltpu.VMEM)
SCALAR = pl.BlockSpec(memory_space=pltpu.SMEM)


class Refs:
    def __init__(self, names, refs):
        for name, ref in zip(names, refs):
            setattr(self, name, ref)


def run_kernel(body, name, ins, outs, scratch, limit, flops, copies, remote=None, collective_id=None):
    names = [*ins, *outs, *scratch]
    semaphores = [pltpu.SemaphoreType.DMA((copies,)), pltpu.SemaphoreType.DMA((2,))]
    if remote is not None:
        semaphores += [pltpu.SemaphoreType.DMA((remote,))] * 2
    moved = sum(math.prod(s) * jnp.dtype(d).itemsize for s, d, _ in outs.values())
    moved += sum(a.size * a.dtype.itemsize for a, _ in ins.values())

    def kernel(*refs):
        body(Refs([*names, "sems"], [*refs[: len(names)], refs[len(names) :]]))

    results = pl.pallas_call(
        kernel,
        name=name,
        in_specs=[spec for _, spec in ins.values()],
        out_specs=[spec for _, _, spec in outs.values()],
        out_shape=[jax.ShapeDtypeStruct(s, d) for s, d, _ in outs.values()],
        scratch_shapes=[pltpu.VMEM(s, d) for s, d in scratch.values()] + semaphores,
        compiler_params=pltpu.CompilerParams(
            vmem_limit_bytes=limit,
            collective_id=collective_id,
            has_side_effects=remote is not None,
        ),
        cost_estimate=pl.CostEstimate(flops=flops, bytes_accessed=moved, transcendentals=0),
    )(*[array for array, _ in ins.values()])
    return Refs(list(outs), results)


def fetch_weights(grid, blocks, weights, semaphore, first, slots, to=0):
    rows, cols = blocks.shape[-2:]
    target = weights.at[pl.ds(to, slots)]
    for group, split, index in grid.places():
        pltpu.make_async_copy(
            blocks.at[(*index, pl.ds(first, slots))],
            target.at[:, pl.ds(group * rows, rows), pl.ds(split * cols, cols)],
            semaphore,
        ).start()
    return pltpu.make_async_copy(target, target, semaphore)


def store_blocks(grid, blocks, slot, grad, first_split=0):
    rows, cols = blocks.shape[-2:]
    low = grad.astype(BF)
    for group, split, index in grid.places():
        begin = (split - first_split) * cols
        if 0 <= begin < low.shape[1]:
            blocks[(*index, slot)] = low[group * rows : (group + 1) * rows, begin : begin + cols]


def forward(grid, r):
    grid.greet()
    moves = Moves(r.sems[0])
    column = lax.axis_index("tensor")
    rows_all, width = r.low.shape
    keys = r.memory_low.shape[0]
    masters = [
        moves.start(r.attention_master, r.attention_float),
        moves.start(r.feed_master, r.feed_float),
    ]
    x_here = moves.start(r.inputs.at[pl.ds(pl.multiple_of(column * rows_all, rows_all), rows_all)], r.mix_one)
    memory_here = moves.start(r.memory.at[pl.ds(pl.multiple_of(column * keys, keys), keys)], r.mix_two)
    own_rows = r.norm_master.shape[1]
    slots = r.norm_master.shape[0]
    spot = lax.broadcasted_iota(jnp.int32, (own_rows, width), 1)
    spot_row = lax.broadcasted_iota(jnp.int32, (own_rows, width), 0) + lax.axis_index("dp") * own_rows
    spread = jnp.where(spot == spot_row, 1.0, 0.0).astype(BF)
    r.norm_shard[...] = jnp.zeros_like(r.norm_shard)
    r.norm_shard[0:slots, :] = nn(r.norm_master[...].astype(BF), spread).astype(BF)
    for copy in masters:
        copy.wait()
    r.attention_shard[...] = r.attention_float[...].astype(BF)
    r.feed_shard[...] = r.feed_float[...].astype(BF)
    attention_pairs = [[(0, (2 * p,)), (0, (2 * p + 1,))] for p in range(4)]
    attention_pairs[1].append((2, ()))
    quarter = r.feed_shard.shape[2] // 4
    feed_chunks = [
        (1, (slot, slice(None), slice(q * quarter, (q + 1) * quarter))) for slot in range(2) for q in range(4)
    ]
    feed_pairs = [feed_chunks[2 * p : 2 * p + 2] for p in range(4)]
    links = Links(r.sems[2], r.sems[3])
    gather = Gather(
        grid,
        (r.attention_shard, r.feed_shard, r.norm_shard),
        (r.attention, r.feed, r.norm_blocks),
        attention_pairs + feed_pairs,
        links,
        moves,
    )
    grid.meet()
    gather.begin()
    blocks = r.owner_list.shape[0]
    block_rows = width // blocks
    for block in range(blocks):
        here = lax.broadcasted_iota(jnp.int32, (block_rows, width), 1)
        there = lax.broadcasted_iota(jnp.int32, (block_rows, width), 0) + r.owner_list[block] * block_rows
        r.place[block * block_rows : (block + 1) * block_rows, :] = jnp.where(here == there, 1.0, 0.0).astype(BF)
    moves.send(r.place, r.place_out)
    gather.place_own()
    gather.run([(0, 1), (1, 1), (2, 1)])
    x_here.wait()
    r.low[...] = nn(r.mix_one[...], r.place[...]).astype(BF)
    moves.send(r.low, r.low_out)
    gather.run([(0, 2), (1, 2), (3, 1)])
    memory_here.wait()
    r.memory_low[...] = nn(r.mix_two[...], r.place[...]).astype(BF)
    moves.send(r.memory_low, r.memory_low_out)
    mask = r.key_mask[pl.ds(column, 1), :]
    first = lax.broadcasted_iota(jnp.int32, (1, keys), 1) == 0
    bias = jnp.where((mask == 1) | first, 0.0, FLOOR_SCORE)
    r.guard[...] = jnp.broadcast_to(bias, (PAIR, keys)).T.astype(BF)
    moves.send(r.guard, r.guard_out)
    gather.run([(0, 3), (1, 3), (0, 4), (1, 4)])
    self_weights = fetch_weights(grid, r.attention, r.weights, r.sems[1].at[0], 0, 4)
    norm_here = moves.start(r.norm_blocks, r.norm_all)
    self_weights.wait()
    for part in range(3):
        r.qkv[:, part * width : (part + 1) * width] = nn(r.low[...], r.weights[part]).astype(BF)
    moves.send(r.qkv, r.qkv_out)
    gather.run([(2, 2), (3, 2)])
    steps = [[(4, 1)], [(2, 3), (3, 3), (5, 1)], [(4, 2)], [(2, 4), (3, 4), (5, 2), (6, 1)]]
    for pair in range(width // PAIR):
        pair_forward(
            (r.qkv, 0), (r.qkv, width), (r.qkv, 2 * width), None, (r.mix_one, 0), r.logs_one, pair,
            r.keys_ref, r.values_t, True,
        )
        gather.run(steps[pair])
    moves.send(r.mix_one, r.mix_one_out)
    moves.send(r.logs_one, r.logs_one_out)
    cross_weights = fetch_weights(grid, r.attention, r.weights, r.sems[1].at[1], 4, 4, 4)
    r.unit_one[...] = nt(r.mix_one[...], r.weights[3])
    norm_here.wait()
    total = jnp.zeros((8, width), F32)
    for group, split, index in grid.places():
        if split == 0:
            total = total + r.norm_all[index][0:8, :].astype(F32)
    r.norms[...] = total

    def first_rows(rows):
        unit_rows, scale_rows = standardised(r.low[rows, :].astype(F32) + r.unit_one[rows, :])
        r.unit_one[rows, :] = unit_rows
        r.scale_one[rows, :] = wide(scale_rows)
        r.first_low[rows, :] = (unit_rows * r.norms[0:1, :] + r.norms[1:2, :]).astype(BF)

    row_loop(rows_all, first_rows)
    moves.send(r.unit_one, r.unit_one_out)
    moves.send(r.scale_one, r.scale_one_out)
    gather.run([(4, 3), (7, 1)])
    cross_weights.wait()
    r.query[...] = nn(r.first_low[...], r.weights[4]).astype(BF)
    moves.send(r.query, r.query_out)
    for part in range(2):
        r.key_value[:, part * width : (part + 1) * width] = nn(r.memory_low[...], r.weights[5 + part]).astype(BF)
    moves.send(r.key_value, r.key_value_out)
    gather.run([(6, 2), (5, 3)])
    steps = [[(4, 4), (7, 2)], [(6, 3), (5, 4)], [(7, 3)], [(6, 4)]]
    for pair in range(width // PAIR):
        pair_forward(
            (r.query, 0), (r.key_value, 0), (r.key_value, width), r.guard, (r.mix_two, 0), r.logs_two, pair,
            r.keys_ref, r.values_t, False,
        )
        gather.run(steps[pair])
    moves.send(r.mix_two, r.mix_two_out)
    moves.send(r.logs_two, r.logs_two_out)
    r.unit_two[...] = nt(r.mix_two[...], r.weights[7])

    def second_rows(rows):
        second_sum = r.unit_one[rows, :] * r.norms[0:1, :] + r.norms[1:2, :] + r.unit_two[rows, :]
        unit_rows, scale_rows = standardised(second_sum)
        r.unit_two[rows, :] = unit_rows
        r.scale_two[rows, :] = wide(scale_rows)

    row_loop(rows_all, second_rows)
    gather.run([(7, 4)])
    moves.send(r.unit_two, r.unit_two_out)
    moves.send(r.scale_two, r.scale_two_out)
    links.finish()
    moves.finish()


def gelu_both(values):
    half = 0.5 * (1.0 + lax.erf(values * (0.5**0.5)))
    bell = jnp.exp(-0.5 * values * values) * (0.5 / math.pi) ** 0.5
    return values * half, half + values * bell


def feed_both(grid, r):
    moves = Moves(r.sems[0])
    column = lax.axis_index("tensor")
    rows_all, width = r.low.shape
    first = moves.start(r.unit_in, r.unit)
    gathered = fetch_weights(grid, r.feed, r.weights, r.sems[1].at[0], 0, 2)
    begin_row = pl.multiple_of(column * rows_all, rows_all)
    others = [
        moves.start(r.low_in, r.low),
        moves.start(r.cotangent_in.at[pl.ds(begin_row, rows_all)], r.cotangent),
        moves.start(r.place_in, r.place),
        moves.start(r.scale_in, r.scale),
    ]
    hidden = r.weights.shape[2]
    chunk = min(width, hidden)
    r.sums[...] = jnp.zeros_like(r.sums)
    first.wait()
    norms = r.norms

    def second_of(rows):
        return r.unit[rows, :] * norms[2:3, :] + norms[3:4, :]

    def lower(rows):
        r.second_low[rows, :] = second_of(rows).astype(BF)

    row_loop(rows_all, lower)
    gathered.wait()
    for copy in others:
        copy.wait()
    length = r.lengths[column]
    tile_rows = min(FEED_ROWS, rows_all)

    def tile(index, carry):
        begin = pl.multiple_of(index * tile_rows, tile_rows)
        here = pl.ds(begin, tile_rows)
        cot = nn(r.cotangent[here, :], r.place[...])
        for begin_col in range(0, hidden, chunk):
            cols = slice(begin_col, begin_col + chunk)
            value, slope_part = gelu_both(nn(r.second_low[here, :], r.weights[0, :, cols]))
            r.active[here, cols] = value.astype(BF)
            r.slope[:, cols] = slope_part
        fed = nt(r.active[here, :], r.weights[1])
        for part in range(0, tile_rows, ROWS):
            rows = pl.ds(pl.multiple_of(begin + part, ROWS), ROWS)
            place_rows = lax.broadcasted_iota(jnp.int32, (ROWS, 1), 0) + (begin + part)
            live = jnp.where(place_rows < length, 1.0, 0.0)
            third_sum = second_of(rows) + fed[part : part + ROWS, :] + r.low[rows, :].astype(F32)
            unit_rows, scale_rows = standardised(third_sum)
            third = live * (unit_rows * norms[4:5, :] + norms[5:6, :])
            r.output[rows, :] = third.astype(BF)
            grad = live * cot[part : part + ROWS, :]
            grad_rows = norm_gradient(grad, norms[4:5, :], unit_rows, scale_rows)
            r.grad_third[rows, :] = grad_rows
            r.third_low[rows, :] = grad_rows.astype(BF)
            r.sums[2] += fold_rows(grad * unit_rows)
            r.sums[3] += fold_rows(grad)
        r.output[here, :] = nt(r.output[here, :], r.place[...]).astype(BF)
        for begin_col in range(0, hidden, chunk):
            cols = slice(begin_col, begin_col + chunk)
            back = nn(r.third_low[here, :], r.weights[1, :, cols]) * r.slope[:, cols]
            r.inner_grad[here, cols] = back.astype(BF)
        fed_back = nt(r.inner_grad[here, :], r.weights[0])
        for part in range(0, tile_rows, ROWS):
            rows = pl.ds(pl.multiple_of(begin + part, ROWS), ROWS)
            unit_rows = r.unit[rows, :]
            grad = fed_back[part : part + ROWS, :] + r.grad_third[rows, :]
            r.grad_second[rows, :] = norm_gradient(grad, norms[2:3, :], unit_rows, r.scale[rows, 0:1])
            r.sums[0] += fold_rows(grad * unit_rows)
            r.sums[1] += fold_rows(grad)
        return carry

    lax.fori_loop(0, rows_all // tile_rows, tile, 0)
    moves.send(r.output, r.output_out)
    moves.send(r.grad_third, r.grad_third_out)
    moves.send(r.grad_second, r.grad_second_out)
    r.norm_grads[...] = jnp.sum(r.sums[...], axis=1)
    cols_one = r.grads.shape[-1]
    for split in range(hidden // cols_one):
        cols = slice(split * cols_one, (split + 1) * cols_one)
        store_blocks(grid, r.grads, 0, tn(r.second_low[...], r.inner_grad[:, cols]), split)
        store_blocks(grid, r.grads, 1, tn(r.third_low[...], r.active[:, cols]), split)
    moves.send(r.grads, r.grads_out)
    moves.finish()


def backward(grid, names, r):
    grid.greet()
    moves = Moves(r.sems[0])
    links = Links(r.sems[2], r.sems[3])
    rows_all, width = r.mix.shape
    quarter = r.feed_grads.shape[-1] // 4

    def arrived(member, phases):
        return [getattr(r, name) for name in phases]

    feed_pairs = []
    for p in range(4):
        pair = []
        for member in range(2):
            slot, q = divmod(2 * p + member, 4)
            cols = slice(q * quarter, (q + 1) * quarter)
            pair.append(
                Part(
                    r.feed_grads, (slot, slice(None), cols), arrived(member, names["feed", p, member]),
                    r.feed_sum.at[slot, :, cols], r.feed_half,
                )
            )
        feed_pairs.append(pair)

    def attention_pairs(kind, blocks, first):
        return [
            [
                Part(
                    blocks, (2 * p + member,), arrived(member, names[kind, p, member]),
                    r.attention_sum.at[first + 2 * p + member],
                )
                for member in range(2)
            ]
            for p in range(2)
        ]

    cross_pairs = attention_pairs("cross", r.cross_grads, 4)
    self_pairs = attention_pairs("self", r.self_grads, 0)
    cross_pairs.append([self_pairs[1].pop()])
    reduce = Reduce(grid, links, moves)
    start = moves.start(r.grad_second_in, r.grad_second)
    gathered = fetch_weights(grid, r.attention, r.weights, r.sems[1].at[0], 4, 4, 4)
    stage = [
        moves.start(r.mix_two_in, r.mix),
        moves.start(r.query_in, r.qkv.at[:, pl.ds(0, width)]),
        moves.start(r.key_value_in, r.qkv.at[:, pl.ds(width, 2 * width)]),
        moves.start(r.logs_two_in, r.logs),
        moves.start(r.guard_in, r.guard),
    ]
    late = [
        moves.start(r.memory_low_in, r.memory_low),
        moves.start(r.unit_in, r.unit),
        moves.start(r.scale_in, r.scale),
    ]
    self_weights = fetch_weights(grid, r.attention, r.weights, r.sems[1].at[1], 0, 4, 0)
    start.wait()

    def lower(rows):
        r.grad_low[rows, :] = r.grad_second[rows, :].astype(BF)

    row_loop(rows_all, lower)
    grid.meet()
    reduce.begin(feed_pairs)
    gathered.wait()
    for copy in stage:
        copy.wait()
    r.grad_mix[...] = nn(r.grad_low[...], r.weights[7]).astype(BF)
    store_blocks(grid, r.cross_grads, 3, tn(r.grad_low[...], r.mix[...]))
    f0, f1, f2, f3 = feed_pairs
    reduce.run((f0, 0), (f1, 0))
    steps = [
        [(f2, 0), (f0, 1)],
        [(f1, 1), (f3, 0), (f0, 2)],
        [(f2, 1), (f1, 2), (f0, 3)],
        [(f3, 1), (f2, 2), (f1, 3)],
    ]
    for pair in range(width // PAIR):
        pair_backward(
            (r.qkv, 0), (r.qkv, width), (r.qkv, 2 * width), r.guard, (r.mix, 0), (r.grad_mix, 0), r.logs, pair,
            r.keys_ref, (r.key_sum, r.value_sum), ((r.qkv_grad, 0), (r.qkv_grad, width), (r.qkv_grad, 2 * width)),
            False,
        )
        reduce.run(*steps[pair])
    stage = [
        moves.start(r.mix_one_in, r.mix),
        moves.start(r.qkv_in, r.qkv),
        moves.start(r.logs_one_in, r.logs),
        moves.start(r.low_in, r.low),
    ]
    for copy in late:
        copy.wait()
    r.key_value_grad[...] = r.qkv_grad[:, width:]
    reduce.run((f3, 2), (f2, 3))
    r.grad_first[...] = nt(r.qkv_grad[:, :width], r.weights[4])
    r.sums[...] = jnp.zeros_like(r.sums)
    norms = r.norms

    def back(rows):
        unit_rows = r.unit[rows, :]
        grad = r.grad_first[rows, :] + r.grad_second[rows, :]
        r.first_low[rows, :] = (unit_rows * norms[0:1, :] + norms[1:2, :]).astype(BF)
        grad_rows = norm_gradient(grad, norms[0:1, :], unit_rows, r.scale[rows, 0:1])
        r.grad_first[rows, :] = grad_rows
        r.grad_low[rows, :] = grad_rows.astype(BF)
        r.sums[0] += fold_rows(grad * unit_rows)
        r.sums[1] += fold_rows(grad)

    row_loop(rows_all, back)
    third = moves.start(r.grad_third_in, r.unit)
    r.norm_value[0] = jnp.concatenate(
        [jnp.sum(r.sums[...], axis=1), r.feed_norms[...], jnp.zeros((2, width), F32)], axis=0
    )
    total = Total(grid, r.norm_value, [getattr(r, name) for name in names["norm"]], links)
    total.send(0)
    reduce.run((f3, 3))
    store_blocks(grid, r.cross_grads, 0, tn(r.first_low[...], r.qkv_grad[:, :width]))
    store_blocks(grid, r.cross_grads, 1, tn(r.memory_low[...], r.qkv_grad[:, width : 2 * width]))
    store_blocks(grid, r.cross_grads, 2, tn(r.memory_low[...], r.qkv_grad[:, 2 * width :]))
    reduce.begin(cross_pairs[:2])

    self_weights.wait()
    for copy in stage:
        copy.wait()
    r.grad_mix[...] = nn(r.grad_low[...], r.weights[3]).astype(BF)
    store_blocks(grid, r.self_grads, 3, tn(r.grad_low[...], r.mix[...]))
    reduce.begin(cross_pairs[2:])
    c0, c1, c2 = cross_pairs
    reduce.run((c0, 0), (c1, 0))
    steps = [
        [(c2, 0), (c0, 1)],
        [(c1, 1), (c0, 2)],
        [(c2, 1), (c1, 2), (c0, 3)],
        [(c2, 2), (c1, 3)],
    ]
    for pair in range(width // PAIR):
        pair_backward(
            (r.qkv, 0), (r.qkv, width), (r.qkv, 2 * width), None, (r.mix, 0), (r.grad_mix, 0), r.logs, pair,
            r.keys_ref, (r.key_sum, r.value_sum), ((r.qkv_grad, 0), (r.qkv_grad, width), (r.qkv_grad, 2 * width)),
            True,
        )
        total.advance(pair)
        reduce.run(*steps[pair])
    s0, s1 = self_pairs
    for part in range(3):
        grad = tn(r.low[...], r.qkv_grad[:, part * width : (part + 1) * width])
        store_blocks(grid, r.self_grads, part, grad)
        if part == 1:
            reduce.begin([s0])
    reduce.begin([s1])
    reduce.run((s0, 0), (c2, 3))
    third.wait()
    back_input = r.grad_first[...] + r.unit[...]
    back_input = back_input + nt(r.qkv_grad[:, :width], r.weights[0])
    reduce.run((s1, 0))
    back_input = back_input + nt(r.qkv_grad[:, width : 2 * width], r.weights[1])
    back_input = back_input + nt(r.qkv_grad[:, 2 * width :], r.weights[2])
    r.input_low[...] = back_input.astype(BF)
    moves.send(r.input_low, r.grad_input_out)
    reduce.run((s0, 1))
    back_memory = nt(r.key_value_grad[:, :width], r.weights[5])
    reduce.run((s1, 1))
    back_memory = back_memory + nt(r.key_value_grad[:, width:], r.weights[6])
    r.outgoing[...] = back_memory.astype(BF)
    moves.send(r.outgoing, r.grad_memory_out)
    reduce.run((s0, 2), (s1, 2), (s0, 3), (s1, 3))
    r.norm_sum[...] = r.norm_value[4]
    links.finish()
    moves.finish()


def run_layer(
    inputs, memory, cotangent, lengths, key_mask, owner_list, attention_master, feed_master, norm_master, groups, splits
):
    grid = Grid(groups, splits)
    width = inputs.shape[1]
    rows = inputs.shape[0] // splits
    keys = memory.shape[0] // splits
    own_rows = attention_master.shape[1]
    attention_t, feed_t = attention_master.shape, feed_master.shape
    hidden = splits * feed_t[2]
    pairs = width // PAIR
    low_t, full_t, keys_low_t = ((rows, width), BF), ((rows, width), F32), ((keys, width), BF)
    scale_t, logs_t, place_t = ((rows, 128), F32), ((pairs, 2, rows), F32), ((width, width), BF)
    qkv_t, key_value_t = ((rows, 3 * width), BF), ((keys, 2 * width), BF)
    guard_t, halves_t, norm_t = ((keys, PAIR), BF), ((2, keys, PAIR), BF), ((8, width), F32)
    eight_t = ((8, width, width), BF)
    attention_blocks, feed_blocks = (*grid.dims, *attention_t), (*grid.dims, *feed_t)
    norm_shard_t = ((16, width), BF)
    pair_flops = 2 * rows * keys * width
    dense = 2 * rows * width * width

    def hbm(item):
        return (*item, ANY)

    f = run_kernel(
        functools.partial(forward, grid),
        "forward",
        {
            "inputs": (inputs, ANY),
            "memory": (memory, ANY),
            "key_mask": (key_mask, WHOLE),
            "owner_list": (owner_list, SCALAR),
            "attention_master": (attention_master, ANY),
            "feed_master": (feed_master, ANY),
            "norm_master": (norm_master, WHOLE),
        },
        {
            "attention": (attention_blocks, BF, ANY),
            "feed": (feed_blocks, BF, ANY),
            "norm_blocks": ((*grid.dims, *norm_shard_t[0]), BF, ANY),
            "place_out": hbm(place_t),
            "guard_out": hbm(guard_t),
            "low_out": hbm(low_t),
            "memory_low_out": hbm(keys_low_t),
            "qkv_out": hbm(qkv_t),
            "mix_one_out": hbm(low_t),
            "logs_one_out": hbm(logs_t),
            "unit_one_out": hbm(full_t),
            "scale_one_out": hbm(scale_t),
            "query_out": hbm(low_t),
            "key_value_out": hbm(key_value_t),
            "mix_two_out": hbm(low_t),
            "logs_two_out": hbm(logs_t),
            "unit_two_out": hbm(full_t),
            "scale_two_out": hbm(scale_t),
            "norms": (*norm_t, WHOLE),
        },
        {
            "attention_float": (attention_t, F32),
            "feed_float": (feed_t, F32),
            "attention_shard": (attention_t, BF),
            "feed_shard": (feed_t, BF),
            "norm_shard": norm_shard_t,
            "norm_all": ((*grid.dims, *norm_shard_t[0]), BF),
            "place": place_t,
            "guard": guard_t,
            "low": low_t,
            "memory_low": keys_low_t,
            "weights": eight_t,
            "qkv": qkv_t,
            "mix_one": low_t,
            "logs_one": logs_t,
            "unit_one": full_t,
            "scale_one": scale_t,
            "first_low": low_t,
            "query": low_t,
            "key_value": key_value_t,
            "mix_two": low_t,
            "logs_two": logs_t,
            "unit_two": full_t,
            "scale_two": scale_t,
            "keys_ref": halves_t,
            "values_t": ((PAIR, keys), BF),
        },
        58 << 20,
        10 * dense + 14 * pair_flops,
        32,
        17 * grid.copies,
        0,
    )
    d = run_kernel(
        functools.partial(feed_both, grid),
        "feed_both",
        {
            "lengths": (lengths, SCALAR),
            "low_in": (f.low_out, ANY),
            "cotangent_in": (cotangent, ANY),
            "place_in": (f.place_out, ANY),
            "feed": (f.feed, ANY),
            "norms": (f.norms, WHOLE),
            "unit_in": (f.unit_two_out, ANY),
            "scale_in": (f.scale_two_out, ANY),
        },
        {
            "output_out": hbm(low_t),
            "grad_third_out": hbm(full_t),
            "grad_second_out": hbm(full_t),
            "grads_out": (feed_blocks, BF, ANY),
            "norm_grads": ((4, width), F32, WHOLE),
        },
        {
            "low": low_t,
            "cotangent": low_t,
            "place": place_t,
            "weights": ((2, width, hidden), BF),
            "unit": full_t,
            "scale": scale_t,
            "second_low": low_t,
            "third_low": low_t,
            "active": ((rows, hidden), BF),
            "slope": ((min(FEED_ROWS, rows), hidden), F32),
            "inner_grad": ((rows, hidden), BF),
            "output": low_t,
            "grad_third": full_t,
            "grad_second": full_t,
            "grads": (feed_blocks, BF),
            "sums": ((4, 8, width), F32),
        },
        56 << 20,
        2 * dense + 12 * rows * width * hidden,
        16,
    )

    scratch = {
        "grad_second": full_t,
        "mix": low_t,
        "weights": eight_t,
        "qkv": qkv_t,
        "logs": logs_t,
        "guard": guard_t,
        "memory_low": keys_low_t,
        "low": low_t,
        "unit": full_t,
        "scale": scale_t,
        "grad_low": low_t,
        "key_value_grad": key_value_t,
        "grad_mix": low_t,
        "qkv_grad": qkv_t,
        "first_low": low_t,
        "outgoing": keys_low_t,
        "input_low": low_t,
        "grad_first": full_t,
        "cross_grads": ((*grid.dims, 4, *attention_t[1:]), BF),
        "self_grads": ((*grid.dims, 4, *attention_t[1:]), BF),
        "feed_half": ((*[a.size for n, a in grid.axes.items() if n != "core"], *feed_t), BF),
        "sums": ((2, 8, width), F32),
        "norm_value": ((5, 8, width), F32),
        "keys_ref": halves_t,
        "key_sum": ((keys, PAIR), F32),
        "value_sum": ((keys, PAIR), F32),
    }
    names = {}
    kinds = [("feed", p, m, (feed_t[1], feed_t[2] // 4)) for p in range(4) for m in range(2)]
    kinds += [
        (kind, p, m, attention_t[1:]) for kind in ("cross", "self") for p in range(2) for m in range(2)
    ]
    for kind, p, m, shard in kinds:
        names[kind, p, m] = []
        parity = 0 if (kind, p) == ("self", 1) else m
        for phase, shape in enumerate(arrival_shapes(grid, parity, shard, BF)):
            name = f"{kind}{p}{m}{phase}"
            scratch[name] = shape
            names[kind, p, m].append(name)
    names["norm"] = []
    for phase, axis in enumerate(grid.orders[0][::-1]):
        scratch[f"norm{phase}"] = ((grid.axes[axis].size - 1, 8, width), F32)
        names["norm"].append(f"norm{phase}")
    b = run_kernel(
        functools.partial(backward, grid, names),
        "backward",
        {
            "grad_second_in": (d.grad_second_out, ANY),
            "mix_two_in": (f.mix_two_out, ANY),
            "attention": (f.attention, ANY),
            "query_in": (f.query_out, ANY),
            "key_value_in": (f.key_value_out, ANY),
            "logs_two_in": (f.logs_two_out, ANY),
            "guard_in": (f.guard_out, ANY),
            "memory_low_in": (f.memory_low_out, ANY),
            "unit_in": (f.unit_one_out, ANY),
            "scale_in": (f.scale_one_out, ANY),
            "mix_one_in": (f.mix_one_out, ANY),
            "qkv_in": (f.qkv_out, ANY),
            "logs_one_in": (f.logs_one_out, ANY),
            "low_in": (f.low_out, ANY),
            "grad_third_in": (d.grad_third_out, ANY),
            "feed_grads": (d.grads_out, ANY),
            "norms": (f.norms, WHOLE),
            "feed_norms": (d.norm_grads, WHOLE),
        },
        {
            "grad_memory_out": hbm(keys_low_t),
            "grad_input_out": hbm(low_t),
            "attention_sum": (attention_t, F32, WHOLE),
            "feed_sum": (feed_t, F32, WHOLE),
            "norm_sum": (*norm_t, WHOLE),
        },
        scratch,
        61 << 20,
        18 * dense + 35 * pair_flops,
        40,
        17 * grid.copies,
        1,
    )
    return d.output_out, b.grad_input_out, b.grad_memory_out, b.attention_sum, b.feed_sum, b.norm_sum, f.place_out


def adam_moments(rotated, moment, second):
    moment_new = BETA_FIRST * moment + (1.0 - BETA_FIRST) * rotated
    second_new = BETA_SECOND * second + (1.0 - BETA_SECOND) * rotated * rotated
    direction = (
        moment_new
        / (1.0 - BETA_FIRST**STEP)
        / (jnp.sqrt(second_new / (1.0 - BETA_SECOND**STEP)) + ADAM_EPSILON)
    )
    return (moment_new, second_new, direction)


def finish(weight, average, update, rate, decay):
    weight_new = weight - rate * (update + decay * weight)
    average_new = AVERAGE_DECAY * average + (1.0 - AVERAGE_DECAY) * weight_new
    return (weight_new, average_new, weight_new.astype(jnp.bfloat16))


def split(values):
    high = values.astype(BF)
    return high, (values - high.astype(F32)).astype(BF)


def rotate(values, basis, back):
    times = nt if back else nn
    rows = values[0].shape[0]
    top = times(jnp.concatenate(values, axis=0), basis[0])
    return top[:rows] + top[rows:] + times(values[0], basis[1])


STATES = ("grad", "master", "moment", "second", "average", "basis")
RESULTS = ("moment", "second", "weight", "average", "copy")


def update(r):
    moves = Moves(r.sems[0])
    lead = [
        (moves.start(r.place_in, r.place), moves.start(r.grad_input_in, r.grad_input)),
        (moves.start(r.grad_memory_in, r.grad_memory),),
    ]
    loads = {
        (kind, name): moves.start(getattr(r, f"{kind}_{name}_in"), getattr(r, f"{kind}_{name}"))
        for kind in ("attention", "feed")
        for name in STATES
    }
    for copies, low, out in zip(
        lead, (r.grad_input, r.grad_memory), (r.grad_input_out, r.grad_memory_out)
    ):
        for copy in copies:
            copy.wait()
        low[...] = nt(low[...], r.place[...]).astype(BF)
        moves.send(low, out)
    for kind, rate in (("attention", RATE_ATTENTION), ("feed", RATE_FEED)):
        for name in STATES:
            loads[kind, name].wait()
        grad, master, moment, second, average, basis = (getattr(r, f"{kind}_{n}") for n in STATES)
        low = getattr(r, f"{kind}_copy")
        for slot in range(grad.shape[0]):
            turn = split(basis[slot])
            rotated = rotate(split(grad[slot]), turn, False)
            moment[slot], second[slot], direction = adam_moments(rotated, moment[slot], second[slot])
            master[slot], average[slot], low[slot] = finish(
                master[slot], average[slot], rotate(split(direction), turn, True), rate, WEIGHT_DECAY
            )
        for name, ref in zip(RESULTS, (moment, second, master, average, low)):
            moves.send(ref, getattr(r, f"{kind}_{name}_out"))
    slots, own_rows = r.norm_master_in.shape
    piece = r.norm_moment_out.shape[1]

    def own(values, first):
        shape = (values.shape[1], 128)
        here = lax.broadcasted_iota(jnp.int32, shape, 0)
        there = lax.broadcasted_iota(jnp.int32, shape, 1)
        select = jnp.where(here == there + first, 1.0, 0.0)
        picked = lax.dot_general(
            values, select, (((1,), (0,)), ((), ())), precision=HIGHEST, preferred_element_type=F32
        )
        return picked[:slots, :piece]

    begin = lax.axis_index("tensor") * piece
    grad = own(r.norm_sum[...], lax.axis_index("dp") * own_rows + begin)
    master, moment, second, average = (
        own(ref[...], begin)
        for ref in (r.norm_master_in, r.norm_moment_in, r.norm_second_in, r.norm_average_in)
    )
    moment, second, direction = adam_moments(grad, moment, second)
    results = (moment, second, *finish(master, average, direction, RATE_NORMS, 0.0))
    for name, value in zip(RESULTS, results):
        getattr(r, f"norm_{name}_out")[...] = value
    moves.finish()


def run_update(grad_input, grad_memory, place, norm_sum, states):
    ins = {
        "grad_input_in": (grad_input, ANY),
        "grad_memory_in": (grad_memory, ANY),
        "place_in": (place, ANY),
        "norm_sum": (norm_sum, WHOLE),
    }
    outs = {
        "grad_input_out": (grad_input.shape, BF, ANY),
        "grad_memory_out": (grad_memory.shape, BF, ANY),
    }
    scratch = {
        "place": (place.shape, BF),
        "grad_input": (grad_input.shape, BF),
        "grad_memory": (grad_memory.shape, BF),
    }
    for kind in ("attention", "feed"):
        shape = states[kind]["grad"].shape
        for name in STATES:
            ins[f"{kind}_{name}_in"] = (states[kind][name], ANY)
            scratch[f"{kind}_{name}"] = (states[kind][name].shape, F32)
        scratch[f"{kind}_copy"] = (shape, BF)
        for name in RESULTS:
            outs[f"{kind}_{name}_out"] = (shape, BF if name == "copy" else F32, ANY)
    for name, array in states["norm"].items():
        ins[f"norm_{name}_in"] = (array, WHOLE)
    slots, own_rows = states["norm"]["master"].shape
    for name in RESULTS:
        shape = (slots, own_rows // lax.axis_size("tensor"))
        outs[f"norm_{name}_out"] = (shape, BF if name == "copy" else F32, WHOLE)
    return run_kernel(update, "update", ins, outs, scratch, 60 << 20, 1 << 31, 32)


def on_device(
    inputs,
    memory,
    cotangent,
    lengths,
    key_mask,
    owner_list,
    attention_master,
    attention_moment,
    attention_second,
    attention_average,
    attention_basis,
    feed_master,
    feed_moment,
    feed_second,
    feed_average,
    feed_basis,
    norm_master,
    norm_moment,
    norm_second,
    norm_average,
):
    groups = lax.axis_size("dp")
    splits = lax.axis_size("tensor")
    output, grad_input, grad_memory, attention_grad, feed_grad, norm_sum, place = run_layer(
        inputs,
        memory,
        cotangent,
        lengths,
        key_mask,
        owner_list,
        attention_master,
        feed_master,
        norm_master,
        groups,
        splits,
    )
    u = run_update(
        grad_input,
        grad_memory,
        place,
        norm_sum,
        {
            "attention": dict(
                grad=attention_grad,
                master=attention_master,
                moment=attention_moment,
                second=attention_second,
                average=attention_average,
                basis=attention_basis,
            ),
            "feed": dict(
                grad=feed_grad,
                master=feed_master,
                moment=feed_moment,
                second=feed_second,
                average=feed_average,
                basis=feed_basis,
            ),
            "norm": dict(
                master=norm_master, moment=norm_moment, second=norm_second, average=norm_average
            ),
        },
    )
    results = [
        getattr(u, f"{kind}_{name}_out") for kind in ("attention", "feed", "norm") for name in RESULTS
    ]
    return (output, u.grad_input_out, u.grad_memory_out, *results)


def solution(mesh):
    in_specs = (
        P("dp", None),
        P("dp", None),
        P("dp", None),
        P("dp"),
        P("dp", None),
        P(),
        P(None, "dp", "tensor"),
        P(None, "dp", "tensor"),
        P(None, "dp", "tensor"),
        P(None, "dp", "tensor"),
        P(None, "tensor", None),
        P(None, "dp", "tensor"),
        P(None, "dp", "tensor"),
        P(None, "dp", "tensor"),
        P(None, "dp", "tensor"),
        P(None, "tensor", None),
        P(None, "dp"),
        P(None, "dp"),
        P(None, "dp"),
        P(None, "dp"),
    )
    out_specs = (
        P(("dp", "tensor"), None),
        P(("dp", "tensor"), None),
        P(("dp", "tensor"), None),
        P(None, "dp", "tensor"),
        P(None, "dp", "tensor"),
        P(None, "dp", "tensor"),
        P(None, "dp", "tensor"),
        P(None, "dp", "tensor"),
        P(None, "dp", "tensor"),
        P(None, "dp", "tensor"),
        P(None, "dp", "tensor"),
        P(None, "dp", "tensor"),
        P(None, "dp", "tensor"),
        P(None, ("dp", "tensor")),
        P(None, ("dp", "tensor")),
        P(None, ("dp", "tensor")),
        P(None, ("dp", "tensor")),
        P(None, ("dp", "tensor")),
    )
    return jax.shard_map(
        on_device, mesh=mesh, in_specs=in_specs, out_specs=out_specs, check_vma=False
    )
```

```python
import functools
import math

import jax
import jax.numpy as jnp
from jax import lax
from jax.experimental import pallas as pl
from jax.experimental.pallas import tpu as pltpu
from jax.sharding import PartitionSpec as P

HDIM = 64
STEP = 10


FLOOR_SCORE = -1e30
NORM_EPSILON = 1e-05
BETA_FIRST = 0.9
BETA_SECOND = 0.95
ADAM_EPSILON = 1e-08
AVERAGE_DECAY = 0.6
RATE_ATTENTION = 0.07
RATE_FEED = 0.03
RATE_NORMS = 0.5
WEIGHT_DECAY = 0.01
HIGHEST = lax.Precision.HIGHEST


BF = jnp.bfloat16
F32 = jnp.float32
PAIR = 2 * HDIM
QUERY_BLOCK = 512
ROWS = 128
FEED_ROWS = 512


def nn(left, right):
    return lax.dot_general(left, right, (((1,), (0,)), ((), ())), preferred_element_type=F32)


def nt(left, right):
    return lax.dot_general(left, right, (((1,), (1,)), ((), ())), preferred_element_type=F32)


def tn(left, right):
    return lax.dot_general(left, right, (((0,), (0,)), ((), ())), preferred_element_type=F32)


def lane(shape):
    return lax.broadcasted_iota(jnp.int32, shape, 1)


def causal_floor(scores, key_begin, query_begin):
    key = lax.broadcasted_iota(jnp.int32, scores.shape, 0) + key_begin
    query = lax.broadcasted_iota(jnp.int32, scores.shape, 1) + query_begin
    return jnp.where(key <= query, scores, FLOOR_SCORE)


def head_queries(scaled, half, guarded):
    here = lane(scaled.shape)
    other = jnp.zeros_like(scaled)
    if guarded:
        other = jnp.where(here == (1 - half) * HDIM, jnp.ones_like(scaled), other)
    return jnp.where(here // HDIM == half, scaled, other)


def guarded_keys(keys, guard, half):
    here = lane(keys.shape)
    other = jnp.where(here == (1 - half) * HDIM, guard, jnp.zeros_like(keys))
    return jnp.where(here // HDIM == half, keys, other)


def key_chunks(begin, rows, keys, causal):
    if not causal:
        return [(0, keys, False)]
    chunks = [(0, begin, False)] if begin else []
    return chunks + [(begin, rows, True)]


def pair_forward(q, k, v, guard, mix, logs, pair, keys_ref, values_t, causal):
    rows = q[0].shape[0]
    keys = k[0].shape[0]

    def columns(operand):
        return pl.ds(pl.multiple_of(operand[1] + pair * PAIR, PAIR), PAIR)

    key_all = k[0][:, columns(k)]
    values_t[...] = v[0][:, columns(v)].T
    for half in range(2):
        keys_ref[half] = key_all if guard is None else guarded_keys(key_all, guard[...], half)
    block = min(QUERY_BLOCK if causal else rows, rows)
    for begin in range(0, rows, block):
        scaled = q[0][begin : begin + block, columns(q)] * jnp.asarray(HDIM**-0.5, BF)
        queries = [head_queries(scaled, half, guard is not None) for half in range(2)]
        chunks = key_chunks(begin, block, keys, causal)
        scores = [[], []]
        for first, count, diagonal in chunks:
            for half in range(2):
                score = nt(keys_ref[half, first : first + count, :], queries[half])
                scores[half].append(causal_floor(score, first, begin) if diagonal else score)
        tops = []
        for half in range(2):
            top = jnp.max(scores[half][0], axis=0, keepdims=True)
            for score in scores[half][1:]:
                top = jnp.maximum(top, jnp.max(score, axis=0, keepdims=True))
            tops.append(top)
        mixed = []
        for half in range(2):
            total = None
            out = None
            for (first, count, _), score in zip(chunks, scores[half]):
                expd = jnp.exp(score - tops[half])
                part = jnp.sum(expd, axis=0, keepdims=True)
                value = values_t[half * HDIM : (half + 1) * HDIM, first : first + count]
                term = nn(value, expd.astype(BF))
                total = part if total is None else total + part
                out = term if out is None else out + term
            mixed.append(out * (1.0 / total))
            logs[pair, half : half + 1, begin : begin + block] = tops[half] + jnp.log(total)
        mix[0][begin : begin + block, columns(mix)] = jnp.concatenate(mixed, axis=0).T.astype(BF)


def pair_backward(q, k, v, guard, mix, grad_mix, logs, pair, keys_ref, sums, grads, causal):
    rows = q[0].shape[0]
    keys = k[0].shape[0]
    grad_key, grad_value = sums

    def columns(operand):
        return pl.ds(pl.multiple_of(operand[1] + pair * PAIR, PAIR), PAIR)

    key_all = k[0][:, columns(k)]
    for half in range(2):
        keys_ref[half] = key_all if guard is None else guarded_keys(key_all, guard[...], half)
    keys_t = key_all.T
    block = min(QUERY_BLOCK, rows)
    for begin in range(0, rows, block):
        here = slice(begin, begin + block)
        scaled = q[0][here, columns(q)] * jnp.asarray(HDIM**-0.5, BF)
        grad = grad_mix[0][here, columns(grad_mix)]
        weighed = (grad.astype(F32) * mix[0][here, columns(mix)].astype(F32)).T
        parts = []
        for half in range(2):
            own = lane(scaled.shape) // HDIM == half
            centre = jnp.sum(weighed[half * HDIM : (half + 1) * HDIM, :], axis=0, keepdims=True)
            parts.append(
                (
                    head_queries(scaled, half, guard is not None),
                    jnp.where(own, scaled, jnp.zeros_like(scaled)),
                    jnp.where(own, grad, jnp.zeros_like(grad)),
                    centre,
                    logs[pair, half : half + 1, here],
                )
            )
        grad_query = [None, None]
        for first, count, diagonal in key_chunks(begin, block, keys, causal):
            there = slice(first, first + count)
            value = v[0][there, columns(v)]
            raw = []
            for half in range(2):
                score = nt(keys_ref[half, there, :], parts[half][0])
                if diagonal:
                    score = causal_floor(score, first, begin)
                raw.append((score, nt(value, parts[half][2])))
            low = []
            for half in range(2):
                prob = jnp.exp(raw[half][0] - parts[half][4])
                grad_score = (prob * (raw[half][1] - parts[half][3])).astype(BF)
                low.append((prob.astype(BF), grad_score))
            add_value = nn(low[0][0], parts[0][2]) + nn(low[1][0], parts[1][2])
            add_key = nn(low[0][1], parts[0][1]) + nn(low[1][1], parts[1][1])
            fresh = diagonal if causal else begin == 0
            if fresh:
                grad_value[there, :] = add_value
                grad_key[there, :] = add_key
            else:
                grad_value[there, :] += add_value
                grad_key[there, :] += add_key
            for half in range(2):
                term = nn(keys_t[half * HDIM : (half + 1) * HDIM, there], low[half][1])
                grad_query[half] = term if grad_query[half] is None else grad_query[half] + term
        both = jnp.concatenate(grad_query, axis=0).T * HDIM**-0.5
        grads[0][0][here, columns(grads[0])] = both.astype(BF)
    grads[1][0][:, columns(grads[1])] = grad_key[...].astype(BF)
    grads[2][0][:, columns(grads[2])] = grad_value[...].astype(BF)


def row_loop(rows, body, begin_row=0):
    step = min(ROWS, rows)

    def turn(index, carry):
        body(pl.ds(pl.multiple_of(begin_row + index * step, step), step))
        return carry

    lax.fori_loop(0, rows // step, turn, 0, unroll=2)


def standardised(values):
    centred = values - jnp.mean(values, axis=-1, keepdims=True)
    scale = lax.rsqrt(jnp.mean(centred * centred, axis=-1, keepdims=True) + NORM_EPSILON)
    return centred * scale, scale


def norm_gradient(grad, gain, unit, scale):
    weighted = grad * gain
    return scale * (
        weighted
        - jnp.mean(weighted, axis=-1, keepdims=True)
        - unit * jnp.mean(weighted * unit, axis=-1, keepdims=True)
    )


def fold_rows(values):
    return jnp.sum(values.reshape(values.shape[0] // 8, 8, values.shape[1]), axis=0)


def wide(scale):
    return jnp.broadcast_to(scale, (scale.shape[0], 128))


class Moves:
    def __init__(self, semaphores):
        self.semaphores = semaphores
        self.count = 0
        self.open = []

    def start(self, source, target):
        copy = pltpu.make_async_copy(source, target, self.semaphores.at[self.count])
        self.count += 1
        copy.start()
        return copy

    def send(self, source, target):
        self.open.append(self.start(source, target))

    def finish(self):
        for copy in self.open:
            copy.wait()
        self.open = []


MESH_ID = pl.DeviceIdType.MESH


class Axis:
    def __init__(self, mesh_axis, stride, size):
        self.mesh_axis, self.stride, self.size = mesh_axis, stride, size

    def own(self):
        return lax.rem(lax.axis_index(self.mesh_axis) // self.stride, self.size)

    def peer(self, offset):
        own = self.own()
        there = lax.rem(own + offset, self.size)
        return there, {
            self.mesh_axis: lax.axis_index(self.mesh_axis) + (there - own) * self.stride
        }


class Grid:
    def __init__(self, groups, splits):
        if (groups, splits) == (8, 4):
            self.axes = {
                "z": Axis("dp", 2, 4),
                "x": Axis("dp", 1, 2),
                "y": Axis("tensor", 2, 2),
                "core": Axis("tensor", 1, 2),
            }
        elif (groups, splits) == (32, 4):
            self.axes = {
                "z": Axis("dp", 8, 4),
                "x": Axis("dp", 2, 4),
                "core": Axis("dp", 1, 2),
                "y": Axis("tensor", 1, 4),
            }
        else:
            raise ValueError("unknown mesh")
        self.orders = (("z", "x", "y", "core"), ("z", "y", "x", "core"))
        self.names = tuple(self.axes)
        self.dims = tuple(axis.size for axis in self.axes.values())
        self.copies = sum(axis.size - 1 for axis in self.axes.values())

    def greet(self):
        barrier = pltpu.get_barrier_semaphore()
        for axis in self.axes.values():
            for offset in range(1, axis.size):
                device = axis.peer(offset)[1]
                pl.semaphore_signal(barrier, inc=1, device_id=device, device_id_type=MESH_ID)

    def meet(self):
        pl.semaphore_wait(pltpu.get_barrier_semaphore(), self.copies)

    def places(self):
        for flat in range(math.prod(self.dims)):
            index = []
            rest = flat
            for size in reversed(self.dims):
                index.append(rest % size)
                rest //= size
            splits = math.prod(a.size for a in self.axes.values() if a.mesh_axis == "tensor")
            yield flat // splits, flat % splits, tuple(reversed(index))


class Links:
    def __init__(self, send_sems, recv_sems):
        self.send_sems, self.recv_sems = send_sems, recv_sems
        self.count = 0
        self.open = []

    def start(self, source, target, device):
        copy = pltpu.make_async_remote_copy(
            src_ref=source,
            dst_ref=target,
            send_sem=self.send_sems.at[self.count],
            recv_sem=self.recv_sems.at[self.count],
            device_id=device,
            device_id_type=MESH_ID,
        )
        self.count += 1
        copy.start()
        self.open.append(copy)
        return copy

    def finish(self):
        for copy in self.open:
            copy.wait_send()


class Gather:
    def __init__(self, grid, shards, outs, pairs, links, moves):
        self.grid, self.shards, self.outs, self.pairs = grid, shards, outs, pairs
        self.links, self.moves = links, moves
        self.sent = {}

    def region(self, order, phase, chunk):
        index = [
            slice(None) if name in order[:phase] else self.grid.axes[name].own()
            for name in self.grid.names
        ]
        return self.outs[chunk[0]].at[(*index, *chunk[1])]

    def send(self, pair, member, phase):
        chunk = self.pairs[pair][member]
        order = self.grid.orders[member % 2]
        axis = self.grid.axes[order[phase]]
        target = self.region(order, phase, chunk)
        source = self.shards[chunk[0]].at[chunk[1]] if phase == 0 else target
        self.sent[pair, member, phase] = [
            self.links.start(source, target, axis.peer(offset)[1]) for offset in range(1, axis.size)
        ]

    def begin(self):
        for pair, chunks in enumerate(self.pairs):
            for member in range(len(chunks)):
                self.send(pair, member, 0)
        own = tuple(axis.own() for axis in self.grid.axes.values())
        self.placed = [
            self.moves.start(shard, out.at[own]) for shard, out in zip(self.shards, self.outs)
        ]

    def place_own(self):
        for copy in self.placed:
            copy.wait()

    def advance(self, pair, phase):
        for member in range(len(self.pairs[pair])):
            for copy in self.sent[pair, member, phase - 1]:
                copy.wait_recv()
            if phase < 4:
                self.send(pair, member, phase)

    def run(self, steps):
        for pair, phase in steps:
            self.advance(pair, phase)


class Part:
    def __init__(self, blocks, index, arrivals, out, half=None):
        self.blocks, self.index, self.arrivals, self.out, self.half = blocks, index, arrivals, out, half


class Reduce:
    def __init__(self, grid, links, moves):
        self.grid, self.links, self.moves = grid, links, moves
        self.sent = {}
        self.loads = {}

    def order(self, member):
        return self.grid.orders[member % 2][::-1]

    def view(self, part, member, phase, coordinate):
        order = self.order(member)
        held = part.half is not None and phase >= 0
        index = []
        for name in self.grid.names:
            if held and name == order[0]:
                continue
            if phase >= 0 and name == order[phase]:
                index.append(coordinate)
            elif name in order[: max(phase, 0)]:
                index.append(self.grid.axes[name].own())
            else:
                index.append(slice(None))
        return (part.half if held else part.blocks).at[(*index, *part.index)]

    def outgoing(self, part, member, phase, coordinate):
        if phase == 0 and part.half is not None:
            order = self.order(member)
            index = [coordinate if n == order[0] else slice(None) for n in self.grid.names]
            return part.blocks.at[(*index, *part.index)]
        return self.view(part, member, phase, coordinate)

    def send(self, key, part, member, phase):
        axis = self.grid.axes[self.order(member)[phase]]
        copies = []
        for offset in range(1, axis.size):
            there, device = axis.peer(offset)
            source = self.outgoing(part, member, phase, there)
            copies.append(self.links.start(source, part.arrivals[phase].at[offset - 1], device))
        self.sent[key, phase] = copies

    def begin(self, pairs):
        for pair in pairs:
            for member, part in enumerate(pair):
                self.send(part, part, member, 0)
        for pair in pairs:
            for member, part in enumerate(pair):
                if part.half is not None:
                    own = self.grid.axes[self.order(member)[0]].own()
                    target = part.half.at[
                        (*[slice(None)] * (len(self.grid.names) - 1), *part.index)
                    ]
                    self.loads[part] = self.moves.start(
                        self.outgoing(part, member, 0, own), target
                    )

    def advance(self, pair, phase):
        for member, part in enumerate(pair):
            for copy in self.sent[part, phase]:
                copy.wait_recv()
            if phase == 0 and part.half is not None:
                self.loads[part].wait()
            self.add(part, member, phase)
            if phase < 3:
                self.send(part, part, member, phase + 1)

    def add(self, part, member, phase):
        own = self.grid.axes[self.order(member)[phase]].own()
        target = self.view(part, member, phase, own)
        came = part.arrivals[phase]
        if phase < 3 and came.shape[0] == 1:
            target[...] = target[...] + came[0]
            return
        total = target[...].astype(F32)
        for peer in range(came.shape[0]):
            total = total + came[peer].astype(F32)
        if phase == 3:
            part.out[...] = total
        else:
            target[...] = total.astype(target.dtype)

    def run(self, *steps):
        for pair, phase in steps:
            self.advance(pair, phase)


class Total:
    def __init__(self, grid, value, arrivals, links):
        self.grid, self.value, self.arrivals, self.links = grid, value, arrivals, links
        self.order = grid.orders[0][::-1]

    def send(self, phase):
        axis = self.grid.axes[self.order[phase]]
        self.sent = [
            self.links.start(self.value.at[phase], self.arrivals[phase].at[offset - 1], axis.peer(offset)[1])
            for offset in range(1, axis.size)
        ]

    def advance(self, phase):
        for copy in self.sent:
            copy.wait_recv()
        total = self.value[phase]
        for peer in range(self.arrivals[phase].shape[0]):
            total = total + self.arrivals[phase][peer]
        self.value[phase + 1] = total
        if phase < 3:
            self.send(phase + 1)


def arrival_shapes(grid, member, shard, dtype):
    order = grid.orders[member % 2][::-1]
    return [
        (
            (
                grid.axes[order[phase]].size - 1,
                *[a.size for n, a in grid.axes.items() if n not in order[: phase + 1]],
                *shard,
            ),
            dtype,
        )
        for phase in range(4)
    ]


ANY = pl.BlockSpec(memory_space=pl.ANY)
WHOLE = pl.BlockSpec(memory_space=pltpu.VMEM)
SCALAR = pl.BlockSpec(memory_space=pltpu.SMEM)


class Refs:
    def __init__(self, names, refs):
        for name, ref in zip(names, refs):
            setattr(self, name, ref)


def run_kernel(body, name, ins, outs, scratch, limit, flops, copies, remote=None, collective_id=None):
    names = [*ins, *outs, *scratch]
    semaphores = [pltpu.SemaphoreType.DMA((copies,)), pltpu.SemaphoreType.DMA((2,))]
    if remote is not None:
        semaphores += [pltpu.SemaphoreType.DMA((remote,))] * 2
    moved = sum(math.prod(s) * jnp.dtype(d).itemsize for s, d, _ in outs.values())
    moved += sum(a.size * a.dtype.itemsize for a, _ in ins.values())

    def kernel(*refs):
        body(Refs([*names, "sems"], [*refs[: len(names)], refs[len(names) :]]))

    results = pl.pallas_call(
        kernel,
        name=name,
        in_specs=[spec for _, spec in ins.values()],
        out_specs=[spec for _, _, spec in outs.values()],
        out_shape=[jax.ShapeDtypeStruct(s, d) for s, d, _ in outs.values()],
        scratch_shapes=[pltpu.VMEM(s, d) for s, d in scratch.values()] + semaphores,
        compiler_params=pltpu.CompilerParams(
            vmem_limit_bytes=limit,
            collective_id=collective_id,
            has_side_effects=remote is not None,
        ),
        cost_estimate=pl.CostEstimate(flops=flops, bytes_accessed=moved, transcendentals=0),
    )(*[array for array, _ in ins.values()])
    return Refs(list(outs), results)


def fetch_weights(grid, blocks, weights, semaphore, first, slots, to=0):
    rows, cols = blocks.shape[-2:]
    target = weights.at[pl.ds(to, slots)]
    for group, split, index in grid.places():
        pltpu.make_async_copy(
            blocks.at[(*index, pl.ds(first, slots))],
            target.at[:, pl.ds(group * rows, rows), pl.ds(split * cols, cols)],
            semaphore,
        ).start()
    return pltpu.make_async_copy(target, target, semaphore)


def store_blocks(grid, blocks, slot, grad, first_split=0):
    rows, cols = blocks.shape[-2:]
    low = grad.astype(BF)
    for group, split, index in grid.places():
        begin = (split - first_split) * cols
        if 0 <= begin < low.shape[1]:
            blocks[(*index, slot)] = low[group * rows : (group + 1) * rows, begin : begin + cols]


def forward(grid, r):
    grid.greet()
    moves = Moves(r.sems[0])
    column = lax.axis_index("tensor")
    rows_all, width = r.low.shape
    keys = r.guard.shape[0]
    masters = [
        moves.start(r.attention_master, r.attention_float),
        moves.start(r.feed_master, r.feed_float),
    ]
    x_here = moves.start(r.inputs.at[pl.ds(pl.multiple_of(column * rows_all, rows_all), rows_all)], r.mix_one)
    memory_here = moves.start(r.memory.at[pl.ds(pl.multiple_of(column * keys, keys), keys)], r.mix_two)
    cotangent_here = moves.start(
        r.cotangent_in.at[pl.ds(pl.multiple_of(column * rows_all, rows_all), rows_all)], r.cotangent
    )
    own_rows = r.norm_master.shape[1]
    slots = r.norm_master.shape[0]
    spot = lax.broadcasted_iota(jnp.int32, (own_rows, width), 1)
    spot_row = lax.broadcasted_iota(jnp.int32, (own_rows, width), 0) + lax.axis_index("dp") * own_rows
    spread = jnp.where(spot == spot_row, 1.0, 0.0).astype(BF)
    r.norm_shard[...] = jnp.zeros_like(r.norm_shard)
    r.norm_shard[0:slots, :] = nn(r.norm_master[...].astype(BF), spread).astype(BF)
    for copy in masters:
        copy.wait()
    r.attention_shard[...] = r.attention_float[...].astype(BF)
    r.feed_shard[...] = r.feed_float[...].astype(BF)
    attention_pairs = [[(0, (2 * p,)), (0, (2 * p + 1,))] for p in range(4)]
    attention_pairs[1].append((2, ()))
    quarter = r.feed_shard.shape[2] // 4
    feed_chunks = [
        (1, (slot, slice(None), slice(q * quarter, (q + 1) * quarter))) for slot in range(2) for q in range(4)
    ]
    feed_pairs = [feed_chunks[2 * p : 2 * p + 2] for p in range(4)]
    links = Links(r.sems[2], r.sems[3])
    gather = Gather(
        grid,
        (r.attention_shard, r.feed_shard, r.norm_shard),
        (r.attention, r.feed, r.norm_blocks),
        attention_pairs + feed_pairs,
        links,
        moves,
    )
    grid.meet()
    gather.begin()
    blocks = r.owner_list.shape[0]
    block_rows = width // blocks
    for block in range(blocks):
        here = lax.broadcasted_iota(jnp.int32, (block_rows, width), 1)
        there = lax.broadcasted_iota(jnp.int32, (block_rows, width), 0) + r.owner_list[block] * block_rows
        r.place[block * block_rows : (block + 1) * block_rows, :] = jnp.where(here == there, 1.0, 0.0).astype(BF)
    moves.send(r.place, r.place_out)
    gather.place_own()
    gather.run([(0, 1), (1, 1)])
    x_here.wait()
    r.low[...] = nn(r.mix_one[...], r.place[...]).astype(BF)
    moves.send(r.low, r.low_out)
    gather.run([(0, 2), (1, 2)])
    memory_here.wait()
    r.wide_two[:, 3 * width :] = nn(r.mix_two[...], r.place[...]).astype(BF)
    moves.send(r.wide_two.at[:, pl.ds(3 * width, width)], r.memory_low_out)
    mask = r.key_mask[pl.ds(column, 1), :]
    first = lax.broadcasted_iota(jnp.int32, (1, keys), 1) == 0
    bias = jnp.where((mask == 1) | first, 0.0, FLOOR_SCORE)
    r.guard[...] = jnp.broadcast_to(bias, (PAIR, keys)).T.astype(BF)
    moves.send(r.guard, r.guard_out)
    gather.run([(2, 1), (0, 3), (0, 4), (3, 1), (1, 3), (5, 1), (2, 2), (1, 4)])
    self_weights = fetch_weights(grid, r.attention, r.weights, r.sems[1].at[0], 0, 4)
    norm_here = moves.start(r.norm_blocks, r.norm_all)
    self_weights.wait()
    for part in range(3):
        r.wide_one[:, part * width : (part + 1) * width] = nn(r.low[...], r.weights[part]).astype(BF)
    moves.send(r.wide_one.at[:, pl.ds(0, 3 * width)], r.qkv_out)
    gather.run([(3, 2)])
    steps = [[(4, 1), (6, 1)], [(7, 1), (2, 3)], [(2, 4), (3, 3)], [(4, 2), (3, 4)]]
    for pair in range(width // PAIR):
        pair_forward(
            (r.wide_one, 0), (r.wide_one, width), (r.wide_one, 2 * width), None, (r.mix_one, 0), r.logs_one, pair,
            r.keys_ref, r.values_t, True,
        )
        gather.run(steps[pair])
    moves.send(r.mix_one, r.mix_one_out)
    moves.send(r.logs_one, r.logs_one_out)
    r.unit_one[...] = nt(r.mix_one[...], r.weights[3])
    cross_weights = fetch_weights(grid, r.attention, r.weights, r.sems[1].at[1], 4, 4, 4)
    norm_here.wait()
    total = jnp.zeros((8, width), F32)
    for group, split, index in grid.places():
        if split == 0:
            total = total + r.norm_all[index][0:8, :].astype(F32)
    r.norms[...] = total

    def first_rows(rows):
        unit_rows, scale_rows = standardised(r.low[rows, :].astype(F32) + r.unit_one[rows, :])
        r.unit_one[rows, :] = unit_rows
        r.scale_one[rows, :] = wide(scale_rows)
        r.wide_two[rows, 2 * width : 3 * width] = (unit_rows * r.norms[0:1, :] + r.norms[1:2, :]).astype(BF)

    row_loop(rows_all, first_rows)
    moves.send(r.unit_one, r.unit_one_out)
    moves.send(r.scale_one, r.scale_one_out)
    gather.run([(6, 2), (5, 2)])
    cross_weights.wait()
    r.wide_one[:, 3 * width :] = nn(r.wide_two[:, 2 * width : 3 * width], r.weights[4]).astype(BF)
    moves.send(r.wide_one.at[:, pl.ds(3 * width, width)], r.query_out)
    for part in range(2):
        r.wide_two[:, part * width : (part + 1) * width] = nn(r.wide_two[:, 3 * width :], r.weights[5 + part]).astype(BF)
    moves.send(r.wide_two.at[:, pl.ds(0, 2 * width)], r.key_value_out)
    steps = [[(4, 3)], [(7, 2), (4, 4)], [(5, 3)], [(6, 3), (5, 4)]]
    for pair in range(width // PAIR):
        pair_forward(
            (r.wide_one, 3 * width), (r.wide_two, 0), (r.wide_two, width), r.guard, (r.mix_two, 0), r.logs_two, pair,
            r.keys_ref, r.values_t, False,
        )
        gather.run(steps[pair])
        if pair == 3:
            up_weights = fetch_weights(grid, r.feed, r.feed_weights, r.sems[1].at[0], 0, 1)
    moves.send(r.mix_two, r.mix_two_out)
    moves.send(r.logs_two, r.logs_two_out)
    r.unit_two[...] = nt(r.mix_two[...], r.weights[7])
    gather.run([(7, 3)])
    moves.finish()

    def second_rows(rows):
        second_sum = r.unit_one[rows, :] * r.norms[0:1, :] + r.norms[1:2, :] + r.unit_two[rows, :]
        unit_rows, scale_rows = standardised(second_sum)
        r.unit_two[rows, :] = unit_rows
        r.scale_two[rows, :] = wide(scale_rows)
        r.mix_one[rows, :] = (unit_rows * r.norms[2:3, :] + r.norms[3:4, :]).astype(BF)

    row_loop(rows_all, second_rows)
    gather.run([(6, 4), (7, 4)])
    down_weights = fetch_weights(grid, r.feed, r.feed_weights, r.sems[1].at[1], 1, 1, 1)
    up_weights.wait()
    down_weights.wait()
    cotangent_here.wait()
    feed_both(grid, r, moves, r.lengths[column])
    links.finish()
    moves.finish()


def gelu_both(values):
    half = 0.5 * (1.0 + lax.erf(values * (0.5**0.5)))
    bell = jnp.exp(-0.5 * values * values) * (0.5 / math.pi) ** 0.5
    return values * half, half + values * bell


def feed_both(grid, r, moves, length):
    rows_all, width = r.low.shape
    weights, unit, scale, norms = r.feed_weights, r.unit_two, r.scale_two, r.norms
    second_low, third_low, active, inner_grad = r.mix_one, r.mix_two, r.wide_one, r.wide_two
    grad_third = r.unit_one
    hidden = weights.shape[2]
    chunk = min(width, hidden)
    r.sums[...] = jnp.zeros_like(r.sums)

    def second_of(rows):
        return unit[rows, :] * norms[2:3, :] + norms[3:4, :]

    tile_rows = min(FEED_ROWS, rows_all)

    def tile(index, carry):
        begin = pl.multiple_of(index * tile_rows, tile_rows)
        here = pl.ds(begin, tile_rows)
        cot = nn(r.cotangent[here, :], r.place[...])
        for begin_col in range(0, hidden, chunk):
            cols = slice(begin_col, begin_col + chunk)
            value, slope_part = gelu_both(nn(second_low[here, :], weights[0, :, cols]))
            active[here, cols] = value.astype(BF)
            r.slope[:, cols] = slope_part
        fed = nt(active[here, :], weights[1])
        for part in range(0, tile_rows, ROWS):
            rows = pl.ds(pl.multiple_of(begin + part, ROWS), ROWS)
            place_rows = lax.broadcasted_iota(jnp.int32, (ROWS, 1), 0) + (begin + part)
            live = jnp.where(place_rows < length, 1.0, 0.0)
            third_sum = second_of(rows) + fed[part : part + ROWS, :] + r.low[rows, :].astype(F32)
            unit_rows, scale_rows = standardised(third_sum)
            third = live * (unit_rows * norms[4:5, :] + norms[5:6, :])
            r.output[rows, :] = third.astype(BF)
            grad = live * cot[part : part + ROWS, :]
            grad_rows = norm_gradient(grad, norms[4:5, :], unit_rows, scale_rows)
            grad_third[rows, :] = grad_rows
            third_low[rows, :] = grad_rows.astype(BF)
            r.sums[2] += fold_rows(grad * unit_rows)
            r.sums[3] += fold_rows(grad)
        for begin_col in range(0, hidden, chunk):
            cols = slice(begin_col, begin_col + chunk)
            back = nn(third_low[here, :], weights[1, :, cols]) * r.slope[:, cols]
            inner_grad[here, cols] = back.astype(BF)
        fed_back = nt(inner_grad[here, :], weights[0])
        for part in range(0, tile_rows, ROWS):
            rows = pl.ds(pl.multiple_of(begin + part, ROWS), ROWS)
            unit_rows = unit[rows, :]
            grad = fed_back[part : part + ROWS, :] + grad_third[rows, :]
            r.grad_second[rows, :] = norm_gradient(grad, norms[2:3, :], unit_rows, scale[rows, 0:1])
            r.sums[0] += fold_rows(grad * unit_rows)
            r.sums[1] += fold_rows(grad)
        return carry

    lax.fori_loop(0, rows_all // tile_rows, tile, 0)
    moves.send(r.output, r.output_out)
    moves.send(grad_third, r.grad_third_out)
    moves.send(r.grad_second, r.grad_second_out)
    r.norm_grads[...] = jnp.sum(r.sums[...], axis=1)
    cols_one = r.grads.shape[-1]
    for split in range(hidden // cols_one):
        cols = slice(split * cols_one, (split + 1) * cols_one)
        store_blocks(grid, r.grads, 0, tn(second_low[...], inner_grad[:, cols]), split)
        store_blocks(grid, r.grads, 1, tn(third_low[...], active[:, cols]), split)
    moves.send(r.grads, r.grads_out)


def backward(grid, names, r):
    grid.greet()
    moves = Moves(r.sems[0])
    links = Links(r.sems[2], r.sems[3])
    rows_all, width = r.mix.shape
    quarter = r.feed_grads.shape[-1] // 4

    def arrived(member, phases):
        return [getattr(r, name) for name in phases]

    feed_pairs = []
    for p in range(4):
        pair = []
        for member in range(2):
            slot, q = divmod(2 * p + member, 4)
            cols = slice(q * quarter, (q + 1) * quarter)
            pair.append(
                Part(
                    r.feed_grads, (slot, slice(None), cols), arrived(member, names["feed", p, member]),
                    r.feed_sum.at[slot, :, cols], r.feed_half,
                )
            )
        feed_pairs.append(pair)

    def attention_pairs(kind, blocks, first):
        return [
            [
                Part(
                    blocks, (2 * p + member,), arrived(member, names[kind, p, member]),
                    r.attention_sum.at[first + 2 * p + member],
                )
                for member in range(2)
            ]
            for p in range(2)
        ]

    cross_pairs = attention_pairs("cross", r.cross_grads, 4)
    self_pairs = attention_pairs("self", r.self_grads, 0)
    c1, c0 = cross_pairs
    c2 = [self_pairs[1].pop()]
    reduce = Reduce(grid, links, moves)
    start = moves.start(r.grad_second_in, r.grad_second)
    gathered = fetch_weights(grid, r.attention, r.weights, r.sems[1].at[0], 4, 4, 4)
    stage = [
        moves.start(r.mix_two_in, r.mix),
        moves.start(r.query_in, r.qkv.at[:, pl.ds(0, width)]),
        moves.start(r.key_value_in, r.qkv.at[:, pl.ds(width, 2 * width)]),
        moves.start(r.logs_two_in, r.logs),
        moves.start(r.guard_in, r.guard),
    ]
    late = [
        moves.start(r.memory_low_in, r.memory_low),
        moves.start(r.unit_in, r.unit),
        moves.start(r.scale_in, r.scale),
    ]
    self_weights = fetch_weights(grid, r.attention, r.weights, r.sems[1].at[1], 0, 4, 0)
    start.wait()

    def lower(rows):
        r.grad_low[rows, :] = r.grad_second[rows, :].astype(BF)

    row_loop(rows_all, lower)
    grid.meet()
    reduce.begin(feed_pairs)
    gathered.wait()
    for copy in stage:
        copy.wait()
    r.grad_mix[...] = nn(r.grad_low[...], r.weights[7]).astype(BF)
    store_blocks(grid, r.cross_grads, 3, tn(r.grad_low[...], r.mix[...]))
    f0, f1, f2, f3 = feed_pairs
    reduce.run((f0, 0), (f1, 0))
    steps = [
        [(f0, 1), (f2, 0)],
        [(f0, 2), (f1, 1), (f3, 0)],
        [(f1, 2), (f2, 1), (f0, 3)],
        [(f2, 2), (f3, 1), (f1, 3)],
    ]
    for pair in range(width // PAIR):
        pair_backward(
            (r.qkv, 0), (r.qkv, width), (r.qkv, 2 * width), r.guard, (r.mix, 0), (r.grad_mix, 0), r.logs, pair,
            r.keys_ref, (r.key_sum, r.value_sum), ((r.qkv_grad, 0), (r.qkv_grad, width), (r.qkv_grad, 2 * width)),
            False,
        )
        reduce.run(*steps[pair])
    stage = [
        moves.start(r.mix_one_in, r.mix),
        moves.start(r.qkv_in, r.qkv),
        moves.start(r.logs_one_in, r.logs),
        moves.start(r.low_in, r.low),
    ]
    for copy in late:
        copy.wait()
    store_blocks(grid, r.cross_grads, 2, tn(r.memory_low[...], r.qkv_grad[:, 2 * width :]))
    reduce.begin([c0])
    store_blocks(grid, r.cross_grads, 1, tn(r.memory_low[...], r.qkv_grad[:, width : 2 * width]))
    r.key_value_grad[...] = r.qkv_grad[:, width:]
    r.grad_first[...] = nt(r.qkv_grad[:, :width], r.weights[4])
    reduce.run((f3, 2), (f2, 3))
    r.sums[...] = jnp.zeros_like(r.sums)
    norms = r.norms

    def back(rows):
        unit_rows = r.unit[rows, :]
        grad = r.grad_first[rows, :] + r.grad_second[rows, :]
        r.first_low[rows, :] = (unit_rows * norms[0:1, :] + norms[1:2, :]).astype(BF)
        grad_rows = norm_gradient(grad, norms[0:1, :], unit_rows, r.scale[rows, 0:1])
        r.grad_first[rows, :] = grad_rows
        r.grad_low[rows, :] = grad_rows.astype(BF)
        r.sums[0] += fold_rows(grad * unit_rows)
        r.sums[1] += fold_rows(grad)

    row_loop(rows_all, back)
    third = moves.start(r.grad_third_in, r.unit)
    r.norm_value[0] = jnp.concatenate(
        [jnp.sum(r.sums[...], axis=1), r.feed_norms[...], jnp.zeros((2, width), F32)], axis=0
    )
    total = Total(grid, r.norm_value, [getattr(r, name) for name in names["norm"]], links)
    total.send(0)
    reduce.run((c0, 0), (f3, 3))
    store_blocks(grid, r.cross_grads, 0, tn(r.first_low[...], r.qkv_grad[:, :width]))
    reduce.begin([c1])

    self_weights.wait()
    for copy in stage:
        copy.wait()
    r.grad_mix[...] = nn(r.grad_low[...], r.weights[3]).astype(BF)
    store_blocks(grid, r.self_grads, 3, tn(r.grad_low[...], r.mix[...]))
    reduce.begin([c2])
    steps = [
        [(c0, 1), (c1, 0)],
        [(c0, 2), (c2, 0)],
        [(c1, 1), (c0, 3)],
        [(c1, 2), (c2, 1)],
    ]
    for pair in range(width // PAIR):
        pair_backward(
            (r.qkv, 0), (r.qkv, width), (r.qkv, 2 * width), None, (r.mix, 0), (r.grad_mix, 0), r.logs, pair,
            r.keys_ref, (r.key_sum, r.value_sum), ((r.qkv_grad, 0), (r.qkv_grad, width), (r.qkv_grad, 2 * width)),
            True,
        )
        total.advance(pair)
        reduce.run(*steps[pair])
    s0, s1 = self_pairs
    for part in range(3):
        grad = tn(r.low[...], r.qkv_grad[:, part * width : (part + 1) * width])
        store_blocks(grid, r.self_grads, part, grad)
        if part == 1:
            reduce.begin([s0])
    reduce.begin([s1])
    reduce.run((s0, 0), (c2, 2))
    third.wait()
    back_input = r.grad_first[...] + r.unit[...]
    back_input = back_input + nt(r.qkv_grad[:, :width], r.weights[0])
    reduce.run((s1, 0))
    back_input = back_input + nt(r.qkv_grad[:, width : 2 * width], r.weights[1])
    back_input = back_input + nt(r.qkv_grad[:, 2 * width :], r.weights[2])
    r.input_low[...] = back_input.astype(BF)
    moves.send(r.input_low, r.grad_input_out)
    reduce.run((s0, 1))
    back_memory = nt(r.key_value_grad[:, :width], r.weights[5])
    reduce.run((s1, 1))
    back_memory = back_memory + nt(r.key_value_grad[:, width:], r.weights[6])
    r.outgoing[...] = back_memory.astype(BF)
    moves.send(r.outgoing, r.grad_memory_out)
    reduce.run((c1, 3), (c2, 3), (s0, 2), (s1, 2), (s0, 3), (s1, 3))
    r.norm_sum[...] = r.norm_value[4]
    links.finish()
    moves.finish()


def run_layer(
    inputs, memory, cotangent, lengths, key_mask, owner_list, attention_master, feed_master, norm_master, groups, splits
):
    grid = Grid(groups, splits)
    width = inputs.shape[1]
    rows = inputs.shape[0] // splits
    keys = memory.shape[0] // splits
    own_rows = attention_master.shape[1]
    attention_t, feed_t = attention_master.shape, feed_master.shape
    hidden = splits * feed_t[2]
    if rows != keys or hidden != 4 * width:
        raise ValueError("unexpected sizes")
    pairs = width // PAIR
    low_t, full_t, keys_low_t = ((rows, width), BF), ((rows, width), F32), ((keys, width), BF)
    scale_t, logs_t, place_t = ((rows, 128), F32), ((pairs, 2, rows), F32), ((width, width), BF)
    qkv_t, key_value_t = ((rows, 3 * width), BF), ((keys, 2 * width), BF)
    guard_t, halves_t, norm_t = ((keys, PAIR), BF), ((2, keys, PAIR), BF), ((8, width), F32)
    eight_t = ((8, width, width), BF)
    attention_blocks, feed_blocks = (*grid.dims, *attention_t), (*grid.dims, *feed_t)
    norm_shard_t = ((16, width), BF)
    pair_flops = 2 * rows * keys * width
    dense = 2 * rows * width * width

    def hbm(item):
        return (*item, ANY)

    f = run_kernel(
        functools.partial(forward, grid),
        "forward",
        {
            "inputs": (inputs, ANY),
            "memory": (memory, ANY),
            "key_mask": (key_mask, WHOLE),
            "owner_list": (owner_list, SCALAR),
            "attention_master": (attention_master, ANY),
            "feed_master": (feed_master, ANY),
            "norm_master": (norm_master, WHOLE),
            "cotangent_in": (cotangent, ANY),
            "lengths": (lengths, SCALAR),
        },
        {
            "attention": (attention_blocks, BF, ANY),
            "feed": (feed_blocks, BF, ANY),
            "norm_blocks": ((*grid.dims, *norm_shard_t[0]), BF, ANY),
            "place_out": hbm(place_t),
            "guard_out": hbm(guard_t),
            "low_out": hbm(low_t),
            "memory_low_out": hbm(keys_low_t),
            "qkv_out": hbm(qkv_t),
            "mix_one_out": hbm(low_t),
            "logs_one_out": hbm(logs_t),
            "unit_one_out": hbm(full_t),
            "scale_one_out": hbm(scale_t),
            "query_out": hbm(low_t),
            "key_value_out": hbm(key_value_t),
            "mix_two_out": hbm(low_t),
            "logs_two_out": hbm(logs_t),
            "norms": (*norm_t, WHOLE),
            "output_out": hbm(low_t),
            "grad_third_out": hbm(full_t),
            "grad_second_out": hbm(full_t),
            "grads_out": (feed_blocks, BF, ANY),
            "norm_grads": ((4, width), F32, WHOLE),
        },
        {
            "attention_float": (attention_t, F32),
            "feed_float": (feed_t, F32),
            "attention_shard": (attention_t, BF),
            "feed_shard": (feed_t, BF),
            "norm_shard": norm_shard_t,
            "norm_all": ((*grid.dims, *norm_shard_t[0]), BF),
            "place": place_t,
            "guard": guard_t,
            "low": low_t,
            "weights": eight_t,
            "wide_one": ((rows, hidden), BF),
            "wide_two": ((rows, hidden), BF),
            "mix_one": low_t,
            "logs_one": logs_t,
            "unit_one": full_t,
            "scale_one": scale_t,
            "mix_two": low_t,
            "logs_two": logs_t,
            "unit_two": full_t,
            "scale_two": scale_t,
            "keys_ref": halves_t,
            "values_t": ((PAIR, keys), BF),
            "cotangent": low_t,
            "feed_weights": ((2, width, hidden), BF),
            "slope": ((min(FEED_ROWS, rows), hidden), F32),
            "output": low_t,
            "grad_second": full_t,
            "grads": (feed_blocks, BF),
            "sums": ((4, 8, width), F32),
        },
        61 << 20,
        12 * dense + 14 * pair_flops + 12 * rows * width * hidden,
        32,
        17 * grid.copies,
        0,
    )

    scratch = {
        "grad_second": full_t,
        "mix": low_t,
        "weights": eight_t,
        "qkv": qkv_t,
        "logs": logs_t,
        "guard": guard_t,
        "memory_low": keys_low_t,
        "low": low_t,
        "unit": full_t,
        "scale": scale_t,
        "grad_low": low_t,
        "key_value_grad": key_value_t,
        "grad_mix": low_t,
        "qkv_grad": qkv_t,
        "first_low": low_t,
        "outgoing": keys_low_t,
        "input_low": low_t,
        "grad_first": full_t,
        "cross_grads": ((*grid.dims, 4, *attention_t[1:]), BF),
        "self_grads": ((*grid.dims, 4, *attention_t[1:]), BF),
        "feed_half": ((*[a.size for n, a in grid.axes.items() if n != "core"], *feed_t), BF),
        "sums": ((2, 8, width), F32),
        "norm_value": ((5, 8, width), F32),
        "keys_ref": halves_t,
        "key_sum": ((keys, PAIR), F32),
        "value_sum": ((keys, PAIR), F32),
    }
    names = {}
    kinds = [("feed", p, m, (feed_t[1], feed_t[2] // 4)) for p in range(4) for m in range(2)]
    kinds += [
        (kind, p, m, attention_t[1:]) for kind in ("cross", "self") for p in range(2) for m in range(2)
    ]
    for kind, p, m, shard in kinds:
        names[kind, p, m] = []
        parity = 0 if (kind, p) == ("self", 1) else m
        for phase, shape in enumerate(arrival_shapes(grid, parity, shard, BF)):
            name = f"{kind}{p}{m}{phase}"
            scratch[name] = shape
            names[kind, p, m].append(name)
    names["norm"] = []
    for phase, axis in enumerate(grid.orders[0][::-1]):
        scratch[f"norm{phase}"] = ((grid.axes[axis].size - 1, 8, width), F32)
        names["norm"].append(f"norm{phase}")
    b = run_kernel(
        functools.partial(backward, grid, names),
        "backward",
        {
            "grad_second_in": (f.grad_second_out, ANY),
            "mix_two_in": (f.mix_two_out, ANY),
            "attention": (f.attention, ANY),
            "query_in": (f.query_out, ANY),
            "key_value_in": (f.key_value_out, ANY),
            "logs_two_in": (f.logs_two_out, ANY),
            "guard_in": (f.guard_out, ANY),
            "memory_low_in": (f.memory_low_out, ANY),
            "unit_in": (f.unit_one_out, ANY),
            "scale_in": (f.scale_one_out, ANY),
            "mix_one_in": (f.mix_one_out, ANY),
            "qkv_in": (f.qkv_out, ANY),
            "logs_one_in": (f.logs_one_out, ANY),
            "low_in": (f.low_out, ANY),
            "grad_third_in": (f.grad_third_out, ANY),
            "feed_grads": (f.grads_out, ANY),
            "norms": (f.norms, WHOLE),
            "feed_norms": (f.norm_grads, WHOLE),
        },
        {
            "grad_memory_out": hbm(keys_low_t),
            "grad_input_out": hbm(low_t),
            "attention_sum": (attention_t, F32, WHOLE),
            "feed_sum": (feed_t, F32, WHOLE),
            "norm_sum": (*norm_t, WHOLE),
        },
        scratch,
        61 << 20,
        18 * dense + 35 * pair_flops,
        40,
        17 * grid.copies,
        1,
    )
    return f.output_out, b.grad_input_out, b.grad_memory_out, b.attention_sum, b.feed_sum, b.norm_sum, f.place_out


def adam_moments(rotated, moment, second):
    moment_new = BETA_FIRST * moment + (1.0 - BETA_FIRST) * rotated
    second_new = BETA_SECOND * second + (1.0 - BETA_SECOND) * rotated * rotated
    direction = (
        moment_new
        / (1.0 - BETA_FIRST**STEP)
        / (jnp.sqrt(second_new / (1.0 - BETA_SECOND**STEP)) + ADAM_EPSILON)
    )
    return (moment_new, second_new, direction)


def finish(weight, average, update, rate, decay):
    weight_new = weight - rate * (update + decay * weight)
    average_new = AVERAGE_DECAY * average + (1.0 - AVERAGE_DECAY) * weight_new
    return (weight_new, average_new, weight_new.astype(jnp.bfloat16))


def split(values):
    high = values.astype(BF)
    return high, (values - high.astype(F32)).astype(BF)


def rotate(values, basis, back):
    times = nt if back else nn
    rows = values[0].shape[0]
    top = times(jnp.concatenate(values, axis=0), basis[0])
    return top[:rows] + top[rows:] + times(values[0], basis[1])


STATES = ("grad", "master", "moment", "second", "average", "basis")
RESULTS = ("moment", "second", "weight", "average", "copy")


def update(r):
    moves = Moves(r.sems[0])
    lead = [
        (moves.start(r.place_in, r.place), moves.start(r.output_in, r.output)),
        (moves.start(r.grad_input_in, r.grad_input),),
        (moves.start(r.grad_memory_in, r.grad_memory),),
    ]
    loads = {
        (kind, name): moves.start(getattr(r, f"{kind}_{name}_in"), getattr(r, f"{kind}_{name}"))
        for kind in ("attention", "feed")
        for name in STATES
    }
    for copies, low, out in zip(
        lead,
        (r.output, r.grad_input, r.grad_memory),
        (r.output_out, r.grad_input_out, r.grad_memory_out),
    ):
        for copy in copies:
            copy.wait()
        low[...] = nt(low[...], r.place[...]).astype(BF)
        moves.send(low, out)
    for kind, rate in (("attention", RATE_ATTENTION), ("feed", RATE_FEED)):
        for name in STATES:
            loads[kind, name].wait()
        grad, master, moment, second, average, basis = (getattr(r, f"{kind}_{n}") for n in STATES)
        low = getattr(r, f"{kind}_copy")
        for slot in range(grad.shape[0]):
            turn = split(basis[slot])
            rotated = rotate(split(grad[slot]), turn, False)
            moment[slot], second[slot], direction = adam_moments(rotated, moment[slot], second[slot])
            master[slot], average[slot], low[slot] = finish(
                master[slot], average[slot], rotate(split(direction), turn, True), rate, WEIGHT_DECAY
            )
        for name, ref in zip(RESULTS, (moment, second, master, average, low)):
            moves.send(ref, getattr(r, f"{kind}_{name}_out"))
    slots, own_rows = r.norm_master_in.shape
    piece = r.norm_moment_out.shape[1]

    def own(values, first):
        shape = (values.shape[1], 128)
        here = lax.broadcasted_iota(jnp.int32, shape, 0)
        there = lax.broadcasted_iota(jnp.int32, shape, 1)
        select = jnp.where(here == there + first, 1.0, 0.0)
        picked = lax.dot_general(
            values, select, (((1,), (0,)), ((), ())), precision=HIGHEST, preferred_element_type=F32
        )
        return picked[:slots, :piece]

    begin = lax.axis_index("tensor") * piece
    grad = own(r.norm_sum[...], lax.axis_index("dp") * own_rows + begin)
    master, moment, second, average = (
        own(ref[...], begin)
        for ref in (r.norm_master_in, r.norm_moment_in, r.norm_second_in, r.norm_average_in)
    )
    moment, second, direction = adam_moments(grad, moment, second)
    results = (moment, second, *finish(master, average, direction, RATE_NORMS, 0.0))
    for name, value in zip(RESULTS, results):
        getattr(r, f"norm_{name}_out")[...] = value
    moves.finish()


def run_update(output, grad_input, grad_memory, place, norm_sum, states):
    ins = {
        "output_in": (output, ANY),
        "grad_input_in": (grad_input, ANY),
        "grad_memory_in": (grad_memory, ANY),
        "place_in": (place, ANY),
        "norm_sum": (norm_sum, WHOLE),
    }
    outs = {
        "output_out": (output.shape, BF, ANY),
        "grad_input_out": (grad_input.shape, BF, ANY),
        "grad_memory_out": (grad_memory.shape, BF, ANY),
    }
    scratch = {
        "place": (place.shape, BF),
        "output": (output.shape, BF),
        "grad_input": (grad_input.shape, BF),
        "grad_memory": (grad_memory.shape, BF),
    }
    for kind in ("attention", "feed"):
        shape = states[kind]["grad"].shape
        for name in STATES:
            ins[f"{kind}_{name}_in"] = (states[kind][name], ANY)
            scratch[f"{kind}_{name}"] = (states[kind][name].shape, F32)
        scratch[f"{kind}_copy"] = (shape, BF)
        for name in RESULTS:
            outs[f"{kind}_{name}_out"] = (shape, BF if name == "copy" else F32, ANY)
    for name, array in states["norm"].items():
        ins[f"norm_{name}_in"] = (array, WHOLE)
    slots, own_rows = states["norm"]["master"].shape
    for name in RESULTS:
        shape = (slots, own_rows // lax.axis_size("tensor"))
        outs[f"norm_{name}_out"] = (shape, BF if name == "copy" else F32, WHOLE)
    return run_kernel(update, "update", ins, outs, scratch, 60 << 20, 1 << 31, 32)


def on_device(
    inputs,
    memory,
    cotangent,
    lengths,
    key_mask,
    owner_list,
    attention_master,
    attention_moment,
    attention_second,
    attention_average,
    attention_basis,
    feed_master,
    feed_moment,
    feed_second,
    feed_average,
    feed_basis,
    norm_master,
    norm_moment,
    norm_second,
    norm_average,
):
    groups = lax.axis_size("dp")
    splits = lax.axis_size("tensor")
    output, grad_input, grad_memory, attention_grad, feed_grad, norm_sum, place = run_layer(
        inputs,
        memory,
        cotangent,
        lengths,
        key_mask,
        owner_list,
        attention_master,
        feed_master,
        norm_master,
        groups,
        splits,
    )
    u = run_update(
        output,
        grad_input,
        grad_memory,
        place,
        norm_sum,
        {
            "attention": dict(
                grad=attention_grad,
                master=attention_master,
                moment=attention_moment,
                second=attention_second,
                average=attention_average,
                basis=attention_basis,
            ),
            "feed": dict(
                grad=feed_grad,
                master=feed_master,
                moment=feed_moment,
                second=feed_second,
                average=feed_average,
                basis=feed_basis,
            ),
            "norm": dict(
                master=norm_master, moment=norm_moment, second=norm_second, average=norm_average
            ),
        },
    )
    results = [
        getattr(u, f"{kind}_{name}_out") for kind in ("attention", "feed", "norm") for name in RESULTS
    ]
    return (u.output_out, u.grad_input_out, u.grad_memory_out, *results)


def solution(mesh):
    in_specs = (
        P("dp", None),
        P("dp", None),
        P("dp", None),
        P("dp"),
        P("dp", None),
        P(),
        P(None, "dp", "tensor"),
        P(None, "dp", "tensor"),
        P(None, "dp", "tensor"),
        P(None, "dp", "tensor"),
        P(None, "tensor", None),
        P(None, "dp", "tensor"),
        P(None, "dp", "tensor"),
        P(None, "dp", "tensor"),
        P(None, "dp", "tensor"),
        P(None, "tensor", None),
        P(None, "dp"),
        P(None, "dp"),
        P(None, "dp"),
        P(None, "dp"),
    )
    out_specs = (
        P(("dp", "tensor"), None),
        P(("dp", "tensor"), None),
        P(("dp", "tensor"), None),
        P(None, "dp", "tensor"),
        P(None, "dp", "tensor"),
        P(None, "dp", "tensor"),
        P(None, "dp", "tensor"),
        P(None, "dp", "tensor"),
        P(None, "dp", "tensor"),
        P(None, "dp", "tensor"),
        P(None, "dp", "tensor"),
        P(None, "dp", "tensor"),
        P(None, "dp", "tensor"),
        P(None, ("dp", "tensor")),
        P(None, ("dp", "tensor")),
        P(None, ("dp", "tensor")),
        P(None, ("dp", "tensor")),
        P(None, ("dp", "tensor")),
    )
    return jax.shard_map(
        on_device, mesh=mesh, in_specs=in_specs, out_specs=out_specs, check_vma=False
    )
```

```python
import functools
import math

import jax
import jax.numpy as jnp
from jax import lax
from jax.experimental import pallas as pl
from jax.experimental.pallas import tpu as pltpu
from jax.sharding import PartitionSpec as P

HDIM = 64
STEP = 10


FLOOR_SCORE = -1e30
NORM_EPSILON = 1e-05
BETA_FIRST = 0.9
BETA_SECOND = 0.95
ADAM_EPSILON = 1e-08
AVERAGE_DECAY = 0.6
RATE_ATTENTION = 0.07
RATE_FEED = 0.03
RATE_NORMS = 0.5
WEIGHT_DECAY = 0.01
HIGHEST = lax.Precision.HIGHEST


BF = jnp.bfloat16
F32 = jnp.float32
PAIR = 2 * HDIM
QUERY_BLOCK = 512
ROWS = 128
BACK_ROWS = 64
FEED_ROWS = 512


def nn(left, right):
    return lax.dot_general(left, right, (((1,), (0,)), ((), ())), preferred_element_type=F32)


def nt(left, right):
    return lax.dot_general(left, right, (((1,), (1,)), ((), ())), preferred_element_type=F32)


def tn(left, right):
    return lax.dot_general(left, right, (((0,), (0,)), ((), ())), preferred_element_type=F32)


def lane(shape):
    return lax.broadcasted_iota(jnp.int32, shape, 1)


def causal_floor(scores, key_begin, query_begin):
    key = lax.broadcasted_iota(jnp.int32, scores.shape, 0) + key_begin
    query = lax.broadcasted_iota(jnp.int32, scores.shape, 1) + query_begin
    return jnp.where(key <= query, scores, FLOOR_SCORE)


def head_queries(scaled, half, guarded):
    here = lane(scaled.shape)
    other = jnp.zeros_like(scaled)
    if guarded:
        other = jnp.where(here == (1 - half) * HDIM, jnp.ones_like(scaled), other)
    return jnp.where(here // HDIM == half, scaled, other)


def guarded_keys(keys, guard, half):
    here = lane(keys.shape)
    other = jnp.where(here == (1 - half) * HDIM, guard, jnp.zeros_like(keys))
    return jnp.where(here // HDIM == half, keys, other)


def key_chunks(begin, rows, keys, causal):
    if not causal:
        return [(0, keys, False)]
    chunks = [(0, begin, False)] if begin else []
    return chunks + [(begin, rows, True)]


def pair_forward(q, k, v, guard, mix, logs, pair, keys_ref, values_t, causal):
    rows = q[0].shape[0]
    keys = k[0].shape[0]

    def columns(operand):
        return pl.ds(pl.multiple_of(operand[1] + pair * PAIR, PAIR), PAIR)

    key_all = k[0][:, columns(k)]
    values_t[...] = v[0][:, columns(v)].T
    for half in range(2):
        keys_ref[half] = key_all if guard is None else guarded_keys(key_all, guard[...], half)
    block = min(QUERY_BLOCK if causal else rows, rows)
    for begin in range(0, rows, block):
        scaled = q[0][begin : begin + block, columns(q)] * jnp.asarray(HDIM**-0.5, BF)
        queries = [head_queries(scaled, half, guard is not None) for half in range(2)]
        chunks = key_chunks(begin, block, keys, causal)
        scores = [[], []]
        for first, count, diagonal in chunks:
            for half in range(2):
                score = nt(keys_ref[half, first : first + count, :], queries[half])
                scores[half].append(causal_floor(score, first, begin) if diagonal else score)
        tops = []
        for half in range(2):
            top = jnp.max(scores[half][0], axis=0, keepdims=True)
            for score in scores[half][1:]:
                top = jnp.maximum(top, jnp.max(score, axis=0, keepdims=True))
            tops.append(top)
        mixed = []
        for half in range(2):
            total = None
            out = None
            for (first, count, _), score in zip(chunks, scores[half]):
                expd = jnp.exp(score - tops[half])
                part = jnp.sum(expd, axis=0, keepdims=True)
                value = values_t[half * HDIM : (half + 1) * HDIM, first : first + count]
                term = nn(value, expd.astype(BF))
                total = part if total is None else total + part
                out = term if out is None else out + term
            mixed.append(out * (1.0 / total))
            logs[pair, half : half + 1, begin : begin + block] = tops[half] + jnp.log(total)
        mix[0][begin : begin + block, columns(mix)] = jnp.concatenate(mixed, axis=0).T.astype(BF)


def pair_backward(q, k, v, guard, mix, grad_mix, logs, pair, keys_ref, sums, grads, causal):
    rows = q[0].shape[0]
    keys = k[0].shape[0]
    grad_key, grad_value = sums

    def columns(operand):
        return pl.ds(pl.multiple_of(operand[1] + pair * PAIR, PAIR), PAIR)

    key_all = k[0][:, columns(k)]
    for half in range(2):
        keys_ref[half] = key_all if guard is None else guarded_keys(key_all, guard[...], half)
    keys_t = key_all.T
    block = min(QUERY_BLOCK, rows)
    for begin in range(0, rows, block):
        here = slice(begin, begin + block)
        scaled = q[0][here, columns(q)] * jnp.asarray(HDIM**-0.5, BF)
        grad = grad_mix[0][here, columns(grad_mix)]
        weighed = (grad.astype(F32) * mix[0][here, columns(mix)].astype(F32)).T
        parts = []
        for half in range(2):
            own = lane(scaled.shape) // HDIM == half
            centre = jnp.sum(weighed[half * HDIM : (half + 1) * HDIM, :], axis=0, keepdims=True)
            parts.append(
                (
                    head_queries(scaled, half, guard is not None),
                    jnp.where(own, scaled, jnp.zeros_like(scaled)),
                    jnp.where(own, grad, jnp.zeros_like(grad)),
                    centre,
                    logs[pair, half : half + 1, here],
                )
            )
        grad_query = [None, None]
        for first, count, diagonal in key_chunks(begin, block, keys, causal):
            there = slice(first, first + count)
            value = v[0][there, columns(v)]
            raw = []
            for half in range(2):
                score = nt(keys_ref[half, there, :], parts[half][0])
                if diagonal:
                    score = causal_floor(score, first, begin)
                raw.append((score, nt(value, parts[half][2])))
            low = []
            for half in range(2):
                prob = jnp.exp(raw[half][0] - parts[half][4])
                grad_score = (prob * (raw[half][1] - parts[half][3])).astype(BF)
                low.append((prob.astype(BF), grad_score))
            add_value = nn(low[0][0], parts[0][2]) + nn(low[1][0], parts[1][2])
            add_key = nn(low[0][1], parts[0][1]) + nn(low[1][1], parts[1][1])
            fresh = diagonal if causal else begin == 0
            if fresh:
                grad_value[there, :] = add_value
                grad_key[there, :] = add_key
            else:
                grad_value[there, :] += add_value
                grad_key[there, :] += add_key
            for half in range(2):
                term = nn(keys_t[half * HDIM : (half + 1) * HDIM, there], low[half][1])
                grad_query[half] = term if grad_query[half] is None else grad_query[half] + term
        both = jnp.concatenate(grad_query, axis=0).T * HDIM**-0.5
        grads[0][0][here, columns(grads[0])] = both.astype(BF)
    grads[1][0][:, columns(grads[1])] = grad_key[...].astype(BF)
    grads[2][0][:, columns(grads[2])] = grad_value[...].astype(BF)


def row_loop(rows, body, step=ROWS):
    def turn(index, carry):
        body(pl.ds(pl.multiple_of(index * step, step), step))
        return carry

    lax.fori_loop(0, rows // step, turn, 0, unroll=2)


def standardised(values):
    centred = values - jnp.mean(values, axis=-1, keepdims=True)
    scale = lax.rsqrt(jnp.mean(centred * centred, axis=-1, keepdims=True) + NORM_EPSILON)
    return centred * scale, scale


def norm_gradient(grad, gain, unit, scale):
    weighted = grad * gain
    return scale * (
        weighted
        - jnp.mean(weighted, axis=-1, keepdims=True)
        - unit * jnp.mean(weighted * unit, axis=-1, keepdims=True)
    )


def fold_rows(values):
    return jnp.sum(values.reshape(values.shape[0] // 8, 8, values.shape[1]), axis=0)


def wide(scale):
    return jnp.broadcast_to(scale, (scale.shape[0], 128))


class Moves:
    def __init__(self, semaphores):
        self.semaphores = semaphores
        self.count = 0
        self.open = []

    def start(self, source, target):
        copy = pltpu.make_async_copy(source, target, self.semaphores.at[self.count])
        self.count += 1
        copy.start()
        return copy

    def send(self, source, target):
        self.open.append(self.start(source, target))

    def finish(self):
        for copy in self.open:
            copy.wait()
        self.open = []


MESH_ID = pl.DeviceIdType.MESH


class Axis:
    def __init__(self, mesh_axis, stride, size):
        self.mesh_axis, self.stride, self.size = mesh_axis, stride, size

    def own(self):
        return lax.rem(lax.axis_index(self.mesh_axis) // self.stride, self.size)

    def peer(self, offset):
        own = self.own()
        there = lax.rem(own + offset, self.size)
        return there, {
            self.mesh_axis: lax.axis_index(self.mesh_axis) + (there - own) * self.stride
        }


class Grid:
    def __init__(self, groups, splits):
        if (groups, splits) == (8, 4):
            self.axes = {
                "z": Axis("dp", 2, 4),
                "x": Axis("dp", 1, 2),
                "y": Axis("tensor", 2, 2),
                "core": Axis("tensor", 1, 2),
            }
        elif (groups, splits) == (32, 4):
            self.axes = {
                "z": Axis("dp", 8, 4),
                "x": Axis("dp", 2, 4),
                "core": Axis("dp", 1, 2),
                "y": Axis("tensor", 1, 4),
            }
        else:
            raise ValueError("unknown mesh")
        self.orders = (("z", "x", "y", "core"), ("z", "y", "x", "core"))
        self.names = tuple(self.axes)
        self.dims = tuple(axis.size for axis in self.axes.values())
        self.copies = sum(axis.size - 1 for axis in self.axes.values())

    def greet(self):
        barrier = pltpu.get_barrier_semaphore()
        for axis in self.axes.values():
            for offset in range(1, axis.size):
                device = axis.peer(offset)[1]
                pl.semaphore_signal(barrier, inc=1, device_id=device, device_id_type=MESH_ID)

    def meet(self):
        pl.semaphore_wait(pltpu.get_barrier_semaphore(), self.copies)

    def places(self):
        for flat in range(math.prod(self.dims)):
            index = []
            rest = flat
            for size in reversed(self.dims):
                index.append(rest % size)
                rest //= size
            splits = math.prod(a.size for a in self.axes.values() if a.mesh_axis == "tensor")
            yield flat // splits, flat % splits, tuple(reversed(index))


class Links:
    def __init__(self, send_sems, recv_sems):
        self.send_sems, self.recv_sems = send_sems, recv_sems
        self.count = 0
        self.open = []

    def start(self, source, target, device):
        copy = pltpu.make_async_remote_copy(
            src_ref=source,
            dst_ref=target,
            send_sem=self.send_sems.at[self.count],
            recv_sem=self.recv_sems.at[self.count],
            device_id=device,
            device_id_type=MESH_ID,
        )
        self.count += 1
        copy.start()
        self.open.append(copy)
        return copy

    def finish(self):
        for copy in self.open:
            copy.wait_send()


class Gather:
    def __init__(self, grid, shards, outs, pairs, links, moves):
        self.grid, self.shards, self.outs, self.pairs = grid, shards, outs, pairs
        self.links, self.moves = links, moves
        self.sent = {}

    def region(self, order, phase, chunk):
        index = [
            slice(None) if name in order[:phase] else self.grid.axes[name].own()
            for name in self.grid.names
        ]
        return self.outs[chunk[0]].at[(*index, *chunk[1])]

    def send(self, pair, member, phase):
        chunk = self.pairs[pair][member]
        order = self.grid.orders[member % 2]
        axis = self.grid.axes[order[phase]]
        target = self.region(order, phase, chunk)
        source = self.shards[chunk[0]].at[chunk[1]] if phase == 0 else target
        self.sent[pair, member, phase] = [
            self.links.start(source, target, axis.peer(offset)[1]) for offset in range(1, axis.size)
        ]

    def begin(self):
        for pair, chunks in enumerate(self.pairs):
            for member in range(len(chunks)):
                self.send(pair, member, 0)
        own = tuple(axis.own() for axis in self.grid.axes.values())
        self.placed = [
            self.moves.start(shard, out.at[own]) for shard, out in zip(self.shards, self.outs)
        ]

    def place_own(self):
        for copy in self.placed:
            copy.wait()

    def advance(self, pair, phase):
        for member in range(len(self.pairs[pair])):
            for copy in self.sent[pair, member, phase - 1]:
                copy.wait_recv()
            if phase < 4:
                self.send(pair, member, phase)

    def run(self, steps):
        for pair, phase in steps:
            self.advance(pair, phase)


class Part:
    def __init__(self, blocks, index, arrivals, out, half=None):
        self.blocks, self.index, self.arrivals, self.out, self.half = blocks, index, arrivals, out, half


class Reduce:
    def __init__(self, grid, links, moves):
        self.grid, self.links, self.moves = grid, links, moves
        self.sent = {}
        self.loads = {}

    def order(self, member):
        return self.grid.orders[member % 2][::-1]

    def view(self, part, member, phase, coordinate):
        order = self.order(member)
        held = part.half is not None and phase >= 0
        index = []
        for name in self.grid.names:
            if held and name == order[0]:
                continue
            if phase >= 0 and name == order[phase]:
                index.append(coordinate)
            elif name in order[: max(phase, 0)]:
                index.append(self.grid.axes[name].own())
            else:
                index.append(slice(None))
        return (part.half if held else part.blocks).at[(*index, *part.index)]

    def outgoing(self, part, member, phase, coordinate):
        if phase == 0 and part.half is not None:
            order = self.order(member)
            index = [coordinate if n == order[0] else slice(None) for n in self.grid.names]
            return part.blocks.at[(*index, *part.index)]
        return self.view(part, member, phase, coordinate)

    def send(self, key, part, member, phase):
        axis = self.grid.axes[self.order(member)[phase]]
        copies = []
        for offset in range(1, axis.size):
            there, device = axis.peer(offset)
            source = self.outgoing(part, member, phase, there)
            copies.append(self.links.start(source, part.arrivals[phase].at[offset - 1], device))
        self.sent[key, phase] = copies

    def begin(self, pairs):
        for pair in pairs:
            for member, part in enumerate(pair):
                self.send(part, part, member, 0)
        for pair in pairs:
            for member, part in enumerate(pair):
                if part.half is not None:
                    own = self.grid.axes[self.order(member)[0]].own()
                    target = part.half.at[
                        (*[slice(None)] * (len(self.grid.names) - 1), *part.index)
                    ]
                    self.loads[part] = self.moves.start(
                        self.outgoing(part, member, 0, own), target
                    )

    def advance(self, pair, phase):
        for member, part in enumerate(pair):
            for copy in self.sent[part, phase]:
                copy.wait_recv()
            if phase == 0 and part.half is not None:
                self.loads[part].wait()
            self.add(part, member, phase)
            if phase < 3:
                self.send(part, part, member, phase + 1)

    def add(self, part, member, phase):
        own = self.grid.axes[self.order(member)[phase]].own()
        target = self.view(part, member, phase, own)
        came = part.arrivals[phase]
        if phase < 3 and came.shape[0] == 1:
            target[...] = target[...] + came[0]
            return
        total = target[...].astype(F32)
        for peer in range(came.shape[0]):
            total = total + came[peer].astype(F32)
        if phase == 3:
            part.out[...] = total
        else:
            target[...] = total.astype(target.dtype)

    def run(self, *steps):
        for pair, phase in steps:
            self.advance(pair, phase)


class Total:
    def __init__(self, grid, value, arrivals, links):
        self.grid, self.value, self.arrivals, self.links = grid, value, arrivals, links
        self.order = grid.orders[0][::-1]

    def send(self, phase):
        axis = self.grid.axes[self.order[phase]]
        self.sent = [
            self.links.start(self.value.at[phase], self.arrivals[phase].at[offset - 1], axis.peer(offset)[1])
            for offset in range(1, axis.size)
        ]

    def advance(self, phase):
        for copy in self.sent:
            copy.wait_recv()
        total = self.value[phase]
        for peer in range(self.arrivals[phase].shape[0]):
            total = total + self.arrivals[phase][peer]
        self.value[phase + 1] = total
        if phase < 3:
            self.send(phase + 1)


def arrival_shapes(grid, member, shard, dtype):
    order = grid.orders[member % 2][::-1]
    return [
        (
            (
                grid.axes[order[phase]].size - 1,
                *[a.size for n, a in grid.axes.items() if n not in order[: phase + 1]],
                *shard,
            ),
            dtype,
        )
        for phase in range(4)
    ]


ANY = pl.BlockSpec(memory_space=pl.ANY)
WHOLE = pl.BlockSpec(memory_space=pltpu.VMEM)
SCALAR = pl.BlockSpec(memory_space=pltpu.SMEM)


class Refs:
    def __init__(self, names, refs):
        for name, ref in zip(names, refs):
            setattr(self, name, ref)


def run_kernel(body, name, ins, outs, scratch, limit, flops, copies, remote=None, collective_id=None):
    names = [*ins, *outs, *scratch]
    semaphores = [pltpu.SemaphoreType.DMA((copies,)), pltpu.SemaphoreType.DMA((2,))]
    if remote is not None:
        semaphores += [pltpu.SemaphoreType.DMA((remote,))] * 2
    moved = sum(math.prod(s) * jnp.dtype(d).itemsize for s, d, _ in outs.values())
    moved += sum(a.size * a.dtype.itemsize for a, _ in ins.values())

    def kernel(*refs):
        body(Refs([*names, "sems"], [*refs[: len(names)], refs[len(names) :]]))

    results = pl.pallas_call(
        kernel,
        name=name,
        in_specs=[spec for _, spec in ins.values()],
        out_specs=[spec for _, _, spec in outs.values()],
        out_shape=[jax.ShapeDtypeStruct(s, d) for s, d, _ in outs.values()],
        scratch_shapes=[pltpu.VMEM(s, d) for s, d in scratch.values()] + semaphores,
        compiler_params=pltpu.CompilerParams(
            vmem_limit_bytes=limit,
            collective_id=collective_id,
            has_side_effects=remote is not None,
        ),
        cost_estimate=pl.CostEstimate(flops=flops, bytes_accessed=moved, transcendentals=0),
    )(*[array for array, _ in ins.values()])
    return Refs(list(outs), results)


def fetch_weights(grid, blocks, weights, semaphore, first, slots, to=0):
    rows, cols = blocks.shape[-2:]
    target = weights.at[pl.ds(to, slots)]
    for group, split, index in grid.places():
        pltpu.make_async_copy(
            blocks.at[(*index, pl.ds(first, slots))],
            target.at[:, pl.ds(group * rows, rows), pl.ds(split * cols, cols)],
            semaphore,
        ).start()
    return pltpu.make_async_copy(target, target, semaphore)


def store_blocks(grid, blocks, slot, grad, first_split=0):
    rows, cols = blocks.shape[-2:]
    low = grad.astype(BF)
    for group, split, index in grid.places():
        begin = (split - first_split) * cols
        if 0 <= begin < low.shape[1]:
            blocks[(*index, slot)] = low[group * rows : (group + 1) * rows, begin : begin + cols]


def forward(grid, r):
    grid.greet()
    moves = Moves(r.sems[0])
    column = lax.axis_index("tensor")
    rows_all, width = r.low.shape
    keys = r.guard.shape[0]
    masters = [
        moves.start(r.attention_master, r.attention_float),
        moves.start(r.feed_master, r.feed_float),
    ]
    x_here = moves.start(r.inputs.at[pl.ds(pl.multiple_of(column * rows_all, rows_all), rows_all)], r.mix_one)
    memory_here = moves.start(r.memory.at[pl.ds(pl.multiple_of(column * keys, keys), keys)], r.mix_two)
    cotangent_here = moves.start(
        r.cotangent_in.at[pl.ds(pl.multiple_of(column * rows_all, rows_all), rows_all)], r.cotangent
    )
    own_rows = r.norm_master.shape[1]
    slots = r.norm_master.shape[0]
    spot = lax.broadcasted_iota(jnp.int32, (own_rows, width), 1)
    spot_row = lax.broadcasted_iota(jnp.int32, (own_rows, width), 0) + lax.axis_index("dp") * own_rows
    spread = jnp.where(spot == spot_row, 1.0, 0.0).astype(BF)
    r.norm_shard[...] = jnp.zeros_like(r.norm_shard)
    r.norm_shard[0:slots, :] = nn(r.norm_master[...].astype(BF), spread).astype(BF)
    for copy in masters:
        copy.wait()
    r.attention_shard[...] = r.attention_float[...].astype(BF)
    r.feed_shard[...] = r.feed_float[...].astype(BF)
    attention_pairs = [[(0, (2 * p,)), (0, (2 * p + 1,))] for p in range(4)]
    attention_pairs[1].append((2, ()))
    quarter = r.feed_shard.shape[2] // 4
    feed_chunks = [
        (1, (slot, slice(None), slice(q * quarter, (q + 1) * quarter))) for slot in range(2) for q in range(4)
    ]
    feed_pairs = [feed_chunks[2 * p : 2 * p + 2] for p in range(4)]
    links = Links(r.sems[2], r.sems[3])
    gather = Gather(
        grid,
        (r.attention_shard, r.feed_shard, r.norm_shard),
        (r.attention, r.feed, r.norm_blocks),
        attention_pairs + feed_pairs,
        links,
        moves,
    )
    grid.meet()
    gather.begin()
    blocks = r.owner_list.shape[0]
    block_rows = width // blocks
    for block in range(blocks):
        here = lax.broadcasted_iota(jnp.int32, (block_rows, width), 1)
        there = lax.broadcasted_iota(jnp.int32, (block_rows, width), 0) + r.owner_list[block] * block_rows
        r.place[block * block_rows : (block + 1) * block_rows, :] = jnp.where(here == there, 1.0, 0.0).astype(BF)
    moves.send(r.place, r.place_out)
    gather.place_own()
    gather.run([(0, 1), (1, 1)])
    x_here.wait()
    r.low[...] = nn(r.mix_one[...], r.place[...]).astype(BF)
    moves.send(r.low, r.low_out)
    gather.run([(0, 2), (1, 2)])
    memory_here.wait()
    r.wide_two[:, 3 * width :] = nn(r.mix_two[...], r.place[...]).astype(BF)
    moves.send(r.wide_two.at[:, pl.ds(3 * width, width)], r.memory_low_out)
    mask = r.key_mask[pl.ds(column, 1), :]
    first = lax.broadcasted_iota(jnp.int32, (1, keys), 1) == 0
    bias = jnp.where((mask == 1) | first, 0.0, FLOOR_SCORE)
    r.guard[...] = jnp.broadcast_to(bias, (PAIR, keys)).T.astype(BF)
    moves.send(r.guard, r.guard_out)
    gather.run([(2, 1), (0, 3), (0, 4), (3, 1), (1, 3), (5, 1), (2, 2), (1, 4)])
    self_weights = fetch_weights(grid, r.attention, r.weights, r.sems[1].at[0], 0, 4)
    norm_here = moves.start(r.norm_blocks, r.norm_all)
    self_weights.wait()
    for part in range(3):
        r.wide_one[:, part * width : (part + 1) * width] = nn(r.low[...], r.weights[part]).astype(BF)
    moves.send(r.wide_one.at[:, pl.ds(0, 3 * width)], r.qkv_out)
    gather.run([(3, 2)])
    steps = [[(4, 1), (6, 1)], [(7, 1), (2, 3)], [(2, 4), (3, 3)], [(4, 2), (3, 4)]]
    for pair in range(width // PAIR):
        pair_forward(
            (r.wide_one, 0), (r.wide_one, width), (r.wide_one, 2 * width), None, (r.mix_one, 0), r.logs_one, pair,
            r.keys_ref, r.values_t, True,
        )
        gather.run(steps[pair])
    moves.send(r.mix_one, r.mix_one_out)
    moves.send(r.logs_one, r.logs_one_out)
    r.unit_one[...] = nt(r.mix_one[...], r.weights[3])
    cross_weights = fetch_weights(grid, r.attention, r.weights, r.sems[1].at[1], 4, 4, 4)
    norm_here.wait()
    total = jnp.zeros((8, width), F32)
    for group, split, index in grid.places():
        if split == 0:
            total = total + r.norm_all[index][0:8, :].astype(F32)
    r.norms[...] = total

    def first_rows(rows):
        unit_rows, scale_rows = standardised(r.low[rows, :].astype(F32) + r.unit_one[rows, :])
        r.unit_one[rows, :] = unit_rows
        r.scale_one[rows, :] = wide(scale_rows)
        r.wide_two[rows, 2 * width : 3 * width] = (unit_rows * r.norms[0:1, :] + r.norms[1:2, :]).astype(BF)

    row_loop(rows_all, first_rows)
    moves.send(r.unit_one, r.unit_one_out)
    moves.send(r.scale_one, r.scale_one_out)
    gather.run([(6, 2), (5, 2)])
    cross_weights.wait()
    r.wide_one[:, 3 * width :] = nn(r.wide_two[:, 2 * width : 3 * width], r.weights[4]).astype(BF)
    moves.send(r.wide_one.at[:, pl.ds(3 * width, width)], r.query_out)
    for part in range(2):
        r.wide_two[:, part * width : (part + 1) * width] = nn(r.wide_two[:, 3 * width :], r.weights[5 + part]).astype(BF)
    moves.send(r.wide_two.at[:, pl.ds(0, 2 * width)], r.key_value_out)
    steps = [[(4, 3)], [(7, 2), (4, 4)], [(5, 3)], [(6, 3), (5, 4)]]
    for pair in range(width // PAIR):
        pair_forward(
            (r.wide_one, 3 * width), (r.wide_two, 0), (r.wide_two, width), r.guard, (r.mix_two, 0), r.logs_two, pair,
            r.keys_ref, r.values_t, False,
        )
        gather.run(steps[pair])
        if pair == 3:
            up_weights = fetch_weights(grid, r.feed, r.feed_weights, r.sems[1].at[0], 0, 1)
    moves.send(r.mix_two, r.mix_two_out)
    moves.send(r.logs_two, r.logs_two_out)
    r.unit_two[...] = nt(r.mix_two[...], r.weights[7])
    gather.run([(7, 3)])
    moves.finish()

    def second_rows(rows):
        second_sum = r.unit_one[rows, :] * r.norms[0:1, :] + r.norms[1:2, :] + r.unit_two[rows, :]
        unit_rows, scale_rows = standardised(second_sum)
        r.unit_two[rows, :] = unit_rows
        r.scale_two[rows, :] = wide(scale_rows)
        r.mix_one[rows, :] = (unit_rows * r.norms[2:3, :] + r.norms[3:4, :]).astype(BF)

    row_loop(rows_all, second_rows)
    gather.run([(6, 4), (7, 4)])
    down_weights = fetch_weights(grid, r.feed, r.feed_weights, r.sems[1].at[1], 1, 1, 1)
    up_weights.wait()
    down_weights.wait()
    cotangent_here.wait()
    feed_both(grid, r, moves, r.lengths[column])
    links.finish()
    moves.finish()


def gelu_both(values):
    half = 0.5 * (1.0 + lax.erf(values * (0.5**0.5)))
    bell = jnp.exp(-0.5 * values * values) * (0.5 / math.pi) ** 0.5
    return values * half, half + values * bell


def feed_both(grid, r, moves, length):
    rows_all, width = r.low.shape
    weights, unit, scale, norms = r.feed_weights, r.unit_two, r.scale_two, r.norms
    second_low, third_low, active, inner_grad = r.mix_one, r.mix_two, r.wide_one, r.wide_two
    grad_third = r.unit_one
    hidden = weights.shape[2]
    chunk = min(width, hidden)
    r.sums[...] = jnp.zeros_like(r.sums)

    def second_of(rows):
        return unit[rows, :] * norms[2:3, :] + norms[3:4, :]

    tile_rows = min(FEED_ROWS, rows_all)

    def tile(index, carry):
        begin = pl.multiple_of(index * tile_rows, tile_rows)
        here = pl.ds(begin, tile_rows)
        cot = nn(r.cotangent[here, :], r.place[...])
        for begin_col in range(0, hidden, chunk):
            cols = slice(begin_col, begin_col + chunk)
            value, slope_part = gelu_both(nn(second_low[here, :], weights[0, :, cols]))
            active[here, cols] = value.astype(BF)
            r.slope[:, cols] = slope_part
        fed = nt(active[here, :], weights[1])
        for part in range(0, tile_rows, ROWS):
            rows = pl.ds(pl.multiple_of(begin + part, ROWS), ROWS)
            place_rows = lax.broadcasted_iota(jnp.int32, (ROWS, 1), 0) + (begin + part)
            live = jnp.where(place_rows < length, 1.0, 0.0)
            third_sum = second_of(rows) + fed[part : part + ROWS, :] + r.low[rows, :].astype(F32)
            unit_rows, scale_rows = standardised(third_sum)
            third = live * (unit_rows * norms[4:5, :] + norms[5:6, :])
            r.output[rows, :] = third.astype(BF)
            grad = live * cot[part : part + ROWS, :]
            grad_rows = norm_gradient(grad, norms[4:5, :], unit_rows, scale_rows)
            grad_third[rows, :] = grad_rows
            third_low[rows, :] = grad_rows.astype(BF)
            r.sums[2] += fold_rows(grad * unit_rows)
            r.sums[3] += fold_rows(grad)
        for begin_col in range(0, hidden, chunk):
            cols = slice(begin_col, begin_col + chunk)
            back = nn(third_low[here, :], weights[1, :, cols]) * r.slope[:, cols]
            inner_grad[here, cols] = back.astype(BF)
        fed_back = nt(inner_grad[here, :], weights[0])
        for part in range(0, tile_rows, ROWS):
            rows = pl.ds(pl.multiple_of(begin + part, ROWS), ROWS)
            unit_rows = unit[rows, :]
            grad = fed_back[part : part + ROWS, :] + grad_third[rows, :]
            r.grad_second[rows, :] = norm_gradient(grad, norms[2:3, :], unit_rows, scale[rows, 0:1])
            r.sums[0] += fold_rows(grad * unit_rows)
            r.sums[1] += fold_rows(grad)
        return carry

    lax.fori_loop(0, rows_all // tile_rows, tile, 0)
    moves.send(r.output, r.output_out)
    moves.send(grad_third, r.grad_third_out)
    moves.send(r.grad_second, r.grad_second_out)
    r.norm_grads[...] = jnp.sum(r.sums[...], axis=1)
    cols_one = r.grads.shape[-1]
    for split in range(hidden // cols_one):
        cols = slice(split * cols_one, (split + 1) * cols_one)
        store_blocks(grid, r.grads, 0, tn(second_low[...], inner_grad[:, cols]), split)
        store_blocks(grid, r.grads, 1, tn(third_low[...], active[:, cols]), split)
    moves.send(r.grads, r.grads_out)


def backward(grid, names, r):
    grid.greet()
    moves = Moves(r.sems[0])
    links = Links(r.sems[2], r.sems[3])
    rows_all, width = r.mix.shape
    quarter = r.feed_grads.shape[-1] // 4

    def arrived(member, phases):
        return [getattr(r, name) for name in phases]

    feed_pairs = []
    for p in range(4):
        pair = []
        for member in range(2):
            slot, q = divmod(2 * p + member, 4)
            cols = slice(q * quarter, (q + 1) * quarter)
            pair.append(
                Part(
                    r.feed_grads, (slot, slice(None), cols), arrived(member, names["feed", p, member]),
                    r.feed_sum.at[slot, :, cols], r.feed_half,
                )
            )
        feed_pairs.append(pair)

    def attention_pairs(kind, blocks, first):
        return [
            [
                Part(
                    blocks, (2 * p + member,), arrived(member, names[kind, p, member]),
                    r.attention_sum.at[first + 2 * p + member],
                )
                for member in range(2)
            ]
            for p in range(2)
        ]

    cross_pairs = attention_pairs("cross", r.cross_grads, 4)
    self_pairs = attention_pairs("self", r.self_grads, 0)
    c1, c0 = cross_pairs
    c2 = [self_pairs[1].pop()]
    reduce = Reduce(grid, links, moves)
    start = moves.start(r.grad_second_in, r.grad_second)
    gathered = fetch_weights(grid, r.attention, r.weights, r.sems[1].at[0], 4, 4, 4)
    stage = [
        moves.start(r.mix_two_in, r.mix),
        moves.start(r.query_in, r.qkv.at[:, pl.ds(0, width)]),
        moves.start(r.key_value_in, r.qkv.at[:, pl.ds(width, 2 * width)]),
        moves.start(r.logs_two_in, r.logs),
        moves.start(r.guard_in, r.guard),
    ]
    late = [
        moves.start(r.memory_low_in, r.memory_low),
        moves.start(r.unit_in, r.unit),
        moves.start(r.scale_in, r.scale),
    ]
    self_weights = fetch_weights(grid, r.attention, r.weights, r.sems[1].at[1], 0, 4, 0)
    start.wait()

    def lower(rows):
        r.grad_low[rows, :] = r.grad_second[rows, :].astype(BF)

    row_loop(rows_all, lower, BACK_ROWS)
    grid.meet()
    reduce.begin(feed_pairs)
    gathered.wait()
    for copy in stage:
        copy.wait()
    r.grad_mix[...] = nn(r.grad_low[...], r.weights[7]).astype(BF)
    store_blocks(grid, r.cross_grads, 3, tn(r.grad_low[...], r.mix[...]))
    f0, f1, f2, f3 = feed_pairs
    reduce.run((f0, 0), (f1, 0))
    steps = [
        [(f0, 1), (f2, 0)],
        [(f0, 2), (f1, 1), (f3, 0)],
        [(f1, 2), (f2, 1), (f0, 3)],
        [(f2, 2), (f3, 1), (f1, 3)],
    ]
    for pair in range(width // PAIR):
        pair_backward(
            (r.qkv, 0), (r.qkv, width), (r.qkv, 2 * width), r.guard, (r.mix, 0), (r.grad_mix, 0), r.logs, pair,
            r.keys_ref, (r.key_sum, r.value_sum), ((r.qkv_grad, 0), (r.qkv_grad, width), (r.qkv_grad, 2 * width)),
            False,
        )
        reduce.run(*steps[pair])
    stage = [
        moves.start(r.mix_one_in, r.mix),
        moves.start(r.qkv_in, r.qkv),
        moves.start(r.logs_one_in, r.logs),
        moves.start(r.low_in, r.low),
    ]
    for copy in late:
        copy.wait()
    store_blocks(grid, r.cross_grads, 2, tn(r.memory_low[...], r.qkv_grad[:, 2 * width :]))
    reduce.begin([c0])
    store_blocks(grid, r.cross_grads, 1, tn(r.memory_low[...], r.qkv_grad[:, width : 2 * width]))
    r.key_value_grad[...] = r.qkv_grad[:, width:]
    r.grad_first[...] = nt(r.qkv_grad[:, :width], r.weights[4])
    reduce.run((f3, 2), (f2, 3))
    r.sums[...] = jnp.zeros_like(r.sums)
    norms = r.norms

    def back(rows):
        unit_rows = r.unit[rows, :]
        grad = r.grad_first[rows, :] + r.grad_second[rows, :]
        r.first_low[rows, :] = (unit_rows * norms[0:1, :] + norms[1:2, :]).astype(BF)
        grad_rows = norm_gradient(grad, norms[0:1, :], unit_rows, r.scale[rows, 0:1])
        r.grad_first[rows, :] = grad_rows
        r.grad_low[rows, :] = grad_rows.astype(BF)
        r.sums[0] += fold_rows(grad * unit_rows)
        r.sums[1] += fold_rows(grad)

    row_loop(rows_all, back, BACK_ROWS)
    third = moves.start(r.grad_third_in, r.unit)
    r.norm_value[0] = jnp.concatenate(
        [jnp.sum(r.sums[...], axis=1), r.feed_norms[...], jnp.zeros((2, width), F32)], axis=0
    )
    total = Total(grid, r.norm_value, [getattr(r, name) for name in names["norm"]], links)
    total.send(0)
    reduce.run((c0, 0), (f3, 3))
    store_blocks(grid, r.cross_grads, 0, tn(r.first_low[...], r.qkv_grad[:, :width]))
    reduce.begin([c1])

    self_weights.wait()
    for copy in stage:
        copy.wait()
    r.grad_mix[...] = nn(r.grad_low[...], r.weights[3]).astype(BF)
    store_blocks(grid, r.self_grads, 3, tn(r.grad_low[...], r.mix[...]))
    reduce.begin([c2])
    steps = [
        [(c0, 1), (c1, 0)],
        [(c0, 2), (c2, 0)],
        [(c1, 1), (c0, 3)],
        [(c1, 2), (c2, 1)],
    ]
    for pair in range(width // PAIR):
        pair_backward(
            (r.qkv, 0), (r.qkv, width), (r.qkv, 2 * width), None, (r.mix, 0), (r.grad_mix, 0), r.logs, pair,
            r.keys_ref, (r.key_sum, r.value_sum), ((r.qkv_grad, 0), (r.qkv_grad, width), (r.qkv_grad, 2 * width)),
            True,
        )
        total.advance(pair)
        reduce.run(*steps[pair])
    s0, s1 = self_pairs
    for part in range(3):
        grad = tn(r.low[...], r.qkv_grad[:, part * width : (part + 1) * width])
        store_blocks(grid, r.self_grads, part, grad)
        if part == 1:
            reduce.begin([s0])
    reduce.begin([s1])
    reduce.run((s0, 0), (c2, 2))
    third.wait()
    back_input = r.grad_first[...] + r.unit[...]
    back_input = back_input + nt(r.qkv_grad[:, :width], r.weights[0])
    reduce.run((s1, 0))
    back_input = back_input + nt(r.qkv_grad[:, width : 2 * width], r.weights[1])
    back_input = back_input + nt(r.qkv_grad[:, 2 * width :], r.weights[2])
    r.input_low[...] = back_input.astype(BF)
    moves.send(r.input_low, r.grad_input_out)
    reduce.run((s0, 1))
    back_memory = nt(r.key_value_grad[:, :width], r.weights[5])
    reduce.run((s1, 1))
    back_memory = back_memory + nt(r.key_value_grad[:, width:], r.weights[6])
    r.outgoing[...] = back_memory.astype(BF)
    moves.send(r.outgoing, r.grad_memory_out)
    reduce.run((s0, 2), (s1, 2), (c1, 3), (c2, 3), (s0, 3), (s1, 3))
    r.norm_sum[...] = r.norm_value[4]
    links.finish()
    moves.finish()


def run_layer(
    inputs, memory, cotangent, lengths, key_mask, owner_list, attention_master, feed_master, norm_master, groups, splits
):
    grid = Grid(groups, splits)
    width = inputs.shape[1]
    rows = inputs.shape[0] // splits
    keys = memory.shape[0] // splits
    own_rows = attention_master.shape[1]
    attention_t, feed_t = attention_master.shape, feed_master.shape
    hidden = splits * feed_t[2]
    if rows != keys or hidden != 4 * width:
        raise ValueError("unexpected sizes")
    pairs = width // PAIR
    low_t, full_t, keys_low_t = ((rows, width), BF), ((rows, width), F32), ((keys, width), BF)
    scale_t, logs_t, place_t = ((rows, 128), F32), ((pairs, 2, rows), F32), ((width, width), BF)
    qkv_t, key_value_t = ((rows, 3 * width), BF), ((keys, 2 * width), BF)
    guard_t, halves_t, norm_t = ((keys, PAIR), BF), ((2, keys, PAIR), BF), ((8, width), F32)
    eight_t = ((8, width, width), BF)
    attention_blocks, feed_blocks = (*grid.dims, *attention_t), (*grid.dims, *feed_t)
    norm_shard_t = ((16, width), BF)
    pair_flops = 2 * rows * keys * width
    dense = 2 * rows * width * width

    def hbm(item):
        return (*item, ANY)

    f = run_kernel(
        functools.partial(forward, grid),
        "forward",
        {
            "inputs": (inputs, ANY),
            "memory": (memory, ANY),
            "key_mask": (key_mask, WHOLE),
            "owner_list": (owner_list, SCALAR),
            "attention_master": (attention_master, ANY),
            "feed_master": (feed_master, ANY),
            "norm_master": (norm_master, WHOLE),
            "cotangent_in": (cotangent, ANY),
            "lengths": (lengths, SCALAR),
        },
        {
            "attention": (attention_blocks, BF, ANY),
            "feed": (feed_blocks, BF, ANY),
            "norm_blocks": ((*grid.dims, *norm_shard_t[0]), BF, ANY),
            "place_out": hbm(place_t),
            "guard_out": hbm(guard_t),
            "low_out": hbm(low_t),
            "memory_low_out": hbm(keys_low_t),
            "qkv_out": hbm(qkv_t),
            "mix_one_out": hbm(low_t),
            "logs_one_out": hbm(logs_t),
            "unit_one_out": hbm(full_t),
            "scale_one_out": hbm(scale_t),
            "query_out": hbm(low_t),
            "key_value_out": hbm(key_value_t),
            "mix_two_out": hbm(low_t),
            "logs_two_out": hbm(logs_t),
            "norms": (*norm_t, WHOLE),
            "output_out": hbm(low_t),
            "grad_third_out": hbm(full_t),
            "grad_second_out": hbm(full_t),
            "grads_out": (feed_blocks, BF, ANY),
            "norm_grads": ((4, width), F32, WHOLE),
        },
        {
            "attention_float": (attention_t, F32),
            "feed_float": (feed_t, F32),
            "attention_shard": (attention_t, BF),
            "feed_shard": (feed_t, BF),
            "norm_shard": norm_shard_t,
            "norm_all": ((*grid.dims, *norm_shard_t[0]), BF),
            "place": place_t,
            "guard": guard_t,
            "low": low_t,
            "weights": eight_t,
            "wide_one": ((rows, hidden), BF),
            "wide_two": ((rows, hidden), BF),
            "mix_one": low_t,
            "logs_one": logs_t,
            "unit_one": full_t,
            "scale_one": scale_t,
            "mix_two": low_t,
            "logs_two": logs_t,
            "unit_two": full_t,
            "scale_two": scale_t,
            "keys_ref": halves_t,
            "values_t": ((PAIR, keys), BF),
            "cotangent": low_t,
            "feed_weights": ((2, width, hidden), BF),
            "slope": ((min(FEED_ROWS, rows), hidden), F32),
            "output": low_t,
            "grad_second": full_t,
            "grads": (feed_blocks, BF),
            "sums": ((4, 8, width), F32),
        },
        61 << 20,
        12 * dense + 14 * pair_flops + 12 * rows * width * hidden,
        32,
        17 * grid.copies,
        0,
    )

    scratch = {
        "grad_second": full_t,
        "mix": low_t,
        "weights": eight_t,
        "qkv": qkv_t,
        "logs": logs_t,
        "guard": guard_t,
        "memory_low": keys_low_t,
        "low": low_t,
        "unit": full_t,
        "scale": scale_t,
        "grad_low": low_t,
        "key_value_grad": key_value_t,
        "grad_mix": low_t,
        "qkv_grad": qkv_t,
        "first_low": low_t,
        "outgoing": keys_low_t,
        "input_low": low_t,
        "grad_first": full_t,
        "cross_grads": ((*grid.dims, 4, *attention_t[1:]), BF),
        "self_grads": ((*grid.dims, 4, *attention_t[1:]), BF),
        "feed_half": ((*[a.size for n, a in grid.axes.items() if n != "core"], *feed_t), BF),
        "sums": ((2, 8, width), F32),
        "norm_value": ((5, 8, width), F32),
        "keys_ref": halves_t,
        "key_sum": ((keys, PAIR), F32),
        "value_sum": ((keys, PAIR), F32),
    }
    names = {}
    kinds = [("feed", p, m, (feed_t[1], feed_t[2] // 4)) for p in range(4) for m in range(2)]
    kinds += [
        (kind, p, m, attention_t[1:]) for kind in ("cross", "self") for p in range(2) for m in range(2)
    ]
    for kind, p, m, shard in kinds:
        names[kind, p, m] = []
        parity = 0 if (kind, p) == ("self", 1) else m
        for phase, shape in enumerate(arrival_shapes(grid, parity, shard, BF)):
            name = f"{kind}{p}{m}{phase}"
            scratch[name] = shape
            names[kind, p, m].append(name)
    names["norm"] = []
    for phase, axis in enumerate(grid.orders[0][::-1]):
        scratch[f"norm{phase}"] = ((grid.axes[axis].size - 1, 8, width), F32)
        names["norm"].append(f"norm{phase}")
    b = run_kernel(
        functools.partial(backward, grid, names),
        "backward",
        {
            "grad_second_in": (f.grad_second_out, ANY),
            "mix_two_in": (f.mix_two_out, ANY),
            "attention": (f.attention, ANY),
            "query_in": (f.query_out, ANY),
            "key_value_in": (f.key_value_out, ANY),
            "logs_two_in": (f.logs_two_out, ANY),
            "guard_in": (f.guard_out, ANY),
            "memory_low_in": (f.memory_low_out, ANY),
            "unit_in": (f.unit_one_out, ANY),
            "scale_in": (f.scale_one_out, ANY),
            "mix_one_in": (f.mix_one_out, ANY),
            "qkv_in": (f.qkv_out, ANY),
            "logs_one_in": (f.logs_one_out, ANY),
            "low_in": (f.low_out, ANY),
            "grad_third_in": (f.grad_third_out, ANY),
            "feed_grads": (f.grads_out, ANY),
            "norms": (f.norms, WHOLE),
            "feed_norms": (f.norm_grads, WHOLE),
        },
        {
            "grad_memory_out": hbm(keys_low_t),
            "grad_input_out": hbm(low_t),
            "attention_sum": (attention_t, F32, WHOLE),
            "feed_sum": (feed_t, F32, WHOLE),
            "norm_sum": (*norm_t, WHOLE),
        },
        scratch,
        61 << 20,
        18 * dense + 35 * pair_flops,
        40,
        17 * grid.copies,
        1,
    )
    return f.output_out, b.grad_input_out, b.grad_memory_out, b.attention_sum, b.feed_sum, b.norm_sum, f.place_out


def adam_moments(rotated, moment, second):
    moment_new = BETA_FIRST * moment + (1.0 - BETA_FIRST) * rotated
    second_new = BETA_SECOND * second + (1.0 - BETA_SECOND) * rotated * rotated
    direction = (
        moment_new
        / (1.0 - BETA_FIRST**STEP)
        / (jnp.sqrt(second_new / (1.0 - BETA_SECOND**STEP)) + ADAM_EPSILON)
    )
    return (moment_new, second_new, direction)


def finish(weight, average, update, rate, decay):
    weight_new = weight - rate * (update + decay * weight)
    average_new = AVERAGE_DECAY * average + (1.0 - AVERAGE_DECAY) * weight_new
    return (weight_new, average_new, weight_new.astype(jnp.bfloat16))


def split(values):
    high = values.astype(BF)
    return high, (values - high.astype(F32)).astype(BF)


def rotate(values, basis, back):
    times = nt if back else nn
    rows = values[0].shape[0]
    top = times(jnp.concatenate(values, axis=0), basis[0])
    return top[:rows] + top[rows:] + times(values[0], basis[1])


STATES = ("grad", "master", "moment", "second", "average", "basis")
RESULTS = ("moment", "second", "weight", "average", "copy")


def update(r):
    moves = Moves(r.sems[0])
    lead = [
        (moves.start(r.place_in, r.place), moves.start(r.output_in, r.output)),
        (moves.start(r.grad_input_in, r.grad_input),),
        (moves.start(r.grad_memory_in, r.grad_memory),),
    ]
    loads = {
        (kind, name): moves.start(getattr(r, f"{kind}_{name}_in"), getattr(r, f"{kind}_{name}"))
        for kind in ("attention", "feed")
        for name in STATES
    }
    for copies, low, out in zip(
        lead,
        (r.output, r.grad_input, r.grad_memory),
        (r.output_out, r.grad_input_out, r.grad_memory_out),
    ):
        for copy in copies:
            copy.wait()
        low[...] = nt(low[...], r.place[...]).astype(BF)
        moves.send(low, out)
    for kind, rate in (("attention", RATE_ATTENTION), ("feed", RATE_FEED)):
        for name in STATES:
            loads[kind, name].wait()
        grad, master, moment, second, average, basis = (getattr(r, f"{kind}_{n}") for n in STATES)
        low = getattr(r, f"{kind}_copy")
        for slot in range(grad.shape[0]):
            turn = split(basis[slot])
            rotated = rotate(split(grad[slot]), turn, False)
            moment[slot], second[slot], direction = adam_moments(rotated, moment[slot], second[slot])
            master[slot], average[slot], low[slot] = finish(
                master[slot], average[slot], rotate(split(direction), turn, True), rate, WEIGHT_DECAY
            )
        for name, ref in zip(RESULTS, (moment, second, master, average, low)):
            moves.send(ref, getattr(r, f"{kind}_{name}_out"))
    slots, own_rows = r.norm_master_in.shape
    piece = r.norm_moment_out.shape[1]

    def own(values, first):
        shape = (values.shape[1], 128)
        here = lax.broadcasted_iota(jnp.int32, shape, 0)
        there = lax.broadcasted_iota(jnp.int32, shape, 1)
        select = jnp.where(here == there + first, 1.0, 0.0)
        picked = lax.dot_general(
            values, select, (((1,), (0,)), ((), ())), precision=HIGHEST, preferred_element_type=F32
        )
        return picked[:slots, :piece]

    begin = lax.axis_index("tensor") * piece
    grad = own(r.norm_sum[...], lax.axis_index("dp") * own_rows + begin)
    master, moment, second, average = (
        own(ref[...], begin)
        for ref in (r.norm_master_in, r.norm_moment_in, r.norm_second_in, r.norm_average_in)
    )
    moment, second, direction = adam_moments(grad, moment, second)
    results = (moment, second, *finish(master, average, direction, RATE_NORMS, 0.0))
    for name, value in zip(RESULTS, results):
        getattr(r, f"norm_{name}_out")[...] = value
    moves.finish()


def run_update(output, grad_input, grad_memory, place, norm_sum, states):
    ins = {
        "output_in": (output, ANY),
        "grad_input_in": (grad_input, ANY),
        "grad_memory_in": (grad_memory, ANY),
        "place_in": (place, ANY),
        "norm_sum": (norm_sum, WHOLE),
    }
    outs = {
        "output_out": (output.shape, BF, ANY),
        "grad_input_out": (grad_input.shape, BF, ANY),
        "grad_memory_out": (grad_memory.shape, BF, ANY),
    }
    scratch = {
        "place": (place.shape, BF),
        "output": (output.shape, BF),
        "grad_input": (grad_input.shape, BF),
        "grad_memory": (grad_memory.shape, BF),
    }
    for kind in ("attention", "feed"):
        shape = states[kind]["grad"].shape
        for name in STATES:
            ins[f"{kind}_{name}_in"] = (states[kind][name], ANY)
            scratch[f"{kind}_{name}"] = (states[kind][name].shape, F32)
        scratch[f"{kind}_copy"] = (shape, BF)
        for name in RESULTS:
            outs[f"{kind}_{name}_out"] = (shape, BF if name == "copy" else F32, ANY)
    for name, array in states["norm"].items():
        ins[f"norm_{name}_in"] = (array, WHOLE)
    slots, own_rows = states["norm"]["master"].shape
    for name in RESULTS:
        shape = (slots, own_rows // lax.axis_size("tensor"))
        outs[f"norm_{name}_out"] = (shape, BF if name == "copy" else F32, WHOLE)
    return run_kernel(update, "update", ins, outs, scratch, 60 << 20, 1 << 31, 32)


def on_device(
    inputs,
    memory,
    cotangent,
    lengths,
    key_mask,
    owner_list,
    attention_master,
    attention_moment,
    attention_second,
    attention_average,
    attention_basis,
    feed_master,
    feed_moment,
    feed_second,
    feed_average,
    feed_basis,
    norm_master,
    norm_moment,
    norm_second,
    norm_average,
):
    groups = lax.axis_size("dp")
    splits = lax.axis_size("tensor")
    output, grad_input, grad_memory, attention_grad, feed_grad, norm_sum, place = run_layer(
        inputs,
        memory,
        cotangent,
        lengths,
        key_mask,
        owner_list,
        attention_master,
        feed_master,
        norm_master,
        groups,
        splits,
    )
    u = run_update(
        output,
        grad_input,
        grad_memory,
        place,
        norm_sum,
        {
            "attention": dict(
                grad=attention_grad,
                master=attention_master,
                moment=attention_moment,
                second=attention_second,
                average=attention_average,
                basis=attention_basis,
            ),
            "feed": dict(
                grad=feed_grad,
                master=feed_master,
                moment=feed_moment,
                second=feed_second,
                average=feed_average,
                basis=feed_basis,
            ),
            "norm": dict(
                master=norm_master, moment=norm_moment, second=norm_second, average=norm_average
            ),
        },
    )
    results = [
        getattr(u, f"{kind}_{name}_out") for kind in ("attention", "feed", "norm") for name in RESULTS
    ]
    return (u.output_out, u.grad_input_out, u.grad_memory_out, *results)


def solution(mesh):
    in_specs = (
        P("dp", None),
        P("dp", None),
        P("dp", None),
        P("dp"),
        P("dp", None),
        P(),
        P(None, "dp", "tensor"),
        P(None, "dp", "tensor"),
        P(None, "dp", "tensor"),
        P(None, "dp", "tensor"),
        P(None, "tensor", None),
        P(None, "dp", "tensor"),
        P(None, "dp", "tensor"),
        P(None, "dp", "tensor"),
        P(None, "dp", "tensor"),
        P(None, "tensor", None),
        P(None, "dp"),
        P(None, "dp"),
        P(None, "dp"),
        P(None, "dp"),
    )
    out_specs = (
        P(("dp", "tensor"), None),
        P(("dp", "tensor"), None),
        P(("dp", "tensor"), None),
        P(None, "dp", "tensor"),
        P(None, "dp", "tensor"),
        P(None, "dp", "tensor"),
        P(None, "dp", "tensor"),
        P(None, "dp", "tensor"),
        P(None, "dp", "tensor"),
        P(None, "dp", "tensor"),
        P(None, "dp", "tensor"),
        P(None, "dp", "tensor"),
        P(None, "dp", "tensor"),
        P(None, ("dp", "tensor")),
        P(None, ("dp", "tensor")),
        P(None, ("dp", "tensor")),
        P(None, ("dp", "tensor")),
        P(None, ("dp", "tensor")),
    )
    return jax.shard_map(
        on_device, mesh=mesh, in_specs=in_specs, out_specs=out_specs, check_vma=False
    )
```
